32 devices in a mesh: batch: 8 (over y, x, core), head: 4 (over z).
Axes of the slice: x: 2, y: 2, z: 4, core: 2. Of those that a mesh axis runs over, the one named last changes fastest.
Arguments:
- hidden: bfloat16 [8, 512, 3, 1024], P('batch', 'head'), may hold values from -6 to 6
- memory: bfloat16 [8, 1024, 1024], P('batch', 'head'), may hold values from -6 to 6
- grad_out: float32 [8, 512, 3, 1024], P('batch'), may hold values from -6 to 6
- lengths: int32 [8, 4], P('batch'), may hold values from 1 to 256, 512 in all within a row
- key_mask: int32 [8, 512], P('batch'), may hold values 0 or 1
- buckets: int32 [512], replicated, may hold values from 0 to 31, as said below
- self_weight: float32 [1024, 3, 1024], P('batch', None, 'head'), may hold values from -0.1875 to 0.1875
- relpos_weight: float32 [1024, 512], P('batch', 'head'), may hold values from -0.1875 to 0.1875
- selfout_weight: float32 [1024, 1024], P('batch', 'head'), may hold values from -1 to 1
- crossq_weight: float32 [1024, 1024], P('batch', 'head'), may hold values from -0.1875 to 0.1875
- crosskv_weight: float32 [1024, 2, 1024], P('batch', None, 'head'), may hold values from -0.1875 to 0.1875
- crossout_weight: float32 [1024, 1024], P('batch', 'head'), may hold values from -3 to 3
- up_weight: float32 [1024, 4096], P('batch', 'head'), may hold values from -0.1875 to 0.1875
- down_weight: float32 [1024, 4096], P('batch', 'head'), may hold values from -0.09375 to 0.09375
- self_bias: float32 [2, 1024], replicated, may hold values from -1.8 to 1.8
- relpos_bias: float32 [512], replicated, may hold values from -3 to 3
- cross_bias: float32 [2, 1024], replicated, may hold values from -1.8 to 1.8
- up_bias: float32 [4096], replicated, may hold values from -1.8 to 1.8
- norm_gain: float32 [3, 1024], replicated, may hold values from 0.5 to 1.5
- norm_bias: float32 [3, 1024], replicated, may hold values from -1.8 to 1.8
- out_bias: float32 [3, 1024], replicated, may hold values from -1.8 to 1.8
Outputs:
- layer_out: bfloat16 [8, 512, 3, 1024], P('batch')
- grad_hidden: float32 [8, 512, 3, 1024], P('batch', 'head')
- grad_memory: float32 [8, 1024, 1024], P('batch', 'head')
- self_weight_grad: float32 [1024, 3, 1024], P('batch', None, 'head')
- relpos_weight_grad: float32 [1024, 512], P('batch', 'head')
- selfout_weight_grad: float32 [1024, 1024], P('batch', 'head')
- crossq_weight_grad: float32 [1024, 1024], P('batch', 'head')
- crosskv_weight_grad: float32 [1024, 2, 1024], P('batch', None, 'head')
- crossout_weight_grad: float32 [1024, 1024], P('batch', 'head')
- up_weight_grad: float32 [1024, 4096], P('batch', 'head')
- down_weight_grad: float32 [1024, 4096], P('batch', 'head')
- self_bias_grad: float32 [2, 1024], replicated
- relpos_bias_grad: float32 [512], replicated
- cross_bias_grad: float32 [2, 1024], replicated
- up_bias_grad: float32 [4096], replicated
- norm_gain_grad: float32 [3, 1024], replicated
- norm_bias_grad: float32 [3, 1024], replicated
- out_bias_grad: float32 [3, 1024], replicated
The draws below stay inside these ranges and needn't reach their ends.
Inputs may be any that keep to these rules, and one draw needn't show every extreme that they name: The 4 document lengths of a row sum to 512. `key_mask`: 1 marks a key that queries may attend to. buckets[d] is the bucket of a key d positions before its query; it never falls as d grows, and buckets[0] is 0.
All inputs are finite; a program needn't handle non-finite values. No bound on the sum of `key_mask` on one device may be relied on, other than what follows from the above.
Results may differ from the reference program's by a relative error of at most 0.025.
Values may be sent and summed in bfloat16 or wider, within the bound.
No kernel may reach another device: no remote copies, remote signals or barrier semaphores. Data moves between devices by JAX's collectives and lax.ppermute only.
A program may use at most 256 MiB of HBM per device.

```python
import math
import jax
import jax.numpy as jnp
import numpy as np
from jax import lax

D = 1024
HEADS = 16
HEAD_DIM = 64
BUCKETS = 32
FF = 4096
ROW_LEN = 512
MEM_LEN = 1024
DOCS = 4
ROWS = 8


def draw_buckets(key, part):
    breaks_count = min(BUCKETS - 1, ROW_LEN - 1)
    chosen = jax.random.permutation(key, ROW_LEN - 1)[:breaks_count].astype(jnp.int32) + 1
    breaks = jnp.sort(chosen)
    places = lax.iota(jnp.int32, ROW_LEN)
    return jnp.sum((places[:, None] >= breaks[None, :]).astype(jnp.int32), -1)


def touch_ends(drawn, stream_key, smallest, largest):
    longest = drawn.shape.index(max(drawn.shape))
    spots = []
    for shift in (0, 1):
        where = [jax.random.randint(jax.random.fold_in(stream_key, axis), (), 0, length) for axis, length in enumerate(drawn.shape)]
        where[longest] = (where[longest] + shift) % drawn.shape[longest]
        spots.append(tuple(where))
    return drawn.at[spots[0]].set(smallest).at[spots[1]].set(largest)


def block_scale(stream_key, dims, split, least, high):
    def one(dim, parts):
        heights = jax.random.uniform(jax.random.fold_in(jax.random.fold_in(stream_key, 6), dim), (parts,), jnp.float32, least / len(split), high / len(split))
        return jnp.repeat(jnp.exp(heights), dims[dim] // parts).reshape((-1,) + (1,) * (len(dims) - dim - 1))

    gain = one(*split[0])
    for cut in split[1:]:
        gain = gain * one(*cut)
    return gain


def split_up(amount, total, limit, slope):
    loads = [(1 << 20) // math.isqrt(rank ** slope) + 1 for rank in range(2, amount + 1)]
    rest, given = total - limit - (amount - 1), [1] * (amount - 1)
    while rest > 0:
        free = [i for i in range(amount - 1) if given[i] < limit]
        whole, budget = sum([loads[i] for i in free]), rest
        for i in free:
            addition = min(limit - given[i], max(1, budget * loads[i] // whole), rest)
            given[i] = given[i] + addition
            rest = rest - addition
    return np.array([limit] + given)


def uneven_parts(key, number_of, total, most, skew):
    if number_of == 2:
        one = jax.random.randint(key, (), max(1, total - most), min(most, total - 1) + 1)
        return jnp.stack([one, total - one])
    tallies = jnp.asarray(split_up(number_of, total, most, skew), jnp.int32)
    twos = (number_of - 1) // 2
    giver, sink = tallies[1:1 + 2 * twos:2], tallies[2:2 + 2 * twos:2]
    margin = jnp.minimum(giver - 1, most - sink)
    passed = jax.random.randint(jax.random.fold_in(key, 1), (twos,), 0, 1 << 20) % (margin + 1)
    tallies = tallies.at[1:1 + 2 * twos:2].set(giver - passed).at[2:2 + 2 * twos:2].set(sink + passed)
    return tallies[jax.random.permutation(jax.random.fold_in(key, 2), number_of)]


def centred(rng, dims, deviation, most, shards=(), kind=jnp.bfloat16):
    drawn = deviation * jax.random.normal(rng, dims, jnp.float32)
    if shards:
        drawn = drawn * block_scale(rng, dims, shards, -0.22, 0.18)
    return jnp.clip(drawn, -most, most).astype(kind)


def setup_inputs(seed: int = 0) -> dict:
    seeds = jax.random.split(jax.random.key(seed), 22)
    hidden = centred(seeds[0], (ROWS, ROW_LEN, 3, D), 1.0, 6.0, ((0, 8), (1, 4)))
    memory = centred(seeds[1], (ROWS, MEM_LEN, D), 1.0, 6.0, ((0, 8), (1, 4)))
    grad_out = centred(seeds[2], (ROWS, ROW_LEN, 3, D), 1.0, 6.0, ((0, 8),), jnp.float32)
    lengths = jax.vmap(lambda own: uneven_parts(own, DOCS, ROW_LEN, ROW_LEN // 2, 1))(jax.random.split(seeds[3], ROWS)).reshape((ROWS, DOCS)).astype(jnp.int32)
    key_mask = touch_ends((jax.random.randint(seeds[4], (ROWS, ROW_LEN), 0, 8) < 7).astype(jnp.int32), jax.random.fold_in(seeds[4], 1), 0, 1)
    buckets = draw_buckets(jax.random.fold_in(seeds[21], 71), 0)
    self_weight = centred(seeds[6], (D, 3, HEADS * HEAD_DIM), D ** -0.5, 0.1875, ((0, 8), (2, 4)), jnp.float32)
    relpos_weight = centred(seeds[7], (D, HEADS * BUCKETS), D ** -0.5, 0.1875, ((0, 8), (1, 4)), jnp.float32)
    selfout_weight = centred(seeds[8], (D, HEADS * HEAD_DIM), (max(D // 32, 2)) ** -0.5, 1.0, ((0, 8), (1, 4)), jnp.float32)
    crossq_weight = centred(seeds[9], (D, HEADS * HEAD_DIM), D ** -0.5, 0.1875, ((0, 8), (1, 4)), jnp.float32)
    crosskv_weight = centred(seeds[10], (D, 2, HEADS * HEAD_DIM), D ** -0.5, 0.1875, ((0, 8), (2, 4)), jnp.float32)
    crossout_weight = centred(seeds[11], (D, HEADS * HEAD_DIM), (max(D // 256, 2)) ** -0.5, 3.0, ((0, 8), (1, 4)), jnp.float32)
    up_weight = centred(seeds[12], (D, FF), D ** -0.5, 0.1875, ((0, 8), (1, 4)), jnp.float32)
    down_weight = centred(seeds[13], (D, FF), FF ** -0.5, 0.09375, ((0, 8), (1, 4)), jnp.float32)
    self_bias = centred(seeds[14], (2, HEADS * HEAD_DIM), 0.3, 1.8, (), jnp.float32)
    relpos_bias = centred(seeds[15], (HEADS * BUCKETS,), 0.5, 3.0, (), jnp.float32)
    cross_bias = centred(seeds[16], (2, HEADS * HEAD_DIM), 0.3, 1.8, (), jnp.float32)
    up_bias = centred(seeds[17], (FF,), 0.3, 1.8, (), jnp.float32)
    norm_gain = jnp.clip(1.0 + 0.1 * jax.random.normal(seeds[18], (3, D), jnp.float32), 0.5, 1.5)
    norm_bias = centred(seeds[19], (3, D), 0.3, 1.8, (), jnp.float32)
    out_bias = centred(seeds[20], (3, D), 0.3, 1.8, (), jnp.float32)
    return dict(hidden=hidden, memory=memory, grad_out=grad_out, lengths=lengths, key_mask=key_mask, buckets=buckets, self_weight=self_weight, relpos_weight=relpos_weight, selfout_weight=selfout_weight, crossq_weight=crossq_weight, crosskv_weight=crosskv_weight, crossout_weight=crossout_weight, up_weight=up_weight, down_weight=down_weight, self_bias=self_bias, relpos_bias=relpos_bias, cross_bias=cross_bias, up_bias=up_bias, norm_gain=norm_gain, norm_bias=norm_bias, out_bias=out_bias)


highest = lax.Precision.HIGHEST
epsilon = 1e-05
masked_score = -1e+30

@jax.custom_vjp
def low(v):
    return lax.optimization_barrier(v.astype(jnp.bfloat16)).astype(jnp.float32)

@jax.custom_vjp
def low_back(v):
    return v

def low_keep(v):
    return (low(v), None)

def low_pass(kept, grad):
    return (grad,)

def back_keep(v):
    return (v, None)

def back_low(kept, grad):
    return (low(grad),)
low.defvjp(low_keep, low_pass)
low_back.defvjp(back_keep, back_low)

def einsum_high(pattern, former, latter):
    return jnp.einsum(pattern, former, latter, precision=highest)

def normalize(inputs, gain_row, shift_row):
    centered = inputs - lax.optimization_barrier(jnp.mean(inputs, -1, keepdims=True))
    return centered * lax.rsqrt(lax.optimization_barrier(jnp.mean(centered * centered, -1, keepdims=True)) + epsilon) * gain_row + shift_row

def self_track(queries, keys_all, values, relpos, lookup, allowed, own_bucket, which_track):
    rel_heads = jnp.transpose(relpos[:, which_track], (1, 0, 2))
    gathered = jnp.take_along_axis(rel_heads, jnp.broadcast_to(lookup[None], (HEADS, ROW_LEN, ROW_LEN)), axis=2)
    main_part = einsum_high('thc,shc->hts', queries[:, which_track], keys_all[:, 0]) + gathered
    if which_track == 0:
        scores = jnp.where(allowed[None], low_back(main_part), masked_score)
        softmaxed = low(jax.nn.softmax(scores, axis=-1))
        return einsum_high('hts,shc->thc', softmaxed, values[:, 0])
    own_part = jnp.transpose(lax.optimization_barrier(jnp.sum(queries[:, which_track] * keys_all[:, which_track], -1))) + lax.dynamic_index_in_dim(rel_heads, own_bucket, 2, keepdims=False)
    joined = low_back(jnp.concatenate([main_part, own_part[..., None]], -1))
    keeping = jnp.concatenate([jnp.broadcast_to(allowed[None], main_part.shape), jnp.full(own_part.shape + (1,), True)], -1)
    softmaxed = low(jax.nn.softmax(jnp.where(keeping, joined, masked_score), axis=-1))
    mixture = einsum_high('hts,shc->thc', softmaxed[..., :ROW_LEN], values[:, 0])
    return mixture + jnp.transpose(softmaxed[..., ROW_LEN])[..., None] * values[:, which_track]

def row_layer(params, row_data):
    self_weight, relpos_weight, selfout_weight, crossq_weight, crosskv_weight, crossout_weight, up_weight, down_weight, self_bias, relpos_bias, cross_bias, up_bias, norm_gain, norm_bias, out_bias, buckets = params
    hidden, memory, segment, key_mask = row_data
    places = lax.iota(jnp.int32, ROW_LEN)
    lookup = buckets[jnp.clip(places[:, None] - places[None, :], 0, ROW_LEN - 1)]
    base = (segment[:, None] == segment[None, :]) & ((key_mask[None, :] == 1) | (places[:, None] == places[None, :]))
    allowed_main = base & (places[None, :] <= places[:, None])
    allowed_pred = base & (places[None, :] < places[:, None])
    projected = einsum_high('snd,dkc->snkc', hidden, self_weight)
    head_shape = (ROW_LEN, 3, HEADS, HEAD_DIM)
    queries = low((low_back(projected[:, :, 0]) + self_bias[0]) * 0.125).reshape(head_shape)
    keys_all = low(low_back(projected[:, :, 1])).reshape(head_shape)
    values = low(low_back(projected[:, :, 2]) + self_bias[1]).reshape(head_shape)
    relpos = (low_back(einsum_high('snd,dc->snc', hidden, relpos_weight)) + relpos_bias).reshape(ROW_LEN, 3, HEADS, BUCKETS)
    contexts = []
    for which_track in range(3):
        allowed = allowed_main if which_track == 0 else allowed_pred
        contexts.append(self_track(queries, keys_all, values, relpos, lookup, allowed, buckets[0], which_track))
    context = low(low_back(jnp.stack(contexts, 1))).reshape(ROW_LEN, 3, HEADS * HEAD_DIM)
    attended = low_back(einsum_high('snc,dc->snd', context, selfout_weight)) + out_bias[0]
    normed1 = normalize(hidden + attended, norm_gain[0], norm_bias[0])
    cross_queries = low((low_back(einsum_high('snd,dc->snc', low(normed1), crossq_weight)) + cross_bias[0]) * 0.125).reshape(head_shape)
    cross_kv = einsum_high('md,dkc->mkc', memory, crosskv_weight)
    cross_keys = low(low_back(cross_kv[:, 0])).reshape(MEM_LEN, HEADS, HEAD_DIM)
    cross_values = low(low_back(cross_kv[:, 1]) + cross_bias[1]).reshape(MEM_LEN, HEADS, HEAD_DIM)
    cross_contexts = []
    for which_track in range(3):
        scores = low_back(einsum_high('thc,mhc->htm', cross_queries[:, which_track], cross_keys))
        softmaxed = low(jax.nn.softmax(scores, axis=-1))
        cross_contexts.append(einsum_high('htm,mhc->thc', softmaxed, cross_values))
    cross_context = low(low_back(jnp.stack(cross_contexts, 1))).reshape(ROW_LEN, 3, HEADS * HEAD_DIM)
    crossed = low_back(einsum_high('snc,dc->snd', cross_context, crossout_weight)) + out_bias[1]
    normed2 = normalize(normed1 + crossed, norm_gain[1], norm_bias[1])
    upper = low_back(einsum_high('snd,df->snf', low(normed2), up_weight)) + up_bias
    active = low(jax.nn.gelu(upper, approximate=False))
    ffn_out = low_back(einsum_high('snf,df->snd', active, down_weight)) + out_bias[2]
    return normalize(normed2 + ffn_out, norm_gain[2], norm_bias[2])

def forward(weights, hidden, memory, segment, key_mask, buckets):
    rounded = tuple((low(weight) for weight in weights[:8]))
    params = rounded + tuple(weights[8:]) + (buckets,)
    checked = jax.checkpoint(row_layer)
    return lax.map(lambda row_data: checked(params, row_data), (hidden, memory, segment, key_mask))

def reference(hidden, memory, grad_out, lengths, key_mask, buckets, self_weight, relpos_weight, selfout_weight, crossq_weight, crosskv_weight, crossout_weight, up_weight, down_weight, self_bias, relpos_bias, cross_bias, up_bias, norm_gain, norm_bias, out_bias):
    places = lax.iota(jnp.int32, ROW_LEN)
    doc_ends = jnp.cumsum(lengths, axis=-1)
    segment = lax.optimization_barrier(jnp.sum((places[None, :, None] >= doc_ends[:, None, :]).astype(jnp.int32), -1))
    weights = (self_weight, relpos_weight, selfout_weight, crossq_weight, crosskv_weight, crossout_weight, up_weight, down_weight, self_bias, relpos_bias, cross_bias, up_bias, norm_gain, norm_bias, out_bias)

    def runner(weight_set, rows_in, memory_in):
        return forward(weight_set, rows_in, memory_in, segment, key_mask, buckets)
    output, puller = jax.vjp(runner, weights, hidden.astype(jnp.float32), memory.astype(jnp.float32))
    weight_grads, grad_rows, grad_mems = puller(grad_out)
    return (output.astype(jnp.bfloat16), grad_rows, grad_mems, weight_grads[0], weight_grads[1], weight_grads[2], weight_grads[3], weight_grads[4], weight_grads[5], weight_grads[6], weight_grads[7], weight_grads[8], weight_grads[9], weight_grads[10], weight_grads[11], weight_grads[12], weight_grads[13], weight_grads[14])
```

```python
import functools

import jax
import jax.numpy as jnp
from jax import lax
from jax.experimental import pallas as pl
from jax.experimental.pallas import tpu as pltpu
from jax.sharding import PartitionSpec as P

BUCKETS = 32
HEAD_DIM = 64
WIDEST_DOC = 256
EPSILON = 1e-05
MASKED = -1e30
BF = jnp.bfloat16
F32 = jnp.float32
VMEM_BYTES = 56 * 1024 * 1024


def params():
    return pltpu.CompilerParams(vmem_limit_bytes=VMEM_BYTES)


def dot(a, b, ca, cb):
    return lax.dot_general(a, b, (((ca,), (cb,)), ((), ())), preferred_element_type=F32)


def whole(shape):
    return pl.BlockSpec(shape, lambda *_: (0,) * len(shape))


def swap(array_in, axis, bit):
    count = lax.axis_size(axis)
    return lax.ppermute(array_in, axis, [(i, i ^ bit) for i in range(count)])


def bits_of(axis):
    return (lax.axis_size(axis) - 1).bit_length()


def gather_pieces(shard, batch_order):
    nb, nz = bits_of("batch"), bits_of("head")
    blk, cols = shard.shape
    buf = shard.reshape((1,) * (nb + nz) + (blk, cols))
    for bit in range(nz):
        axis = nb + nz - 1 - bit
        buf = jnp.concatenate([buf, swap(buf, "head", 1 << bit)], axis)
    for bit in batch_order:
        buf = jnp.concatenate([buf, swap(buf, "batch", 1 << bit)], bit)
    last = swap(buf, "batch", 1)
    shape = (1 << (nb - 1), 1 << nz, blk, cols)
    return (buf.reshape(shape), last.reshape(shape))


def scatter_pieces(kept, batch_order):
    nb, nz = bits_of("batch"), bits_of("head")
    blk, cols = kept.shape[2:]
    buf = kept.reshape((2,) * (nb - 1 + nz) + (blk, cols))
    live = list(batch_order)
    axes = sorted(live)
    steps = [("batch", bit) for bit in live] + [("head", bit) for bit in reversed(range(nz))]
    names = [("batch", bit) for bit in axes] + [("head", bit) for bit in reversed(range(nz))]
    for number, (axis_name, bit) in enumerate(steps):
        axis = names.index((axis_name, bit))
        names.pop(axis)
        mine = lax.index_in_dim(buf, 0, axis, keepdims=False)
        theirs = lax.index_in_dim(buf, 1, axis, keepdims=False)
        total = mine.astype(F32) + swap(theirs, axis_name, 1 << bit).astype(F32)
        buf = total if number == len(steps) - 1 else total.astype(BF)
    return buf.reshape(blk, cols)


def bit_reverse(number, width):
    turned = 0
    for bit in range(width):
        turned |= ((number >> bit) & 1) << (width - 1 - bit)
    return turned


def reorder_blocks(array_in, table):
    count = table.shape[0]
    rows, features = array_in.shape
    blk = features // count
    if blk % 128:
        return jnp.take(array_in.reshape(rows, count, blk), table, axis=1).reshape(rows, features)

    def body(table_ref, in_ref, out_ref):
        out_ref[...] = in_ref[...]

    return pl.pallas_call(
        body,
        out_shape=jax.ShapeDtypeStruct(array_in.shape, array_in.dtype),
        grid_spec=pltpu.PrefetchScalarGridSpec(
            num_scalar_prefetch=1,
            grid=(count,),
            in_specs=[pl.BlockSpec((rows, blk), lambda p, table_ref: (0, table_ref[p]))],
            out_specs=pl.BlockSpec((rows, blk), lambda p, table_ref: (0, p)),
        ),
        name="reorder",
    )(table, array_in)


def piece_specs(pieces, cols, col_block, step=None):
    count, _, blk, _ = pieces[0].shape
    return [
        pl.BlockSpec((count, 1, blk, cols), lambda j, *c: (0, j, 0, col_block + (c[0] if c else 0)))
        for _ in pieces
    ]


def flat_piece(ref):
    count, _, blk, cols = ref.shape
    return ref[...].reshape(count * blk, cols)


def over_features(x, piece_refs):
    depth = x.shape[1] // len(piece_refs)
    total = None
    for number, ref in enumerate(piece_refs):
        term = dot(x[:, number * depth : (number + 1) * depth], flat_piece(ref), 1, 0)
        total = term if total is None else total + term
    return total


def project(x, pieces, first_col, cols, tile, affine, out_dtype, name):
    rows, features = x.shape
    groups = pieces[0].shape[1]
    per = cols // tile

    def body(x_ref, *refs):
        *piece_refs, affine_ref, out_ref = refs
        acc = over_features(x_ref[...], piece_refs)
        out_ref[...] = ((acc + affine_ref[0:1]) * affine_ref[1:2]).astype(out_ref.dtype)

    return pl.pallas_call(
        body,
        grid=(groups, per),
        in_specs=[whole((rows, features))]
        + piece_specs(pieces, tile, first_col // tile)
        + [pl.BlockSpec((2, tile), lambda j, c: (0, j * per + c))],
        out_specs=pl.BlockSpec((rows, tile), lambda j, c: (0, j * per + c)),
        out_shape=jax.ShapeDtypeStruct((rows, groups * cols), out_dtype),
        compiler_params=params(),
        name=name,
    )(x, *pieces, affine)


def project_plain(x, pieces, first_col, cols, name):
    groups = pieces[0].shape[1]
    affine = jnp.stack([jnp.zeros((groups * cols,), F32), jnp.ones((groups * cols,), F32)])
    return project(x, pieces, first_col, cols, cols, affine, BF, name)


def add_rows(acc_ref, left, piece_refs):
    depth = acc_ref.shape[1] // len(piece_refs)
    for number, ref in enumerate(piece_refs):
        where = slice(number * depth, (number + 1) * depth)
        acc_ref[:, where] += dot(left, flat_piece(ref), 1, 1)


def row_mean(v):
    return jnp.mean(v, -1, keepdims=True)


def column_sum(v):
    return jnp.sum(v, 0, keepdims=True)


def normalize(v):
    centered = v - row_mean(v)
    spread = lax.rsqrt(row_mean(centered * centered) + EPSILON)
    return centered * spread, spread


def normalize_back(upstream, unit, spread, gain):
    a = upstream * gain
    return spread * (a - row_mean(a) - unit * row_mean(a * unit))


def close_sublayer(left, pieces, first_col, cols, residual, vectors, name):
    rows, features = residual.shape
    groups = pieces[0].shape[1]
    count = len(pieces)

    def body(left_ref, *refs):
        piece_refs = refs[:count]
        residual_ref, vectors_ref, normed_ref, low_ref, unit_ref, spread_ref, acc_ref = refs[count:]
        step = pl.program_id(0)

        @pl.when(step == 0)
        def _():
            acc_ref[...] = jnp.zeros_like(acc_ref)

        add_rows(acc_ref, left_ref[...], piece_refs)

        @pl.when(step == groups - 1)
        def _():
            v = residual_ref[...].astype(F32) + (acc_ref[...] + vectors_ref[2:3])
            unit, spread = normalize(v)
            normed = unit * vectors_ref[0:1] + vectors_ref[1:2]
            normed_ref[...] = normed
            low_ref[...] = normed.astype(BF)
            unit_ref[...] = unit
            spread_ref[...] = spread

    return pl.pallas_call(
        body,
        grid=(groups,),
        in_specs=[pl.BlockSpec((rows, cols), lambda j: (0, j))]
        + piece_specs(pieces, cols, first_col // cols)
        + [whole((rows, features)), whole((3, features))],
        out_specs=[whole((rows, features))] * 3 + [whole((rows, 1))],
        out_shape=[
            jax.ShapeDtypeStruct((rows, features), F32),
            jax.ShapeDtypeStruct((rows, features), BF),
            jax.ShapeDtypeStruct((rows, features), F32),
            jax.ShapeDtypeStruct((rows, 1), F32),
        ],
        scratch_shapes=[pltpu.VMEM((rows, features), F32)],
        compiler_params=params(),
        name=name,
    )(left, *pieces, residual, vectors)


def feed_forward(low, normed, up_pieces, down_pieces, up_bias, vectors, grad_out):
    rows, features = normed.shape
    groups, cols = up_pieces[0].shape[1], up_pieces[0].shape[3]
    count = len(up_pieces)

    def body(low_ref, normed_ref, *refs):
        ups, downs = refs[:count], refs[count : 2 * count]
        bias_ref, vectors_ref, grad_ref = refs[2 * count : 2 * count + 3]
        active_ref, slope_ref, out_ref, third_ref, third_low_ref, sums_ref, acc_ref = refs[
            2 * count + 3 :
        ]
        step = pl.program_id(0)

        @pl.when(step == 0)
        def _():
            acc_ref[...] = jnp.zeros_like(acc_ref)

        upper = over_features(low_ref[...], ups) + bias_ref[...]
        cdf = 0.5 * (1.0 + lax.erf(upper * 0.7071067811865476))
        active = (upper * cdf).astype(BF)
        slope = cdf + upper * jnp.exp(-0.5 * upper * upper) * 0.3989422804014327
        active_ref[...] = active
        slope_ref[...] = slope.astype(BF)
        add_rows(acc_ref, active, downs)

        @pl.when(step == groups - 1)
        def _():
            v = normed_ref[...] + (acc_ref[...] + vectors_ref[2:3])
            unit, spread = normalize(v)
            gain = vectors_ref[0:1]
            out_ref[...] = (unit * gain + vectors_ref[1:2]).astype(BF)
            upstream = grad_ref[...]
            third = normalize_back(upstream, unit, spread, gain)
            third_ref[...] = third
            third_low_ref[...] = third.astype(BF)
            sums_ref[0:1] = column_sum(upstream * unit)
            sums_ref[1:2] = column_sum(upstream)
            sums_ref[2:3] = column_sum(third)

    return pl.pallas_call(
        body,
        grid=(groups,),
        in_specs=[whole((rows, features)), whole((rows, features))]
        + piece_specs(up_pieces, cols, 0)
        + piece_specs(down_pieces, cols, 0)
        + [
            pl.BlockSpec((1, cols), lambda j: (0, j)),
            whole((3, features)),
            whole((rows, features)),
        ],
        out_specs=[
            pl.BlockSpec((rows, cols), lambda j: (0, j)),
            pl.BlockSpec((rows, cols), lambda j: (0, j)),
            whole((rows, features)),
            whole((rows, features)),
            whole((rows, features)),
            whole((3, features)),
        ],
        out_shape=[
            jax.ShapeDtypeStruct((rows, groups * cols), BF),
            jax.ShapeDtypeStruct((rows, groups * cols), BF),
            jax.ShapeDtypeStruct((rows, features), BF),
            jax.ShapeDtypeStruct((rows, features), F32),
            jax.ShapeDtypeStruct((rows, features), BF),
            jax.ShapeDtypeStruct((3, features), F32),
        ],
        scratch_shapes=[pltpu.VMEM((rows, features), F32)],
        compiler_params=params(),
        name="feed_forward",
    )(low, normed, *up_pieces, *down_pieces, up_bias, vectors, grad_out)


def norm_back_outputs(upstream, unit, spread, gain, grad_ref, grad_low_ref, sums_ref):
    grad = normalize_back(upstream, unit, spread, gain)
    grad_ref[...] = grad
    grad_low_ref[...] = grad.astype(BF)
    sums_ref[0:1] = column_sum(upstream * unit)
    sums_ref[1:2] = column_sum(upstream)
    sums_ref[2:3] = column_sum(grad)


def feed_forward_back(third_low, third, slope, up_pieces, down_pieces, unit, spread, gain):
    rows, features = third.shape
    groups, cols = up_pieces[0].shape[1], up_pieces[0].shape[3]
    count = len(up_pieces)

    def body(third_low_ref, third_ref, slope_ref, *refs):
        ups, downs = refs[:count], refs[count : 2 * count]
        unit_ref, spread_ref, gain_ref = refs[2 * count : 2 * count + 3]
        upper_ref, bias_ref, grad_ref, grad_low_ref, sums_ref, acc_ref = refs[2 * count + 3 :]
        step = pl.program_id(0)

        @pl.when(step == 0)
        def _():
            acc_ref[...] = jnp.zeros_like(acc_ref)

        grad_upper = over_features(third_low_ref[...], downs) * slope_ref[...].astype(F32)
        bias_ref[...] = column_sum(grad_upper)
        low = grad_upper.astype(BF)
        upper_ref[...] = low
        add_rows(acc_ref, low, ups)

        @pl.when(step == groups - 1)
        def _():
            norm_back_outputs(
                acc_ref[...] + third_ref[...],
                unit_ref[...],
                spread_ref[...],
                gain_ref[...],
                grad_ref,
                grad_low_ref,
                sums_ref,
            )

    return pl.pallas_call(
        body,
        grid=(groups,),
        in_specs=[
            whole((rows, features)),
            whole((rows, features)),
            pl.BlockSpec((rows, cols), lambda j: (0, j)),
        ]
        + piece_specs(up_pieces, cols, 0)
        + piece_specs(down_pieces, cols, 0)
        + [whole((rows, features)), whole((rows, 1)), whole((1, features))],
        out_specs=[
            pl.BlockSpec((rows, cols), lambda j: (0, j)),
            pl.BlockSpec((1, cols), lambda j: (0, j)),
            whole((rows, features)),
            whole((rows, features)),
            whole((3, features)),
        ],
        out_shape=[
            jax.ShapeDtypeStruct((rows, groups * cols), BF),
            jax.ShapeDtypeStruct((1, groups * cols), F32),
            jax.ShapeDtypeStruct((rows, features), F32),
            jax.ShapeDtypeStruct((rows, features), BF),
            jax.ShapeDtypeStruct((3, features), F32),
        ],
        scratch_shapes=[pltpu.VMEM((rows, features), F32)],
        compiler_params=params(),
        name="feed_forward_back",
    )(third_low, third, slope, *up_pieces, *down_pieces, unit, spread, gain)


def cross_query_back(grad_query, pieces, first_col, cols, second, unit, spread, gain):
    rows, features = second.shape
    groups = pieces[0].shape[1]
    count = len(pieces)

    def body(left_ref, *refs):
        piece_refs = refs[:count]
        second_ref, unit_ref, spread_ref, gain_ref, grad_ref, grad_low_ref, sums_ref, acc_ref = refs[
            count:
        ]
        step = pl.program_id(0)

        @pl.when(step == 0)
        def _():
            acc_ref[...] = second_ref[...]

        add_rows(acc_ref, left_ref[...], piece_refs)

        @pl.when(step == groups - 1)
        def _():
            norm_back_outputs(
                acc_ref[...],
                unit_ref[...],
                spread_ref[...],
                gain_ref[...],
                grad_ref,
                grad_low_ref,
                sums_ref,
            )

    return pl.pallas_call(
        body,
        grid=(groups,),
        in_specs=[pl.BlockSpec((rows, cols), lambda j: (0, j))]
        + piece_specs(pieces, cols, first_col // cols)
        + [whole((rows, features)), whole((rows, features)), whole((rows, 1)), whole((1, features))],
        out_specs=[whole((rows, features)), whole((rows, features)), whole((3, features))],
        out_shape=[
            jax.ShapeDtypeStruct((rows, features), F32),
            jax.ShapeDtypeStruct((rows, features), BF),
            jax.ShapeDtypeStruct((3, features), F32),
        ],
        scratch_shapes=[pltpu.VMEM((rows, features), F32)],
        compiler_params=params(),
        name="cross_query_back",
    )(grad_query, *pieces, second, unit, spread, gain)


def rows_back(left, pieces, first_col, cols, name):
    rows = left.shape[0]
    count = len(pieces)
    groups = pieces[0].shape[1]
    features = count * pieces[0].shape[0] * pieces[0].shape[2]

    def body(left_ref, *refs):
        piece_refs = refs[:count]
        out_ref, acc_ref = refs[count:]
        step = pl.program_id(0)

        @pl.when(step == 0)
        def _():
            acc_ref[...] = jnp.zeros_like(acc_ref)

        add_rows(acc_ref, left_ref[...], piece_refs)

        @pl.when(step == groups - 1)
        def _():
            out_ref[...] = acc_ref[...].astype(BF)

    return pl.pallas_call(
        body,
        grid=(groups,),
        in_specs=[pl.BlockSpec((rows, cols), lambda j: (0, j))]
        + piece_specs(pieces, cols, first_col // cols),
        out_specs=whole((rows, features)),
        out_shape=jax.ShapeDtypeStruct((rows, features), BF),
        scratch_shapes=[pltpu.VMEM((rows, features), F32)],
        compiler_params=params(),
        name=name,
    )(left, *pieces)


def input_back(grad_query, grad_kv, grad_rel, pieces, first):
    rows, features = first.shape
    long_rows = grad_kv.shape[0]
    halo = long_rows - rows
    groups = pieces[0].shape[1]
    count = len(pieces)
    width = grad_query.shape[1] // groups
    rel_width = grad_rel.shape[1] // groups

    def body(query_ref, kv_ref, rel_ref, *refs):
        parts = [refs[count * k : count * (k + 1)] for k in range(4)]
        first_ref, halo_ref, own_ref, acc_ref = refs[4 * count :]
        step = pl.program_id(0)

        @pl.when(step == 0)
        def _():
            acc_ref[0:halo] = jnp.zeros((halo, features), F32)
            acc_ref[halo:] = first_ref[...]

        own_acc = acc_ref.at[halo:]
        add_rows(own_acc, query_ref[...], parts[0])
        add_rows(acc_ref, kv_ref[:, 0:width], parts[1])
        add_rows(acc_ref, kv_ref[:, width : 2 * width], parts[2])
        add_rows(own_acc, rel_ref[...], parts[3])

        @pl.when(step == groups - 1)
        def _():
            halo_ref[...] = acc_ref[0:halo].astype(BF)
            own_ref[...] = acc_ref[halo:]

    return pl.pallas_call(
        body,
        grid=(groups,),
        in_specs=[
            pl.BlockSpec((rows, width), lambda j: (0, j)),
            pl.BlockSpec((long_rows, 2 * width), lambda j: (0, j)),
            pl.BlockSpec((rows, rel_width), lambda j: (0, j)),
        ]
        + piece_specs(pieces, width, 0)
        + piece_specs(pieces, width, 1)
        + piece_specs(pieces, width, 2)
        + piece_specs(pieces, rel_width, 3 * width // rel_width)
        + [whole((rows, features))],
        out_specs=[whole((halo, features)), whole((rows, features))],
        out_shape=[
            jax.ShapeDtypeStruct((halo, features), BF),
            jax.ShapeDtypeStruct((rows, features), F32),
        ],
        scratch_shapes=[pltpu.VMEM((long_rows, features), F32)],
        compiler_params=params(),
        name="input_back",
    )(grad_query, grad_kv, grad_rel, *pieces, *pieces, *pieces, *pieces, first)


def weight_products(entries, half, extra, pieces, groups, name):
    features = entries[0][0].shape[1]
    depth = features // 2
    blk = depth // pieces
    widths = [right.shape[1] // groups for _, right in entries]
    total = sum(widths)
    count = len(entries)

    def body(*refs):
        lefts, rights = refs[:count], refs[count : 2 * count]
        out_ref = refs[-1]
        at = 0
        for left_ref, right_ref, width in zip(lefts, rights, widths):
            term = dot(left_ref[...], right_ref[...], 0, 0).reshape(pieces, 1, blk, width)
            if extra is not None:
                term = term + refs[2 * count][:, :, :, at : at + width].astype(F32)
            out_ref[:, :, :, at : at + width] = term.astype(BF)
            at += width

    out_spec = pl.BlockSpec((pieces, 1, blk, total), lambda j: (0, j, 0, 0))
    in_specs = [pl.BlockSpec((left.shape[0], depth), lambda j: (0, half)) for left, _ in entries]
    in_specs += [
        pl.BlockSpec((right.shape[0], width), lambda j: (0, j))
        for (_, right), width in zip(entries, widths)
    ]
    operands = [left for left, _ in entries] + [right for _, right in entries]
    if extra is not None:
        in_specs.append(out_spec)
        operands.append(extra)
    return pl.pallas_call(
        body,
        grid=(groups,),
        in_specs=in_specs,
        out_specs=out_spec,
        out_shape=jax.ShapeDtypeStruct((pieces, groups, blk, total), BF),
        compiler_params=params(),
        name=name,
    )(*operands)


def weight_gradient(entries, batch_order, name):
    groups = lax.axis_size("head")
    pieces = lax.axis_size("batch") // 2
    sent = weight_products(entries, 1, None, pieces, groups, name + "_send")
    came = swap(sent, "batch", 1)
    kept = weight_products(entries, 0, came, pieces, groups, name + "_keep")
    return scatter_pieces(kept, batch_order)


def half_masks(rows):
    lane = lax.broadcasted_iota(jnp.int32, (rows, 128), 1)
    return [
        jnp.where((lane >= 64 * half) & (lane < 64 * half + 64), 1.0, 0.0).astype(F32)
        for half in range(2)
    ]


def skew(array_in, share):
    rows, width = array_in.shape
    parts = [
        pltpu.roll(array_in[n * share : (n + 1) * share], width - share + 1, 1, stride=1, stride_axis=0)
        for n in range(rows // share)
    ]
    return jnp.concatenate(parts, 0)


def self_attention(qkv, relpos, mask, turned, share):
    rows, window = 3 * share, 3 * share
    groups = qkv.shape[1] // 768
    halo = qkv.shape[0] - rows

    def body(q_ref, k_ref, v_ref, rel_ref, mask_ref, turned_ref, ctx_ref, probs_ref, own_ref):
        halves = half_masks(rows)
        lane = lax.broadcasted_iota(jnp.int32, (rows, 128), 1)
        rel = rel_ref[...]
        high = rel.astype(BF)
        split = jnp.concatenate([high, (rel - high.astype(F32)).astype(BF)], 1)
        row_id = lax.broadcasted_iota(jnp.int32, (256, window), 0) & 127
        own_all = jnp.zeros((rows, 128), F32)
        for pair in range(2):
            cols = slice(128 * pair, 128 * pair + 128)
            q = q_ref[halo:, cols]
            k, v = k_ref[0:window, cols], v_ref[0:window, cols]
            own_k = k_ref[halo:, cols].astype(F32)
            own_v = v_ref[halo:, cols].astype(F32)
            product = q.astype(F32) * own_k
            mixed = jnp.zeros((rows, 128), F32)
            for half in range(2):
                head = 2 * pair + half
                scores = dot(q * halves[half].astype(BF), k, 1, 1)
                table = jnp.where(row_id == turned_ref[...] + 32 * head, 1.0, 0.0).astype(BF)
                scores = scores + skew(dot(split, table, 1, 0), share) + mask_ref[...]
                own = jnp.sum(
                    product * halves[half] + jnp.where(lane == 32 * head, rel, 0.0), -1, keepdims=True
                )
                track = lax.broadcasted_iota(jnp.int32, (rows, 1), 0) >= share
                own = jnp.where(track, own, MASKED)
                top = jnp.maximum(jnp.max(scores, -1, keepdims=True), own)
                raised = jnp.exp(scores - top)
                own_raised = jnp.exp(own - top)
                scale = 1.0 / (jnp.sum(raised, -1, keepdims=True) + own_raised)
                probs = (raised * scale).astype(BF)
                own_probs = (own_raised * scale).astype(BF).astype(F32)
                probs_ref[head] = probs
                own_all = jnp.where(lane == head, own_probs, own_all)
                mixed = mixed + (dot(probs, v, 1, 0) + own_probs * own_v) * halves[half]
            ctx_ref[:, cols] = mixed.astype(BF)
        own_ref[...] = own_all

    long_rows = qkv.shape[0]
    return pl.pallas_call(
        body,
        grid=(groups,),
        in_specs=[
            pl.BlockSpec((long_rows, 256), lambda j: (0, 3 * j)),
            pl.BlockSpec((long_rows, 256), lambda j: (0, 3 * j + 1)),
            pl.BlockSpec((long_rows, 256), lambda j: (0, 3 * j + 2)),
            pl.BlockSpec((rows, 128), lambda j: (0, j)),
            whole((rows, window)),
            whole((1, window)),
        ],
        out_specs=[
            pl.BlockSpec((rows, 256), lambda j: (0, j)),
            pl.BlockSpec((4, rows, window), lambda j: (j, 0, 0)),
            pl.BlockSpec((rows, 128), lambda j: (0, j)),
        ],
        out_shape=[
            jax.ShapeDtypeStruct((rows, groups * 256), BF),
            jax.ShapeDtypeStruct((4 * groups, rows, window), BF),
            jax.ShapeDtypeStruct((rows, groups * 128), F32),
        ],
        compiler_params=params(),
        name="self_attention",
    )(qkv, qkv, qkv, relpos, mask, turned)


def self_attention_back(qkv, probs, own_probs, grad_ctx, straight, share):
    rows, window = 3 * share, 3 * share
    groups = qkv.shape[1] // 768
    halo = qkv.shape[0] - rows
    long_rows = qkv.shape[0]

    def body(
        q_ref, k_ref, v_ref, probs_ref, own_ref, grad_ref, straight_ref,
        gq_ref, gkv_ref, grel_ref, sums_ref, rel_sums_ref,
    ):
        halves = half_masks(rows)
        lane = lax.broadcasted_iota(jnp.int32, (rows, 128), 1)
        turn = jnp.where(
            lax.broadcasted_iota(jnp.int32, (window, window), 0)
            + lax.broadcasted_iota(jnp.int32, (window, window), 1)
            == window - 1,
            1.0,
            0.0,
        ).astype(BF)
        column = lax.broadcasted_iota(jnp.int32, (window, 128), 1)
        grel = jnp.zeros((rows, 128), F32)
        for pair in range(2):
            cols = slice(128 * pair, 128 * pair + 128)
            q = q_ref[halo:, cols]
            k, v = k_ref[0:window, cols], v_ref[0:window, cols]
            own_k = k_ref[halo:, cols].astype(F32)
            own_v = v_ref[halo:, cols].astype(F32)
            grad = grad_ref[:, cols]
            grad_wide = grad.astype(F32)
            own_product = grad_wide * own_v
            gq = jnp.zeros((rows, 128), F32)
            own_spread = jnp.zeros((rows, 128), F32)
            own_weight = jnp.zeros((rows, 128), F32)
            score_parts, prob_parts, q_parts, g_parts = [], [], [], []
            for half in range(2):
                head = 2 * pair + half
                low_half = halves[half].astype(BF)
                p = probs_ref[head]
                p_wide = p.astype(F32)
                grad_half = grad * low_half
                grad_probs = dot(grad_half, v, 1, 1)
                own_p = jnp.sum(jnp.where(lane == head, own_ref[...], 0.0), -1, keepdims=True)
                own_grad = jnp.sum(own_product * halves[half], -1, keepdims=True)
                row_dot = jnp.sum(p_wide * grad_probs, -1, keepdims=True) + own_p * own_grad
                grad_scores = (p_wide * (grad_probs - row_dot)).astype(BF)
                grad_own = (own_p * (own_grad - row_dot)).astype(BF).astype(F32)
                gq = gq + (dot(grad_scores, k, 1, 0) + grad_own * own_k) * halves[half]
                own_spread = own_spread + grad_own * halves[half]
                own_weight = own_weight + own_p * halves[half]
                score_parts.append(grad_scores)
                prob_parts.append(p)
                q_parts.append(q * low_half)
                g_parts.append(grad_half)
                turned = skew(dot(grad_scores, turn, 1, 0), share).astype(BF)
                table = jnp.where(column == straight_ref[...] + 32 * head, 1.0, 0.0).astype(BF)
                grel = grel + dot(turned, table, 1, 0) + jnp.where(lane == 32 * head, grad_own, 0.0)
            gk = dot(
                jnp.concatenate(q_parts, 0), jnp.concatenate(score_parts, 0), 0, 0
            ).T
            gv = dot(
                jnp.concatenate(g_parts, 0), jnp.concatenate(prob_parts, 0), 0, 0
            ).T
            gq = gq * 0.125
            gq_ref[:, cols] = gq.astype(BF)
            own_gk = own_spread * q.astype(F32)
            own_gv = own_weight * grad_wide
            vcols = slice(256 + 128 * pair, 256 + 128 * pair + 128)
            gkv_ref[0:window, cols] = gk.astype(BF)
            gkv_ref[0:window, vcols] = gv.astype(BF)
            gkv_ref[window:, cols] = own_gk[share:].astype(BF)
            gkv_ref[window:, vcols] = own_gv[share:].astype(BF)
            sums_ref[0:1, cols] = column_sum(gq)
            sums_ref[1:2, cols] = column_sum(gv) + column_sum(own_gv[share:])
        grel_ref[...] = grel.astype(BF)
        rel_sums_ref[...] = column_sum(grel)

    return pl.pallas_call(
        body,
        grid=(groups,),
        in_specs=[
            pl.BlockSpec((long_rows, 256), lambda j: (0, 3 * j)),
            pl.BlockSpec((long_rows, 256), lambda j: (0, 3 * j + 1)),
            pl.BlockSpec((long_rows, 256), lambda j: (0, 3 * j + 2)),
            pl.BlockSpec((4, rows, window), lambda j: (j, 0, 0)),
            pl.BlockSpec((rows, 128), lambda j: (0, j)),
            pl.BlockSpec((rows, 256), lambda j: (0, j)),
            whole((window, 1)),
        ],
        out_specs=[
            pl.BlockSpec((rows, 256), lambda j: (0, j)),
            pl.BlockSpec((long_rows, 512), lambda j: (0, j)),
            pl.BlockSpec((rows, 128), lambda j: (0, j)),
            pl.BlockSpec((2, 256), lambda j: (0, j)),
            pl.BlockSpec((1, 128), lambda j: (0, j)),
        ],
        out_shape=[
            jax.ShapeDtypeStruct((rows, groups * 256), BF),
            jax.ShapeDtypeStruct((long_rows, groups * 512), BF),
            jax.ShapeDtypeStruct((rows, groups * 128), BF),
            jax.ShapeDtypeStruct((2, groups * 256), F32),
            jax.ShapeDtypeStruct((1, groups * 128), F32),
        ],
        compiler_params=params(),
        name="self_attention_back",
    )(qkv, qkv, qkv, probs, own_probs, grad_ctx, straight)


def cross_attention(queries, kv):
    rows, places = queries.shape[0], kv.shape[0]
    groups = queries.shape[1] // 256

    def body(q_ref, k_ref, v_ref, ctx_ref, probs_ref):
        halves = half_masks(rows)
        for pair in range(2):
            cols = slice(128 * pair, 128 * pair + 128)
            q, k, v = q_ref[:, cols], k_ref[:, cols], v_ref[:, cols]
            mixed = jnp.zeros((rows, 128), F32)
            for half in range(2):
                scores = dot(q * halves[half].astype(BF), k, 1, 1)
                raised = jnp.exp(scores - jnp.max(scores, -1, keepdims=True))
                probs = (raised * (1.0 / jnp.sum(raised, -1, keepdims=True))).astype(BF)
                probs_ref[2 * pair + half] = probs
                mixed = mixed + dot(probs, v, 1, 0) * halves[half]
            ctx_ref[:, cols] = mixed.astype(BF)

    return pl.pallas_call(
        body,
        grid=(groups,),
        in_specs=[
            pl.BlockSpec((rows, 256), lambda j: (0, j)),
            pl.BlockSpec((places, 256), lambda j: (0, 2 * j)),
            pl.BlockSpec((places, 256), lambda j: (0, 2 * j + 1)),
        ],
        out_specs=[
            pl.BlockSpec((rows, 256), lambda j: (0, j)),
            pl.BlockSpec((4, rows, places), lambda j: (j, 0, 0)),
        ],
        out_shape=[
            jax.ShapeDtypeStruct((rows, groups * 256), BF),
            jax.ShapeDtypeStruct((4 * groups, rows, places), BF),
        ],
        compiler_params=params(),
        name="cross_attention",
    )(queries, kv, kv)


def cross_attention_back(queries, kv, probs, grad_ctx):
    rows, places = queries.shape[0], kv.shape[0]
    groups = queries.shape[1] // 256

    def body(q_ref, k_ref, v_ref, probs_ref, grad_ref, gq_ref, gkv_ref, sums_ref):
        halves = half_masks(rows)
        for pair in range(2):
            cols = slice(128 * pair, 128 * pair + 128)
            q, k, v, grad = q_ref[:, cols], k_ref[:, cols], v_ref[:, cols], grad_ref[:, cols]
            gq = jnp.zeros((rows, 128), F32)
            score_parts, prob_parts, q_parts, g_parts = [], [], [], []
            for half in range(2):
                low_half = halves[half].astype(BF)
                p = probs_ref[2 * pair + half]
                p_wide = p.astype(F32)
                grad_half = grad * low_half
                grad_probs = dot(grad_half, v, 1, 1)
                row_dot = jnp.sum(p_wide * grad_probs, -1, keepdims=True)
                grad_scores = (p_wide * (grad_probs - row_dot)).astype(BF)
                gq = gq + dot(grad_scores, k, 1, 0) * halves[half]
                score_parts.append(grad_scores)
                prob_parts.append(p)
                q_parts.append(q * low_half)
                g_parts.append(grad_half)
            gk = dot(
                jnp.concatenate(q_parts, 0), jnp.concatenate(score_parts, 0), 0, 0
            ).T
            gv = dot(
                jnp.concatenate(g_parts, 0), jnp.concatenate(prob_parts, 0), 0, 0
            ).T
            gq = gq * 0.125
            gq_ref[:, cols] = gq.astype(BF)
            vcols = slice(256 + 128 * pair, 256 + 128 * pair + 128)
            gkv_ref[:, cols] = gk.astype(BF)
            gkv_ref[:, vcols] = gv.astype(BF)
            sums_ref[0:1, cols] = column_sum(gq)
            sums_ref[1:2, cols] = column_sum(gv)

    return pl.pallas_call(
        body,
        grid=(groups,),
        in_specs=[
            pl.BlockSpec((rows, 256), lambda j: (0, j)),
            pl.BlockSpec((places, 256), lambda j: (0, 2 * j)),
            pl.BlockSpec((places, 256), lambda j: (0, 2 * j + 1)),
            pl.BlockSpec((4, rows, places), lambda j: (j, 0, 0)),
            pl.BlockSpec((rows, 256), lambda j: (0, j)),
        ],
        out_specs=[
            pl.BlockSpec((rows, 256), lambda j: (0, j)),
            pl.BlockSpec((places, 512), lambda j: (0, j)),
            pl.BlockSpec((2, 256), lambda j: (0, j)),
        ],
        out_shape=[
            jax.ShapeDtypeStruct((rows, groups * 256), BF),
            jax.ShapeDtypeStruct((places, groups * 512), BF),
            jax.ShapeDtypeStruct((2, groups * 256), F32),
        ],
        compiler_params=params(),
        name="cross_attention_back",
    )(queries, kv, kv, probs, grad_ctx)


def per_device(
    hidden,
    memory,
    grad_out,
    lengths,
    key_mask,
    buckets,
    self_weight,
    relpos_weight,
    selfout_weight,
    crossq_weight,
    crosskv_weight,
    crossout_weight,
    up_weight,
    down_weight,
    self_bias,
    relpos_bias,
    cross_bias,
    up_bias,
    norm_gain,
    norm_bias,
    out_bias,
):
    batches, groups = lax.axis_size("batch"), lax.axis_size("head")
    b, z = lax.axis_index("batch"), lax.axis_index("head")
    nb = bits_of("batch")
    share, features = hidden.shape[1], hidden.shape[3]
    length = share * groups
    rows, window = 3 * share, 3 * share
    assert share == 128 and hidden.shape[0] == 1 and WIDEST_DOC <= 2 * share
    assert batches == 1 << nb and features % batches == 0 and groups == 4
    near, far = list(range(1, nb)), list(reversed(range(1, nb)))

    turned_ids = jnp.array([bit_reverse(p, nb) for p in range(batches)], jnp.int32)
    to_exchange = b ^ turned_ids
    natural = lax.iota(jnp.int32, batches) ^ b
    to_natural = jnp.zeros_like(natural)
    for bit in range(nb):
        to_natural = to_natural | (((natural >> bit) & 1) << (nb - 1 - bit))
    group_order = z ^ lax.iota(jnp.int32, groups)

    def small_features(stack):
        count = stack.shape[0]
        blocks = stack.reshape(count, batches, features // batches)
        return jnp.take(blocks, to_exchange, axis=1).reshape(count, features)

    def by_group(vector):
        return jnp.take(vector.reshape(groups, -1), group_order, axis=0)

    blk = self_weight.shape[0]
    weights_self = gather_pieces(
        jnp.concatenate([self_weight.reshape(blk, -1), relpos_weight], 1).astype(BF), near
    )
    weights_cross = gather_pieces(
        jnp.concatenate(
            [selfout_weight, crossq_weight, crosskv_weight.reshape(blk, -1), crossout_weight], 1
        ).astype(BF),
        far,
    )
    weights_up = gather_pieces(up_weight.astype(BF), near)
    weights_down = gather_pieces(down_weight.astype(BF), far)

    own = jnp.transpose(hidden[0], (1, 0, 2)).reshape(rows, features)
    own = reorder_blocks(own, to_exchange)
    main = own[0:share]
    chain = list(range(groups))
    before_one = lax.ppermute(main, "head", [(i, i + 1) for i in chain[:-1]])
    before_two = lax.ppermute(main, "head", [(i, i + 2) for i in chain[:-2]])
    extended = jnp.concatenate([before_two, before_one, own], 0)
    memory_all = reorder_blocks(memory[0], to_exchange)
    memory_all = jnp.concatenate([memory_all, swap(memory_all, "head", 1)], 0)
    memory_all = jnp.concatenate([memory_all, swap(memory_all, "head", 2)], 0)
    upstream = lax.dynamic_slice_in_dim(grad_out[0], z * share, share, 0)
    upstream = jnp.transpose(upstream, (1, 0, 2)).reshape(rows, features)
    upstream = reorder_blocks(upstream, to_exchange)

    vectors = small_features(jnp.concatenate([norm_gain, norm_bias, out_bias], 0))
    vectors = vectors.reshape(3, 3, features).transpose(1, 0, 2)
    ones = jnp.ones((groups, 256), F32)
    none = jnp.zeros((groups, 256), F32)
    query_bias, value_bias = by_group(self_bias[0]), by_group(self_bias[1])
    qkv_affine = jnp.stack(
        [
            jnp.concatenate([query_bias, none, value_bias], 1).reshape(-1),
            jnp.concatenate([0.125 * ones, ones, ones], 1).reshape(-1),
        ]
    )
    rel_affine = jnp.stack([by_group(relpos_bias).reshape(-1), jnp.ones((groups * 128,), F32)])
    cross_query_affine = jnp.stack(
        [by_group(cross_bias[0]).reshape(-1), jnp.full((groups * 256,), 0.125, F32)]
    )
    cross_kv_affine = jnp.stack(
        [
            jnp.concatenate([none, by_group(cross_bias[1])], 1).reshape(-1),
            jnp.ones((groups * 512,), F32),
        ]
    )
    up_row = by_group(up_bias).reshape(1, -1)

    places = lax.iota(jnp.int32, length)
    doc_ends = jnp.cumsum(lengths[0])
    segment = jnp.sum((places[:, None] >= doc_ends[None, :]).astype(jnp.int32), -1)
    lead = window - share
    padded_segment = jnp.concatenate([jnp.full((lead,), -1, jnp.int32), segment])
    padded_mask = jnp.concatenate([jnp.zeros((lead,), jnp.int32), key_mask[0]])
    key_segment = lax.dynamic_slice_in_dim(padded_segment, z * share, window)
    key_open = lax.dynamic_slice_in_dim(padded_mask, z * share, window)
    query_segment = lax.dynamic_slice_in_dim(segment, z * share, share)
    query_at = lax.iota(jnp.int32, share)[:, None] + lead
    key_at = lax.iota(jnp.int32, window)[None, :]
    joined = (query_segment[:, None] == key_segment[None, :]) & (
        (key_open[None, :] == 1) | (query_at == key_at)
    )
    allowed_main = joined & (key_at <= query_at)
    allowed_pred = joined & (key_at < query_at)
    mask = jnp.where(jnp.stack([allowed_main, allowed_pred, allowed_pred]), 0.0, MASKED)
    mask = mask.reshape(rows, window).astype(F32)
    straight = buckets[0:window]
    turned = straight[::-1]

    qkv = project(extended, weights_self, 0, 768, 256, qkv_affine, BF, "self_qkv")
    relpos = project(own, weights_self, 768, 128, 128, rel_affine, F32, "self_rel")
    context, self_probs, self_own = self_attention(qkv, relpos, mask, turned.reshape(1, -1), share)
    normed1, normed1_low, unit1, spread1 = close_sublayer(
        context, weights_cross, 0, 256, own, vectors[0], "self_out"
    )
    cross_kv = project(memory_all, weights_cross, 512, 512, 512, cross_kv_affine, BF, "cross_kv")
    cross_q = project(
        normed1_low, weights_cross, 256, 256, 256, cross_query_affine, BF, "cross_q"
    )
    cross_context, cross_probs = cross_attention(cross_q, cross_kv)
    normed2, normed2_low, unit2, spread2 = close_sublayer(
        cross_context, weights_cross, 1024, 256, normed1, vectors[1], "cross_out"
    )
    active, slope, out_low, third, third_low, sums_third = feed_forward(
        normed2_low, normed2, weights_up, weights_down, up_row, vectors[2], upstream
    )
    out_low = reorder_blocks(out_low, to_natural).reshape(3, share, features)
    layer_out = lax.all_gather(jnp.transpose(out_low, (1, 0, 2)), "head", axis=0, tiled=True)[None]

    grad_down = weight_gradient([(third_low, active)], far, "down_grad")
    upper_low, up_sums, second, second_low, sums_second = feed_forward_back(
        third_low, third, slope, weights_up, weights_down, unit2, spread2, vectors[1][0:1]
    )
    grad_up = weight_gradient([(normed2_low, upper_low)], near, "up_grad")
    grad_cross_ctx = project_plain(second_low, weights_cross, 1024, 256, "cross_ctx_back")
    grad_cross_q, grad_cross_kv, cross_sums = cross_attention_back(
        cross_q, cross_kv, cross_probs, grad_cross_ctx
    )
    grads_cross = weight_gradient(
        [
            (normed1_low, grad_cross_q),
            (memory_all, grad_cross_kv),
            (second_low, cross_context),
        ],
        far,
        "cross_grad",
    )
    memory_part = rows_back(grad_cross_kv, weights_cross, 512, 512, "memory_back")
    first, first_low, sums_first = cross_query_back(
        grad_cross_q, weights_cross, 256, 256, second, unit1, spread1, vectors[0][0:1]
    )
    grad_context = project_plain(first_low, weights_cross, 0, 256, "self_ctx_back")
    grad_q, grad_kv, grad_rel, self_sums, rel_sums = self_attention_back(
        qkv, self_probs, self_own, grad_context, straight.reshape(-1, 1), share
    )
    grads_self = weight_gradient(
        [
            (own, grad_q),
            (extended, grad_kv),
            (own, grad_rel),
            (first_low, context),
        ],
        near,
        "self_grad",
    )
    halo_grad, own_grad = input_back(grad_q, grad_kv, grad_rel, weights_self, first)

    from_two = lax.ppermute(halo_grad[0:share], "head", [(i + 2, i) for i in chain[:-2]])
    from_one = lax.ppermute(halo_grad[share:], "head", [(i + 1, i) for i in chain[:-1]])
    main_grad = own_grad[0:share] + from_one.astype(F32) + from_two.astype(F32)
    own_grad = jnp.concatenate([main_grad, own_grad[share:]], 0)
    own_grad = reorder_blocks(own_grad, to_natural).reshape(3, share, features)
    grad_hidden = jnp.transpose(own_grad, (1, 0, 2))[None]
    span = memory.shape[1]
    pairs = memory_part.reshape(2, 2 * span, features)
    memory_half = pairs[0].astype(F32) + swap(pairs[1], "head", 2).astype(F32)
    memory_half = memory_half.astype(BF)
    memory_grad = memory_half[:span].astype(F32) + swap(memory_half[span:], "head", 1).astype(F32)
    grad_memory = reorder_blocks(memory_grad, to_natural)[None]

    def natural_groups(block):
        return jnp.take(block.reshape(-1, groups, block.shape[1] // groups), group_order, axis=1)

    feature_sums = jnp.concatenate([sums_first, sums_second, sums_third], 0)
    feature_sums = jnp.take(
        feature_sums.reshape(9, batches, features // batches), to_natural, axis=1
    ).reshape(3, 3, features)
    packed = jnp.concatenate(
        [
            natural_groups(self_sums).reshape(-1),
            natural_groups(rel_sums).reshape(-1),
            natural_groups(cross_sums).reshape(-1),
            natural_groups(up_sums).reshape(-1),
            feature_sums.reshape(-1),
        ]
    )
    for bit in range(nb):
        packed = packed + swap(packed, "batch", 1 << bit)
    for bit in range(bits_of("head")):
        packed = packed + swap(packed, "head", 1 << bit)
    ends = [0]
    for size in (2 * features, groups * 128, 2 * features, up_bias.shape[0], 9 * features):
        ends.append(ends[-1] + size)
    self_bias_grad = packed[ends[0] : ends[1]].reshape(2, -1)
    relpos_bias_grad = packed[ends[1] : ends[2]]
    cross_bias_grad = packed[ends[2] : ends[3]].reshape(2, -1)
    up_bias_grad = packed[ends[3] : ends[4]]
    feature_sums = packed[ends[4] : ends[5]].reshape(3, 3, features)

    return (
        layer_out,
        grad_hidden,
        grad_memory,
        jnp.concatenate(
            [
                grads_self[:, 0:256].reshape(blk, 1, 256),
                grads_self[:, 256:768].reshape(blk, 2, 256),
            ],
            1,
        ),
        grads_self[:, 768:896],
        grads_self[:, 896:1152],
        grads_cross[:, 0:256],
        grads_cross[:, 256:768].reshape(blk, 2, 256),
        grads_cross[:, 768:1024],
        grad_up,
        grad_down,
        self_bias_grad,
        relpos_bias_grad,
        cross_bias_grad,
        up_bias_grad,
        feature_sums[:, 0],
        feature_sums[:, 1],
        feature_sums[:, 2],
    )


def solution(mesh):
    in_specs = (
        P("batch", "head", None, None),
        P("batch", "head", None),
        P("batch", None, None, None),
        P("batch", None),
        P("batch", None),
        P(),
        P("batch", None, "head"),
        P("batch", "head"),
        P("batch", "head"),
        P("batch", "head"),
        P("batch", None, "head"),
        P("batch", "head"),
        P("batch", "head"),
        P("batch", "head"),
        P(),
        P(),
        P(),
        P(),
        P(),
        P(),
        P(),
    )
    out_specs = (
        P("batch", None, None, None),
        P("batch", "head", None, None),
        P("batch", "head", None),
        P("batch", None, "head"),
        P("batch", "head"),
        P("batch", "head"),
        P("batch", "head"),
        P("batch", None, "head"),
        P("batch", "head"),
        P("batch", "head"),
        P("batch", "head"),
        P(),
        P(),
        P(),
        P(),
        P(),
        P(),
        P(),
    )
    return jax.shard_map(
        per_device, mesh=mesh, in_specs=in_specs, out_specs=out_specs, check_vma=False
    )
```

```python
import functools

import jax
import jax.numpy as jnp
from jax import lax
from jax.experimental import pallas as pl
from jax.experimental.layout import Layout, with_layout_constraint
from jax.experimental.pallas import tpu as pltpu
from jax.sharding import PartitionSpec as P

BUCKETS = 32
HEAD_DIM = 64
WIDEST_DOC = 256
EPSILON = 1e-05
MASKED = -1e30
BF = jnp.bfloat16
F32 = jnp.float32
VMEM_BYTES = 56 * 1024 * 1024


def params():
    return pltpu.CompilerParams(vmem_limit_bytes=VMEM_BYTES)


def dot(a, b, ca, cb):
    return lax.dot_general(a, b, (((ca,), (cb,)), ((), ())), preferred_element_type=F32)


def whole(shape):
    return pl.BlockSpec(shape, lambda *_: (0,) * len(shape))


def swap(array_in, axis, bit):
    count = lax.axis_size(axis)
    return lax.ppermute(array_in, axis, [(i, i ^ bit) for i in range(count)])


def bits_of(axis):
    return (lax.axis_size(axis) - 1).bit_length()


def after(value, *earlier):
    return lax.optimization_barrier((value,) + earlier)[0]


def pin(value):
    return with_layout_constraint(value, Layout(tuple(range(value.ndim))))


class Line:
    def __init__(self):
        self.last = ()

    def tie(self, value):
        return after(value, *self.last) if self.last else value

    def mark(self, *values):
        self.last = values
        return values[0]


class Gather:
    def __init__(self, line, shard):
        self.line = line
        self.nb, self.nz = bits_of("batch"), bits_of("head")
        self.buf = pin(shard).reshape((1,) * (self.nb + self.nz) + shard.shape)

    def send(self, axis_name, bit):
        self.axis = self.nb + self.nz - 1 - bit if axis_name == "head" else bit
        self.came = swap(self.line.tie(self.buf), axis_name, 1 << bit)

    def take(self):
        mine = self.line.tie(self.buf)
        self.buf = self.line.mark(jnp.concatenate([mine, self.came], self.axis))

    def columns(self, first, count):
        part = Gather.__new__(Gather)
        part.line, part.nb, part.nz = self.line, self.nb, self.nz
        part.buf = pin(self.buf[..., first : first + count])
        return part

    def close(self):
        shape = (1 << (self.nb - 1), 1 << self.nz) + self.buf.shape[-2:]
        return (self.buf.reshape(shape), self.came.reshape(shape))


class Scatter:
    def __init__(self, line, parts, orders):
        nb, self.nz = bits_of("batch"), bits_of("head")
        self.line = line
        self.groups = parts[0][1].shape[1]
        self.blk = parts[0][1].shape[2]
        self.left = [list(order) for order in orders]
        self.names = [sorted(order) for order in orders]
        self.heads = list(range(self.nz))
        self.mine, self.came = [None] * len(parts), [None] * len(parts)
        for number, (theirs, mine) in enumerate(parts):
            self.send(number, theirs, mine)

    def send(self, number, theirs, mine):
        bit = self.left[number].pop(0)
        self.names[number].remove(bit)
        self.mine[number] = mine
        self.came[number] = swap(theirs, "batch", 1 << bit)

    def step(self):
        tied = [self.line.tie(mine) for mine in self.mine]
        came = [after(came, mine) for came, mine in zip(self.came, tied)]
        if self.left[0]:
            halves = []
            for number, (old, new) in enumerate(zip(tied, came)):
                inner = (2,) * len(self.names[number]) + (self.groups, self.blk, old.shape[-1])
                axis = self.names[number].index(self.left[number][0])

                def added(side):
                    one = lax.index_in_dim(old.reshape(inner), side, axis, keepdims=False)
                    two = lax.index_in_dim(new.reshape(inner), side, axis, keepdims=False)
                    total = (one.astype(F32) + two.astype(F32)).astype(BF)
                    return pin(total.reshape(-1, self.groups, self.blk, old.shape[-1]))

                halves.append((added(1), added(0)))
            self.line.mark(*[half for pair in halves for half in pair])
            for number, (theirs, mine) in enumerate(halves):
                self.send(number, theirs, mine)
            return
        sums = [one.astype(F32) + two.astype(F32) for one, two in zip(tied, came)]
        total = sums[0] if len(sums) == 1 else jnp.concatenate(sums, -1)
        if not self.heads:
            self.total = self.line.mark(pin(total.reshape(self.blk, -1)))
            return
        bit = self.heads.pop(0)
        total = total.astype(BF).reshape((-1, 2, self.blk, total.shape[-1]))
        theirs, mine = pin(total[:, 1]), pin(total[:, 0])
        self.line.mark(theirs, mine)
        self.mine = [mine]
        self.came = [swap(theirs, "head", 1 << bit)]


def bit_reverse(number, width):
    turned = 0
    for bit in range(width):
        turned |= ((number >> bit) & 1) << (width - 1 - bit)
    return turned


def reorder_blocks(array_in, table):
    count = table.shape[0]
    rows, features = array_in.shape
    blk = features // count
    if blk % 128:
        return jnp.take(array_in.reshape(rows, count, blk), table, axis=1).reshape(rows, features)

    def body(table_ref, in_ref, out_ref):
        for p in range(count):
            start = pl.multiple_of(table_ref[p] * blk, blk)
            out_ref[:, p * blk : (p + 1) * blk] = in_ref[:, pl.ds(start, blk)]

    return pl.pallas_call(
        body,
        out_shape=jax.ShapeDtypeStruct(array_in.shape, array_in.dtype),
        grid_spec=pltpu.PrefetchScalarGridSpec(
            num_scalar_prefetch=1,
            grid=(1,),
            in_specs=[pl.BlockSpec((rows, features), lambda p, table_ref: (0, 0))],
            out_specs=pl.BlockSpec((rows, features), lambda p, table_ref: (0, 0)),
        ),
        name="reorder",
    )(table, array_in)


def piece_specs(pieces, cols, col_block, step=None):
    count, _, blk, _ = pieces[0].shape
    return [
        pl.BlockSpec((count, 1, blk, cols), lambda j, *c: (0, j, 0, col_block + (c[0] if c else 0)))
        for _ in pieces
    ]


def flat_piece(ref):
    count, _, blk, cols = ref.shape
    return ref[...].reshape(count * blk, cols)


def over_features(x, piece_refs):
    depth = x.shape[1] // len(piece_refs)
    total = None
    for number, ref in enumerate(piece_refs):
        term = dot(x[:, number * depth : (number + 1) * depth], flat_piece(ref), 1, 0)
        total = term if total is None else total + term
    return total


def project(x, pieces, first_col, cols, tile, affine, out_dtype, name):
    rows, features = x.shape
    groups = pieces[0].shape[1]
    per = cols // tile

    def body(x_ref, *refs):
        *piece_refs, affine_ref, out_ref = refs
        acc = over_features(x_ref[...], piece_refs)
        out_ref[...] = ((acc + affine_ref[0:1]) * affine_ref[1:2]).astype(out_ref.dtype)

    return pl.pallas_call(
        body,
        grid=(groups, per),
        in_specs=[whole((rows, features))]
        + piece_specs(pieces, tile, first_col // tile)
        + [pl.BlockSpec((2, tile), lambda j, c: (0, j * per + c))],
        out_specs=pl.BlockSpec((rows, tile), lambda j, c: (0, j * per + c)),
        out_shape=jax.ShapeDtypeStruct((rows, groups * cols), out_dtype),
        compiler_params=params(),
        name=name,
    )(x, *pieces, affine)


def project_plain(x, pieces, first_col, cols, name):
    groups = pieces[0].shape[1]
    affine = jnp.stack([jnp.zeros((groups * cols,), F32), jnp.ones((groups * cols,), F32)])
    return project(x, pieces, first_col, cols, cols, affine, BF, name)


def add_rows(acc_ref, left, piece_refs):
    depth = acc_ref.shape[1] // len(piece_refs)
    for number, ref in enumerate(piece_refs):
        where = slice(number * depth, (number + 1) * depth)
        acc_ref[:, where] += dot(left, flat_piece(ref), 1, 1)


def row_mean(v):
    return jnp.mean(v, -1, keepdims=True)


def column_sum(v):
    return jnp.sum(v, 0, keepdims=True)


def normalize(v):
    centered = v - row_mean(v)
    spread = lax.rsqrt(row_mean(centered * centered) + EPSILON)
    return centered * spread, spread


def normalize_back(upstream, unit, spread, gain):
    a = upstream * gain
    return spread * (a - row_mean(a) - unit * row_mean(a * unit))


def close_sublayer(left, pieces, first_col, cols, residual, vectors, name):
    rows, features = residual.shape
    groups = pieces[0].shape[1]
    count = len(pieces)

    def body(left_ref, *refs):
        piece_refs = refs[:count]
        residual_ref, vectors_ref, normed_ref, low_ref, unit_ref, spread_ref, acc_ref = refs[count:]
        step = pl.program_id(0)

        @pl.when(step == 0)
        def _():
            acc_ref[...] = jnp.zeros_like(acc_ref)

        add_rows(acc_ref, left_ref[...], piece_refs)

        @pl.when(step == groups - 1)
        def _():
            v = residual_ref[...].astype(F32) + (acc_ref[...] + vectors_ref[2:3])
            unit, spread = normalize(v)
            normed = unit * vectors_ref[0:1] + vectors_ref[1:2]
            normed_ref[...] = normed
            low_ref[...] = normed.astype(BF)
            unit_ref[...] = unit
            spread_ref[...] = spread

    return pl.pallas_call(
        body,
        grid=(groups,),
        in_specs=[pl.BlockSpec((rows, cols), lambda j: (0, j))]
        + piece_specs(pieces, cols, first_col // cols)
        + [whole((rows, features)), whole((3, features))],
        out_specs=[whole((rows, features))] * 3 + [whole((rows, 1))],
        out_shape=[
            jax.ShapeDtypeStruct((rows, features), F32),
            jax.ShapeDtypeStruct((rows, features), BF),
            jax.ShapeDtypeStruct((rows, features), F32),
            jax.ShapeDtypeStruct((rows, 1), F32),
        ],
        scratch_shapes=[pltpu.VMEM((rows, features), F32)],
        compiler_params=params(),
        name=name,
    )(left, *pieces, residual, vectors)


def natural_from_exchange(order_ref, first, from_ref, to_ref, blk):
    if blk % 128:
        to_ref[...] = from_ref[...]
        return
    for p in range(from_ref.shape[1] // blk):
        start = pl.multiple_of(order_ref[first + p] * blk, blk)
        to_ref[:, pl.ds(start, blk)] = from_ref[:, p * blk : (p + 1) * blk]


def exchange_from_natural(order_ref, first, from_ref, to_ref, blk):
    if blk % 128:
        to_ref[...] = from_ref[...]
        return
    for p in range(from_ref.shape[1] // blk):
        start = pl.multiple_of(order_ref[first + p] * blk, blk)
        to_ref[:, p * blk : (p + 1) * blk] = from_ref[:, pl.ds(start, blk)]


def flat_natural(ref):
    count, _, blk, cols = ref.shape
    return ref[...].reshape(count * blk, cols)


def feed_forward(order, low, normed, weights, up_bias, vectors, grad_out):
    rows, features = normed.shape
    batches, groups, blk, both = weights.shape
    cols = both // 2

    def body(
        order_ref, low_ref, normed_ref, up_ref, down_ref, bias_ref, vectors_ref, grad_ref,
        active_ref, slope_ref, out_ref, third_ref, third_low_ref, sums_ref,
        natural_ref, acc_ref, turned_ref,
    ):
        step = pl.program_id(0)

        @pl.when(step == 0)
        def _():
            natural_from_exchange(order_ref, groups, low_ref, natural_ref, blk)
            acc_ref[...] = jnp.zeros_like(acc_ref)

        upper = dot(natural_ref[...], flat_natural(up_ref), 1, 0) + bias_ref[...]
        cdf = 0.5 * (1.0 + lax.erf(upper * 0.7071067811865476))
        active = (upper * cdf).astype(BF)
        slope = cdf + upper * jnp.exp(-0.5 * upper * upper) * 0.3989422804014327
        active_ref[...] = active
        slope_ref[...] = slope.astype(BF)
        acc_ref[...] += dot(active, flat_natural(down_ref), 1, 1)

        @pl.when(step == groups - 1)
        def _():
            exchange_from_natural(order_ref, groups, acc_ref, turned_ref, blk)
            v = normed_ref[...] + (turned_ref[...] + vectors_ref[2:3])
            unit, spread = normalize(v)
            gain = vectors_ref[0:1]
            out_ref[...] = (unit * gain + vectors_ref[1:2]).astype(BF)
            upstream = grad_ref[...]
            third = normalize_back(upstream, unit, spread, gain)
            third_ref[...] = third
            third_low_ref[...] = third.astype(BF)
            sums_ref[0:1] = column_sum(upstream * unit)
            sums_ref[1:2] = column_sum(upstream)
            sums_ref[2:3] = column_sum(third)

    return pl.pallas_call(
        body,
        grid_spec=pltpu.PrefetchScalarGridSpec(
            num_scalar_prefetch=1,
            grid=(groups,),
            in_specs=[
                whole((rows, features)),
                whole((rows, features)),
                pl.BlockSpec((batches, 1, blk, cols), lambda j, order: (0, j, 0, 0)),
                pl.BlockSpec((batches, 1, blk, cols), lambda j, order: (0, j, 0, 1)),
                pl.BlockSpec((1, cols), lambda j, order: (0, j)),
                whole((3, features)),
                whole((rows, features)),
            ],
            out_specs=[
                pl.BlockSpec((rows, cols), lambda j, order: (0, j)),
                pl.BlockSpec((rows, cols), lambda j, order: (0, j)),
                whole((rows, features)),
                whole((rows, features)),
                whole((rows, features)),
                whole((3, features)),
            ],
            scratch_shapes=[
                pltpu.VMEM((rows, features), BF),
                pltpu.VMEM((rows, features), F32),
                pltpu.VMEM((rows, features), F32),
            ],
        ),
        out_shape=[
            jax.ShapeDtypeStruct((rows, groups * cols), BF),
            jax.ShapeDtypeStruct((rows, groups * cols), BF),
            jax.ShapeDtypeStruct((rows, features), BF),
            jax.ShapeDtypeStruct((rows, features), F32),
            jax.ShapeDtypeStruct((rows, features), BF),
            jax.ShapeDtypeStruct((3, features), F32),
        ],
        compiler_params=params(),
        name="feed_forward",
    )(order, low, normed, weights, weights, up_bias, vectors, grad_out)


def norm_back_outputs(upstream, unit, spread, gain, grad_ref, grad_low_ref, sums_ref):
    grad = normalize_back(upstream, unit, spread, gain)
    grad_ref[...] = grad
    grad_low_ref[...] = grad.astype(BF)
    sums_ref[0:1] = column_sum(upstream * unit)
    sums_ref[1:2] = column_sum(upstream)
    sums_ref[2:3] = column_sum(grad)


def feed_forward_back(order, third_low, third, slope, weights, unit, spread, gain):
    rows, features = third.shape
    batches, groups, blk, both = weights.shape
    cols = both // 2

    def body(
        order_ref, third_low_ref, third_ref, slope_ref, up_ref, down_ref, unit_ref, spread_ref, gain_ref,
        upper_ref, bias_ref, grad_ref, grad_low_ref, sums_ref,
        natural_ref, acc_ref, turned_ref,
    ):
        step = pl.program_id(0)

        @pl.when(step == 0)
        def _():
            natural_from_exchange(order_ref, groups, third_low_ref, natural_ref, blk)
            acc_ref[...] = jnp.zeros_like(acc_ref)

        grad_upper = dot(natural_ref[...], flat_natural(down_ref), 1, 0)
        grad_upper = grad_upper * slope_ref[...].astype(F32)
        bias_ref[...] = column_sum(grad_upper)
        low = grad_upper.astype(BF)
        upper_ref[...] = low
        acc_ref[...] += dot(low, flat_natural(up_ref), 1, 1)

        @pl.when(step == groups - 1)
        def _():
            exchange_from_natural(order_ref, groups, acc_ref, turned_ref, blk)
            norm_back_outputs(
                turned_ref[...] + third_ref[...],
                unit_ref[...],
                spread_ref[...],
                gain_ref[...],
                grad_ref,
                grad_low_ref,
                sums_ref,
            )

    return pl.pallas_call(
        body,
        grid_spec=pltpu.PrefetchScalarGridSpec(
            num_scalar_prefetch=1,
            grid=(groups,),
            in_specs=[
                whole((rows, features)),
                whole((rows, features)),
                pl.BlockSpec((rows, cols), lambda j, order: (0, j)),
                pl.BlockSpec((batches, 1, blk, cols), lambda j, order: (0, j, 0, 0)),
                pl.BlockSpec((batches, 1, blk, cols), lambda j, order: (0, j, 0, 1)),
                whole((rows, features)),
                whole((rows, 1)),
                whole((1, features)),
            ],
            out_specs=[
                pl.BlockSpec((rows, cols), lambda j, order: (0, j)),
                pl.BlockSpec((1, cols), lambda j, order: (0, j)),
                whole((rows, features)),
                whole((rows, features)),
                whole((3, features)),
            ],
            scratch_shapes=[
                pltpu.VMEM((rows, features), BF),
                pltpu.VMEM((rows, features), F32),
                pltpu.VMEM((rows, features), F32),
            ],
        ),
        out_shape=[
            jax.ShapeDtypeStruct((rows, groups * cols), BF),
            jax.ShapeDtypeStruct((1, groups * cols), F32),
            jax.ShapeDtypeStruct((rows, features), F32),
            jax.ShapeDtypeStruct((rows, features), BF),
            jax.ShapeDtypeStruct((3, features), F32),
        ],
        compiler_params=params(),
        name="feed_forward_back",
    )(order, third_low, third, slope, weights, weights, unit, spread, gain)


def cross_query_back(grad_query, pieces, first_col, cols, second, unit, spread, gain):
    rows, features = second.shape
    groups = pieces[0].shape[1]
    count = len(pieces)

    def body(left_ref, *refs):
        piece_refs = refs[:count]
        second_ref, unit_ref, spread_ref, gain_ref, grad_ref, grad_low_ref, sums_ref, acc_ref = refs[
            count:
        ]
        step = pl.program_id(0)

        @pl.when(step == 0)
        def _():
            acc_ref[...] = second_ref[...]

        add_rows(acc_ref, left_ref[...], piece_refs)

        @pl.when(step == groups - 1)
        def _():
            norm_back_outputs(
                acc_ref[...],
                unit_ref[...],
                spread_ref[...],
                gain_ref[...],
                grad_ref,
                grad_low_ref,
                sums_ref,
            )

    return pl.pallas_call(
        body,
        grid=(groups,),
        in_specs=[pl.BlockSpec((rows, cols), lambda j: (0, j))]
        + piece_specs(pieces, cols, first_col // cols)
        + [whole((rows, features)), whole((rows, features)), whole((rows, 1)), whole((1, features))],
        out_specs=[whole((rows, features)), whole((rows, features)), whole((3, features))],
        out_shape=[
            jax.ShapeDtypeStruct((rows, features), F32),
            jax.ShapeDtypeStruct((rows, features), BF),
            jax.ShapeDtypeStruct((3, features), F32),
        ],
        scratch_shapes=[pltpu.VMEM((rows, features), F32)],
        compiler_params=params(),
        name="cross_query_back",
    )(grad_query, *pieces, second, unit, spread, gain)


def rows_back(left, pieces, first_col, cols, name):
    rows = left.shape[0]
    count = len(pieces)
    groups = pieces[0].shape[1]
    features = count * pieces[0].shape[0] * pieces[0].shape[2]

    def body(left_ref, *refs):
        piece_refs = refs[:count]
        out_ref, acc_ref = refs[count:]
        step = pl.program_id(0)

        @pl.when(step == 0)
        def _():
            acc_ref[...] = jnp.zeros_like(acc_ref)

        add_rows(acc_ref, left_ref[...], piece_refs)

        @pl.when(step == groups - 1)
        def _():
            out_ref[...] = acc_ref[...].astype(BF)

    return pl.pallas_call(
        body,
        grid=(groups,),
        in_specs=[pl.BlockSpec((rows, cols), lambda j: (0, j))]
        + piece_specs(pieces, cols, first_col // cols),
        out_specs=whole((rows, features)),
        out_shape=jax.ShapeDtypeStruct((rows, features), BF),
        scratch_shapes=[pltpu.VMEM((rows, features), F32)],
        compiler_params=params(),
        name=name,
    )(left, *pieces)


def input_back(grad_query, grad_kv, grad_rel, pieces, others, first):
    rows, features = first.shape
    long_rows = grad_kv.shape[0]
    halo = long_rows - rows
    groups = pieces[0].shape[1]
    count = len(pieces)
    width = grad_query.shape[1] // groups
    rel_width = grad_rel.shape[1] // groups

    def body(query_ref, kv_ref, rel_ref, *refs):
        parts = [refs[count * k : count * (k + 1)] for k in range(4)]
        first_ref, halo_ref, own_ref, acc_ref = refs[4 * count :]
        step = pl.program_id(0)

        @pl.when(step == 0)
        def _():
            acc_ref[0:halo] = jnp.zeros((halo, features), F32)
            acc_ref[halo:] = first_ref[...]

        own_acc = acc_ref.at[halo:]
        add_rows(own_acc, query_ref[...], parts[0])
        add_rows(acc_ref, kv_ref[:, 0:width], parts[1])
        add_rows(acc_ref, kv_ref[:, width : 2 * width], parts[2])
        add_rows(own_acc, rel_ref[...], parts[3])

        @pl.when(step == groups - 1)
        def _():
            halo_ref[...] = acc_ref[0:halo].astype(BF)
            own_ref[...] = acc_ref[halo:]

    return pl.pallas_call(
        body,
        grid=(groups,),
        in_specs=[
            pl.BlockSpec((rows, width), lambda j: (0, j)),
            pl.BlockSpec((long_rows, 2 * width), lambda j: (0, j)),
            pl.BlockSpec((rows, rel_width), lambda j: (0, j)),
        ]
        + piece_specs(pieces, width, 0)
        + piece_specs(pieces, width, 1)
        + piece_specs(others, width, 0)
        + piece_specs(others, rel_width, width // rel_width)
        + [whole((rows, features))],
        out_specs=[whole((halo, features)), whole((rows, features))],
        out_shape=[
            jax.ShapeDtypeStruct((halo, features), BF),
            jax.ShapeDtypeStruct((rows, features), F32),
        ],
        scratch_shapes=[pltpu.VMEM((long_rows, features), F32)],
        compiler_params=params(),
        name="input_back",
    )(grad_query, grad_kv, grad_rel, *pieces, *pieces, *others, *others, first)


def weight_products(entries, half, extra, parts, pieces, groups, name):
    features = entries[0][0].shape[1]
    depth = features // 2
    blk = depth // pieces
    widths = [right.shape[1] // groups for _, right in entries]
    total = sum(widths)
    count = len(entries)
    outs = []
    if parts is None:
        outs.append((0, total, list(range(pieces))))
    else:
        at = 0
        for width, bit in parts:
            for side in (1, 0):
                outs.append((at, width, [p for p in range(pieces) if (p >> bit & 1) == side]))
            at += width

    def body(*refs):
        lefts, rights = refs[:count], refs[count : 2 * count]
        out_refs = refs[len(refs) - len(outs) :]
        at = 0
        for left_ref, right_ref, width in zip(lefts, rights, widths):
            term = dot(left_ref[...], right_ref[...], 0, 0).reshape(pieces, blk, width)
            if extra is not None:
                term = term + refs[2 * count][:, 0, :, at : at + width].astype(F32)
            term = term.astype(BF)
            for out_ref, (first, size, members) in zip(out_refs, outs):
                low, high = max(at, first), min(at + width, first + size)
                if low >= high:
                    continue
                for place, piece in enumerate(members):
                    out_ref[place, 0, :, low - first : high - first] = term[
                        piece, :, low - at : high - at
                    ]
            at += width

    def block(number, width):
        return pl.BlockSpec((number, 1, blk, width), lambda j: (0, j, 0, 0))

    in_specs = [pl.BlockSpec((left.shape[0], depth), lambda j: (0, half)) for left, _ in entries]
    in_specs += [
        pl.BlockSpec((right.shape[0], width), lambda j: (0, j))
        for (_, right), width in zip(entries, widths)
    ]
    operands = [left for left, _ in entries] + [right for _, right in entries]
    if extra is not None:
        in_specs.append(block(pieces, total))
        operands.append(extra)
    return pl.pallas_call(
        body,
        grid=(groups,),
        in_specs=in_specs,
        out_specs=[block(len(members), width) for _, width, members in outs],
        out_shape=[
            jax.ShapeDtypeStruct((len(members), groups, blk, width), BF)
            for _, width, members in outs
        ],
        compiler_params=params(),
        name=name,
    )(*operands)


def half_masks(rows):
    lane = lax.broadcasted_iota(jnp.int32, (rows, 128), 1)
    return [
        jnp.where((lane >= 64 * half) & (lane < 64 * half + 64), 1.0, 0.0).astype(F32)
        for half in range(2)
    ]


def skew(array_in, share):
    rows, width = array_in.shape
    parts = [
        pltpu.roll(array_in[n * share : (n + 1) * share], width - share + 1, 1, stride=1, stride_axis=0)
        for n in range(rows // share)
    ]
    return jnp.concatenate(parts, 0)


def self_attention(qk, values, relpos, mask, turned, share):
    rows, window = 3 * share, 3 * share
    groups = values.shape[1] // 256
    long_rows = qk.shape[0]
    halo = long_rows - rows

    def body(q_ref, k_ref, v_ref, rel_ref, mask_ref, turned_ref, ctx_ref, probs_ref, own_ref):
        halves = half_masks(rows)
        lane = lax.broadcasted_iota(jnp.int32, (rows, 128), 1)
        rel = rel_ref[...]
        high = rel.astype(BF)
        split = jnp.concatenate([high, (rel - high.astype(F32)).astype(BF)], 1)
        row_id = lax.broadcasted_iota(jnp.int32, (256, window), 0) & 127
        own_all = jnp.zeros((rows, 128), F32)
        for pair in range(2):
            cols = slice(128 * pair, 128 * pair + 128)
            q = q_ref[halo:, cols]
            k, v = k_ref[0:window, cols], v_ref[0:window, cols]
            own_k = k_ref[halo:, cols].astype(F32)
            own_v = v_ref[halo:, cols].astype(F32)
            product = q.astype(F32) * own_k
            mixed = jnp.zeros((rows, 128), F32)
            for half in range(2):
                head = 2 * pair + half
                scores = dot(q * halves[half].astype(BF), k, 1, 1)
                table = jnp.where(row_id == turned_ref[...] + 32 * head, 1.0, 0.0).astype(BF)
                scores = scores + skew(dot(split, table, 1, 0), share) + mask_ref[...]
                own = jnp.sum(
                    product * halves[half] + jnp.where(lane == 32 * head, rel, 0.0), -1, keepdims=True
                )
                track = lax.broadcasted_iota(jnp.int32, (rows, 1), 0) >= share
                own = jnp.where(track, own, MASKED)
                top = jnp.maximum(jnp.max(scores, -1, keepdims=True), own)
                raised = jnp.exp(scores - top)
                own_raised = jnp.exp(own - top)
                scale = 1.0 / (jnp.sum(raised, -1, keepdims=True) + own_raised)
                probs = (raised * scale).astype(BF)
                own_probs = (own_raised * scale).astype(BF).astype(F32)
                probs_ref[head] = probs
                own_all = jnp.where(lane == head, own_probs, own_all)
                mixed = mixed + (dot(probs, v, 1, 0) + own_probs * own_v) * halves[half]
            ctx_ref[:, cols] = mixed.astype(BF)
        own_ref[...] = own_all

    return pl.pallas_call(
        body,
        grid=(groups,),
        in_specs=[
            pl.BlockSpec((long_rows, 256), lambda j: (0, 2 * j)),
            pl.BlockSpec((long_rows, 256), lambda j: (0, 2 * j + 1)),
            pl.BlockSpec((long_rows, 256), lambda j: (0, j)),
            pl.BlockSpec((rows, 128), lambda j: (0, j)),
            whole((rows, window)),
            whole((1, window)),
        ],
        out_specs=[
            pl.BlockSpec((rows, 256), lambda j: (0, j)),
            pl.BlockSpec((4, rows, window), lambda j: (j, 0, 0)),
            pl.BlockSpec((rows, 128), lambda j: (0, j)),
        ],
        out_shape=[
            jax.ShapeDtypeStruct((rows, groups * 256), BF),
            jax.ShapeDtypeStruct((4 * groups, rows, window), BF),
            jax.ShapeDtypeStruct((rows, groups * 128), F32),
        ],
        compiler_params=params(),
        name="self_attention",
    )(qk, qk, values, relpos, mask, turned)


def self_attention_back(qk, values, probs, own_probs, grad_ctx, straight, share):
    rows, window = 3 * share, 3 * share
    groups = values.shape[1] // 256
    long_rows = qk.shape[0]
    halo = long_rows - rows

    def body(
        q_ref, k_ref, v_ref, probs_ref, own_ref, grad_ref, straight_ref,
        gq_ref, gkv_ref, grel_ref, sums_ref, rel_sums_ref,
    ):
        halves = half_masks(rows)
        lane = lax.broadcasted_iota(jnp.int32, (rows, 128), 1)
        turn = jnp.where(
            lax.broadcasted_iota(jnp.int32, (window, window), 0)
            + lax.broadcasted_iota(jnp.int32, (window, window), 1)
            == window - 1,
            1.0,
            0.0,
        ).astype(BF)
        column = lax.broadcasted_iota(jnp.int32, (window, 128), 1)
        grel = jnp.zeros((rows, 128), F32)
        for pair in range(2):
            cols = slice(128 * pair, 128 * pair + 128)
            q = q_ref[halo:, cols]
            k, v = k_ref[0:window, cols], v_ref[0:window, cols]
            own_k = k_ref[halo:, cols].astype(F32)
            own_v = v_ref[halo:, cols].astype(F32)
            grad = grad_ref[:, cols]
            grad_wide = grad.astype(F32)
            own_product = grad_wide * own_v
            gq = jnp.zeros((rows, 128), F32)
            own_spread = jnp.zeros((rows, 128), F32)
            own_weight = jnp.zeros((rows, 128), F32)
            score_parts, prob_parts, q_parts, g_parts = [], [], [], []
            for half in range(2):
                head = 2 * pair + half
                low_half = halves[half].astype(BF)
                p = probs_ref[head]
                p_wide = p.astype(F32)
                grad_half = grad * low_half
                grad_probs = dot(grad_half, v, 1, 1)
                own_p = jnp.sum(jnp.where(lane == head, own_ref[...], 0.0), -1, keepdims=True)
                own_grad = jnp.sum(own_product * halves[half], -1, keepdims=True)
                row_dot = jnp.sum(p_wide * grad_probs, -1, keepdims=True) + own_p * own_grad
                grad_scores = (p_wide * (grad_probs - row_dot)).astype(BF)
                grad_own = (own_p * (own_grad - row_dot)).astype(BF).astype(F32)
                gq = gq + (dot(grad_scores, k, 1, 0) + grad_own * own_k) * halves[half]
                own_spread = own_spread + grad_own * halves[half]
                own_weight = own_weight + own_p * halves[half]
                score_parts.append(grad_scores)
                prob_parts.append(p)
                q_parts.append(q * low_half)
                g_parts.append(grad_half)
                turned = skew(dot(grad_scores, turn, 1, 0), share).astype(BF)
                table = jnp.where(column == straight_ref[...] + 32 * head, 1.0, 0.0).astype(BF)
                grel = grel + dot(turned, table, 1, 0) + jnp.where(lane == 32 * head, grad_own, 0.0)
            gk = dot(
                jnp.concatenate(q_parts, 0), jnp.concatenate(score_parts, 0), 0, 0
            ).T
            gv = dot(
                jnp.concatenate(g_parts, 0), jnp.concatenate(prob_parts, 0), 0, 0
            ).T
            gq = gq * 0.125
            gq_ref[:, cols] = gq.astype(BF)
            own_gk = own_spread * q.astype(F32)
            own_gv = own_weight * grad_wide
            vcols = slice(256 + 128 * pair, 256 + 128 * pair + 128)
            gkv_ref[0:window, cols] = gk.astype(BF)
            gkv_ref[0:window, vcols] = gv.astype(BF)
            gkv_ref[window:, cols] = own_gk[share:].astype(BF)
            gkv_ref[window:, vcols] = own_gv[share:].astype(BF)
            sums_ref[0:1, cols] = column_sum(gq)
            sums_ref[1:2, cols] = column_sum(gv) + column_sum(own_gv[share:])
        grel_ref[...] = grel.astype(BF)
        rel_sums_ref[...] = column_sum(grel)

    return pl.pallas_call(
        body,
        grid=(groups,),
        in_specs=[
            pl.BlockSpec((long_rows, 256), lambda j: (0, 2 * j)),
            pl.BlockSpec((long_rows, 256), lambda j: (0, 2 * j + 1)),
            pl.BlockSpec((long_rows, 256), lambda j: (0, j)),
            pl.BlockSpec((4, rows, window), lambda j: (j, 0, 0)),
            pl.BlockSpec((rows, 128), lambda j: (0, j)),
            pl.BlockSpec((rows, 256), lambda j: (0, j)),
            whole((window, 1)),
        ],
        out_specs=[
            pl.BlockSpec((rows, 256), lambda j: (0, j)),
            pl.BlockSpec((long_rows, 512), lambda j: (0, j)),
            pl.BlockSpec((rows, 128), lambda j: (0, j)),
            pl.BlockSpec((2, 256), lambda j: (0, j)),
            pl.BlockSpec((1, 128), lambda j: (0, j)),
        ],
        out_shape=[
            jax.ShapeDtypeStruct((rows, groups * 256), BF),
            jax.ShapeDtypeStruct((long_rows, groups * 512), BF),
            jax.ShapeDtypeStruct((rows, groups * 128), BF),
            jax.ShapeDtypeStruct((2, groups * 256), F32),
            jax.ShapeDtypeStruct((1, groups * 128), F32),
        ],
        compiler_params=params(),
        name="self_attention_back",
    )(qk, qk, values, probs, own_probs, grad_ctx, straight)


def cross_attention(queries, kv):
    rows, places = queries.shape[0], kv.shape[0]
    groups = queries.shape[1] // 256

    def body(q_ref, k_ref, v_ref, ctx_ref, probs_ref):
        halves = half_masks(rows)
        for pair in range(2):
            cols = slice(128 * pair, 128 * pair + 128)
            q, k, v = q_ref[:, cols], k_ref[:, cols], v_ref[:, cols]
            mixed = jnp.zeros((rows, 128), F32)
            for half in range(2):
                scores = dot(q * halves[half].astype(BF), k, 1, 1)
                raised = jnp.exp(scores - jnp.max(scores, -1, keepdims=True))
                probs = (raised * (1.0 / jnp.sum(raised, -1, keepdims=True))).astype(BF)
                probs_ref[2 * pair + half] = probs
                mixed = mixed + dot(probs, v, 1, 0) * halves[half]
            ctx_ref[:, cols] = mixed.astype(BF)

    return pl.pallas_call(
        body,
        grid=(groups,),
        in_specs=[
            pl.BlockSpec((rows, 256), lambda j: (0, j)),
            pl.BlockSpec((places, 256), lambda j: (0, 2 * j)),
            pl.BlockSpec((places, 256), lambda j: (0, 2 * j + 1)),
        ],
        out_specs=[
            pl.BlockSpec((rows, 256), lambda j: (0, j)),
            pl.BlockSpec((4, rows, places), lambda j: (j, 0, 0)),
        ],
        out_shape=[
            jax.ShapeDtypeStruct((rows, groups * 256), BF),
            jax.ShapeDtypeStruct((4 * groups, rows, places), BF),
        ],
        compiler_params=params(),
        name="cross_attention",
    )(queries, kv, kv)


def cross_attention_back(queries, kv, probs, grad_ctx):
    rows, places = queries.shape[0], kv.shape[0]
    groups = queries.shape[1] // 256

    def body(q_ref, k_ref, v_ref, probs_ref, grad_ref, gq_ref, gkv_ref, sums_ref):
        halves = half_masks(rows)
        for pair in range(2):
            cols = slice(128 * pair, 128 * pair + 128)
            q, k, v, grad = q_ref[:, cols], k_ref[:, cols], v_ref[:, cols], grad_ref[:, cols]
            gq = jnp.zeros((rows, 128), F32)
            score_parts, prob_parts, q_parts, g_parts = [], [], [], []
            for half in range(2):
                low_half = halves[half].astype(BF)
                p = probs_ref[2 * pair + half]
                p_wide = p.astype(F32)
                grad_half = grad * low_half
                grad_probs = dot(grad_half, v, 1, 1)
                row_dot = jnp.sum(p_wide * grad_probs, -1, keepdims=True)
                grad_scores = (p_wide * (grad_probs - row_dot)).astype(BF)
                gq = gq + dot(grad_scores, k, 1, 0) * halves[half]
                score_parts.append(grad_scores)
                prob_parts.append(p)
                q_parts.append(q * low_half)
                g_parts.append(grad_half)
            gk = dot(
                jnp.concatenate(q_parts, 0), jnp.concatenate(score_parts, 0), 0, 0
            ).T
            gv = dot(
                jnp.concatenate(g_parts, 0), jnp.concatenate(prob_parts, 0), 0, 0
            ).T
            gq = gq * 0.125
            gq_ref[:, cols] = gq.astype(BF)
            vcols = slice(256 + 128 * pair, 256 + 128 * pair + 128)
            gkv_ref[:, cols] = gk.astype(BF)
            gkv_ref[:, vcols] = gv.astype(BF)
            sums_ref[0:1, cols] = column_sum(gq)
            sums_ref[1:2, cols] = column_sum(gv)

    return pl.pallas_call(
        body,
        grid=(groups,),
        in_specs=[
            pl.BlockSpec((rows, 256), lambda j: (0, j)),
            pl.BlockSpec((places, 256), lambda j: (0, 2 * j)),
            pl.BlockSpec((places, 256), lambda j: (0, 2 * j + 1)),
            pl.BlockSpec((4, rows, places), lambda j: (j, 0, 0)),
            pl.BlockSpec((rows, 256), lambda j: (0, j)),
        ],
        out_specs=[
            pl.BlockSpec((rows, 256), lambda j: (0, j)),
            pl.BlockSpec((places, 512), lambda j: (0, j)),
            pl.BlockSpec((2, 256), lambda j: (0, j)),
        ],
        out_shape=[
            jax.ShapeDtypeStruct((rows, groups * 256), BF),
            jax.ShapeDtypeStruct((places, groups * 512), BF),
            jax.ShapeDtypeStruct((2, groups * 256), F32),
        ],
        compiler_params=params(),
        name="cross_attention_back",
    )(queries, kv, kv, probs, grad_ctx)


def per_device(
    hidden,
    memory,
    grad_out,
    lengths,
    key_mask,
    buckets,
    self_weight,
    relpos_weight,
    selfout_weight,
    crossq_weight,
    crosskv_weight,
    crossout_weight,
    up_weight,
    down_weight,
    self_bias,
    relpos_bias,
    cross_bias,
    up_bias,
    norm_gain,
    norm_bias,
    out_bias,
):
    batches, groups = lax.axis_size("batch"), lax.axis_size("head")
    b, z = lax.axis_index("batch"), lax.axis_index("head")
    nb = bits_of("batch")
    share, features = hidden.shape[1], hidden.shape[3]
    length = share * groups
    rows, window = 3 * share, 3 * share
    assert share == 128 and hidden.shape[0] == 1 and WIDEST_DOC <= 2 * share
    assert batches == 1 << nb and features % batches == 0 and groups == 4
    near, far = list(range(1, nb)), list(reversed(range(1, nb)))

    turned_ids = jnp.array([bit_reverse(p, nb) for p in range(batches)], jnp.int32)
    to_exchange = b ^ turned_ids
    natural = lax.iota(jnp.int32, batches) ^ b
    to_natural = jnp.zeros_like(natural)
    for bit in range(nb):
        to_natural = to_natural | (((natural >> bit) & 1) << (nb - 1 - bit))
    group_order = z ^ lax.iota(jnp.int32, groups)

    def small_features(stack):
        count = stack.shape[0]
        blocks = stack.reshape(count, batches, features // batches)
        return jnp.take(blocks, to_exchange, axis=1).reshape(count, features)

    blk = self_weight.shape[0]
    line = Line()
    self_shard = jnp.concatenate([self_weight.reshape(blk, -1), relpos_weight], 1).astype(BF)
    gather_self = Gather(line, line.mark(pin(self_shard)))
    gather_self.send("head", 1)

    columns = jnp.concatenate(
        [
            self_bias[0].reshape(groups, -1),
            self_bias[1].reshape(groups, -1),
            cross_bias[0].reshape(groups, -1),
            cross_bias[1].reshape(groups, -1),
            relpos_bias.reshape(groups, -1),
            up_bias.reshape(groups, -1),
        ],
        1,
    )
    columns = jnp.take(columns, group_order, axis=0)
    query_bias, value_bias = columns[:, 0:256], columns[:, 256:512]
    cross_query_bias, cross_value_bias = columns[:, 512:768], columns[:, 768:1024]
    rel_row = columns[:, 1024:1152].reshape(1, -1)
    up_row = columns[:, 1152:].reshape(1, -1)

    memory_own = line.mark(reorder_blocks(line.tie(memory[0]), to_exchange))
    ffn_shard = jnp.concatenate([up_weight, down_weight], 1).astype(BF)
    own = jnp.transpose(line.tie(hidden[0]), (1, 0, 2)).reshape(rows, features)
    own = line.mark(reorder_blocks(own, to_exchange))
    upstream = lax.dynamic_slice_in_dim(line.tie(grad_out[0]), z * share, share, 0)
    upstream = jnp.transpose(upstream, (1, 0, 2)).reshape(rows, features)
    upstream = line.mark(reorder_blocks(upstream, to_exchange))
    chain = list(range(groups))

    vectors = small_features(jnp.concatenate([norm_gain, norm_bias, out_bias], 0))
    vectors = vectors.reshape(3, 3, features).transpose(1, 0, 2)
    none = jnp.zeros((groups, 256), F32)

    def affine(bias, scale):
        return jnp.stack([bias, jnp.full(bias.shape, scale, F32)])

    scales = jnp.concatenate([none + 0.125, none + 1.0], 1).reshape(-1)
    qk_affine = jnp.stack([jnp.concatenate([query_bias, none], 1).reshape(-1), scales])
    value_affine = affine(value_bias.reshape(-1), 1.0)
    rel_affine = affine(rel_row[0], 1.0)
    cross_query_affine = affine(cross_query_bias.reshape(-1), 0.125)
    cross_kv_affine = affine(jnp.concatenate([none, cross_value_bias], 1).reshape(-1), 1.0)

    places = lax.iota(jnp.int32, length)
    doc_ends = jnp.cumsum(lengths[0])
    segment = jnp.sum((places[:, None] >= doc_ends[None, :]).astype(jnp.int32), -1)
    lead = window - share
    padded_segment = jnp.concatenate([jnp.full((lead,), -1, jnp.int32), segment])
    padded_mask = jnp.concatenate([jnp.zeros((lead,), jnp.int32), key_mask[0]])
    key_segment = lax.dynamic_slice_in_dim(padded_segment, z * share, window)
    key_open = lax.dynamic_slice_in_dim(padded_mask, z * share, window)
    query_segment = lax.dynamic_slice_in_dim(segment, z * share, share)
    query_at = lax.iota(jnp.int32, share)[:, None] + lead
    key_at = lax.iota(jnp.int32, window)[None, :]
    joined = (query_segment[:, None] == key_segment[None, :]) & (
        (key_open[None, :] == 1) | (query_at == key_at)
    )
    allowed_main = joined & (key_at <= query_at)
    allowed_pred = joined & (key_at < query_at)
    mask = jnp.where(jnp.stack([allowed_main, allowed_pred, allowed_pred]), 0.0, MASKED)
    mask = mask.reshape(rows, window).astype(F32)
    straight = buckets[0:window]
    turned = straight[::-1]

    mask = line.mark(line.tie(mask))
    assert nb >= 2 and bits_of("head") == 2
    gather_cross = Gather(
        line,
        jnp.concatenate(
            [selfout_weight, crossq_weight, crosskv_weight.reshape(blk, -1), crossout_weight], 1
        ).astype(BF),
    )
    gather_self.take()
    gather_self.send("head", 0)
    gather_cross.send("head", 1)
    gather_self.take()
    parts_self = [gather_self.columns(0, 512), gather_self.columns(512, 384)]
    orders_self = [near, far]
    for part, part_order in zip(parts_self, orders_self):
        part.send("batch", part_order[0])
    main = line.tie(own[0:share])
    before_one = lax.ppermute(main, "head", [(i, i + 1) for i in chain[:-1]])
    before_two = lax.ppermute(main, "head", [(i, i + 2) for i in chain[:-2]])
    gather_cross.take()
    gather_cross.send("head", 0)
    for number in range(1, nb - 1):
        for part, part_order in zip(parts_self, orders_self):
            part.take()
            part.send("batch", part_order[number])
    extended = line.mark(jnp.concatenate([before_two, before_one, line.tie(own)], 0))
    gather_cross.take()
    parts_cross = [gather_cross.columns(0, 512), gather_cross.columns(512, 768)]
    orders_cross = [far, near]
    gather_ffn = Gather(line, ffn_shard)
    gather_ffn.send("head", 1)
    for part in parts_self:
        part.take()
        part.send("batch", 0)
    for part, part_order in zip(parts_cross, orders_cross):
        part.send("batch", part_order[0])
    gather_ffn.take()
    gather_ffn.send("head", 0)
    memory_came = swap(line.tie(memory_own), "head", 2)
    weights_qk, weights_vr = [part.close() for part in parts_self]

    order = jnp.concatenate([group_order, to_exchange]).astype(jnp.int32)
    values = line.mark(
        project(line.tie(extended), weights_vr, 0, 256, 256, value_affine, BF, "self_v")
    )
    relpos = line.mark(
        project(line.tie(own), weights_vr, 256, 128, 128, rel_affine, F32, "self_rel")
    )
    for number in range(1, nb - 1):
        for part, part_order in zip(parts_cross, orders_cross):
            part.take()
            part.send("batch", part_order[number])
    gather_ffn.take()
    weights_ffn = gather_ffn.buf.reshape((groups,) + ffn_shard.shape)
    weights_ffn = lax.all_gather(weights_ffn, "batch", axis=0)
    if blk % 128:
        weights_ffn = jnp.take(weights_ffn, to_exchange, axis=0)
    qk = line.mark(project(line.tie(extended), weights_qk, 0, 512, 256, qk_affine, BF, "self_qk"))
    memory_half = line.mark(jnp.concatenate([line.tie(memory_own), memory_came], 0))
    memory_came = swap(memory_half, "head", 1)
    context, self_probs, self_own = self_attention(
        line.tie(qk), values, relpos, mask, turned.reshape(1, -1), share
    )
    line.mark(context)
    for part in parts_cross:
        part.take()
        part.send("batch", 0)
    memory_all = line.mark(jnp.concatenate([line.tie(memory_half), memory_came], 0))
    weights_out, weights_kv = [part.close() for part in parts_cross]
    normed1, normed1_low, unit1, spread1 = close_sublayer(
        line.tie(context), weights_out, 0, 256, own, vectors[0], "self_out"
    )
    line.mark(normed1)
    cross_q = line.mark(
        project(
            line.tie(normed1_low), weights_out, 256, 256, 256, cross_query_affine, BF, "cross_q"
        )
    )
    cross_kv = line.mark(
        project(line.tie(memory_all), weights_kv, 0, 512, 256, cross_kv_affine, BF, "cross_kv")
    )
    cross_context, cross_probs = cross_attention(line.tie(cross_q), cross_kv)
    line.mark(cross_context)
    normed2, normed2_low, unit2, spread2 = close_sublayer(
        line.tie(cross_context), weights_kv, 512, 256, normed1, vectors[1], "cross_out"
    )
    line.mark(normed2)
    active, slope, out_low, third, third_low, sums_third = feed_forward(
        order, line.tie(normed2_low), normed2, weights_ffn, up_row, vectors[2], upstream
    )
    line.mark(third)

    def send(entries, name):
        left, right = entries[0]
        entries = [(line.tie(left), right)] + entries[1:]
        (sent,) = weight_products(entries, 1, None, None, batches // 2, groups, name + "_send")
        return swap(line.mark(sent), "batch", 1)

    def keep(entries, came, widths, name):
        left, right = entries[0]
        entries = [(line.tie(left), right)] + entries[1:]
        orders = (near, far)
        parts = [(width, nb - 1 - order[0]) for width, order in zip(widths, orders)]
        outs = weight_products(entries, 0, came, parts, batches // 2, groups, name + "_keep")
        line.mark(outs[0])
        return Scatter(line, [outs[0:2], outs[2:4]], orders)

    def natural_groups(block):
        return jnp.take(block.reshape(-1, groups, block.shape[1] // groups), group_order, axis=1)

    def pack_sums(earlier):
        feature_sums = jnp.concatenate([after(sums_first, earlier), sums_second, sums_third], 0)
        feature_sums = jnp.take(
            feature_sums.reshape(9, batches, features // batches), to_natural, axis=1
        )
        return jnp.concatenate(
            [
                natural_groups(self_sums).reshape(-1),
                natural_groups(rel_sums).reshape(-1),
                natural_groups(cross_sums).reshape(-1),
                natural_groups(up_sums).reshape(-1),
                feature_sums.reshape(-1),
            ]
        )

    down_entries = [(third_low, active)]
    down_came = send(down_entries, "down_grad")
    upper_low, up_sums, second, second_low, sums_second = feed_forward_back(
        order, line.tie(third_low), third, slope, weights_ffn, unit2, spread2, vectors[1][0:1]
    )
    line.mark(second)
    out_low = line.mark(reorder_blocks(line.tie(out_low), to_natural))
    out_low = out_low.reshape(3, share, features)
    layer_out = lax.all_gather(jnp.transpose(out_low, (1, 0, 2)), "head", axis=0, tiled=True)[None]
    scatter_down = keep(down_entries, down_came, (512, 512), "down_grad")
    up_entries = [(normed2_low, upper_low)]
    up_came = send(up_entries, "up_grad")
    grad_cross_ctx = project_plain(line.tie(second_low), weights_kv, 512, 256, "cross_ctx_back")
    line.mark(grad_cross_ctx)
    grad_cross_q, grad_cross_kv, cross_sums = cross_attention_back(
        cross_q, cross_kv, cross_probs, line.tie(grad_cross_ctx)
    )
    line.mark(grad_cross_q)
    scatter_up = keep(up_entries, up_came, (512, 512), "up_grad")
    scatter_down.step()
    cross_entries = [
        (normed1_low, grad_cross_q),
        (memory_all, grad_cross_kv),
        (second_low, cross_context),
    ]
    cross_came = send(cross_entries, "cross_grad")
    first, first_low, sums_first = cross_query_back(
        line.tie(grad_cross_q), weights_out, 256, 256, second, unit1, spread1, vectors[0][0:1]
    )
    line.mark(first)
    grad_context = project_plain(line.tie(first_low), weights_out, 0, 256, "self_ctx_back")
    line.mark(grad_context)
    grad_q, grad_kv, grad_rel, self_sums, rel_sums = self_attention_back(
        qk, values, self_probs, self_own, line.tie(grad_context), straight.reshape(-1, 1), share
    )
    line.mark(grad_q)
    scatter_cross = keep(cross_entries, cross_came, (512, 512), "cross_grad")
    layer_out = line.mark(line.tie(layer_out))
    scatter_up.step()
    scatter_down.step()
    self_entries = [(own, grad_q), (first_low, context), (extended, grad_kv), (own, grad_rel)]
    self_came = send(self_entries, "self_grad")
    halo_grad, own_grad = input_back(
        line.tie(grad_q), grad_kv, grad_rel, weights_qk, weights_vr, first
    )
    line.mark(own_grad)
    from_two = lax.ppermute(halo_grad[0:share], "head", [(i + 2, i) for i in chain[:-2]])
    from_one = lax.ppermute(halo_grad[share:], "head", [(i + 1, i) for i in chain[:-1]])
    memory_part = rows_back(line.tie(grad_cross_kv), weights_kv, 0, 512, "memory_back")
    span = memory.shape[1]
    memory_part = line.mark(memory_part).reshape(2, 2, span, features)
    memory_came = swap(memory_part[1], "head", 1)
    scatter_self = keep(self_entries, self_came, (512, 640), "self_grad")
    scatter_cross.step()
    scatter_up.step()
    scatter_down.step()
    packed = pack_sums(line.last[0])
    packed_bits = [("batch", bit) for bit in range(nb)] + [("head", 0), ("head", 1)]

    def add_packed(packed):
        axis_name, bit = packed_bits.pop(0)
        came = swap(packed, axis_name, 1 << bit)
        packed = line.tie(packed)
        return line.mark(packed + after(came, packed))

    main_grad = line.tie(own_grad[0:share]) + from_one.astype(F32) + from_two.astype(F32)
    own_grad = jnp.concatenate([main_grad, own_grad[share:]], 0)
    own_grad = line.mark(reorder_blocks(own_grad, to_natural)).reshape(3, share, features)
    grad_hidden = jnp.transpose(own_grad, (1, 0, 2))[None]
    packed = add_packed(packed)
    scatter_down.step()
    scatter_up.step()
    memory_part, memory_came = line.tie(memory_part), after(memory_came, *line.last)
    memory_mine = (memory_part[0].astype(F32) + memory_came.astype(F32)).astype(BF)
    memory_mine = line.mark(memory_mine)
    memory_came = swap(pin(memory_mine[1]), "head", 2)
    scatter_cross.step()
    scatter_self.step()
    packed = add_packed(packed)
    scatter_up.step()
    scatter_cross.step()
    memory_mine, memory_came = line.tie(memory_mine), after(memory_came, *line.last)
    memory_grad = memory_mine[0].astype(F32) + memory_came.astype(F32)
    grad_memory = line.mark(reorder_blocks(memory_grad, to_natural))[None]
    scatter_self.step()
    packed = add_packed(packed)
    scatter_cross.step()
    scatter_self.step()
    packed = add_packed(packed)
    scatter_self.step()
    while packed_bits:
        packed = add_packed(packed)
    scatters = (scatter_down, scatter_up, scatter_cross, scatter_self)
    for scatter in scatters:
        while not hasattr(scatter, "total"):
            scatter.step()
    grad_down, grad_up, grads_cross, grads_self = [scatter.total for scatter in scatters]

    ends = [0]
    for size in (2 * features, groups * 128, 2 * features, up_bias.shape[0], 9 * features):
        ends.append(ends[-1] + size)
    self_bias_grad = packed[ends[0] : ends[1]].reshape(2, -1)
    relpos_bias_grad = packed[ends[1] : ends[2]]
    cross_bias_grad = packed[ends[2] : ends[3]].reshape(2, -1)
    up_bias_grad = packed[ends[3] : ends[4]]
    feature_sums = packed[ends[4] : ends[5]].reshape(3, 3, features)

    return (
        layer_out,
        grad_hidden,
        grad_memory,
        jnp.concatenate([grads_self[:, 0:256], grads_self[:, 512:1024]], 1).reshape(blk, 3, 256),
        grads_self[:, 1024:1152],
        grads_self[:, 256:512],
        grads_cross[:, 0:256],
        grads_cross[:, 256:768].reshape(blk, 2, 256),
        grads_cross[:, 768:1024],
        grad_up,
        grad_down,
        self_bias_grad,
        relpos_bias_grad,
        cross_bias_grad,
        up_bias_grad,
        feature_sums[:, 0],
        feature_sums[:, 1],
        feature_sums[:, 2],
    )


def solution(mesh):
    in_specs = (
        P("batch", "head", None, None),
        P("batch", "head", None),
        P("batch", None, None, None),
        P("batch", None),
        P("batch", None),
        P(),
        P("batch", None, "head"),
        P("batch", "head"),
        P("batch", "head"),
        P("batch", "head"),
        P("batch", None, "head"),
        P("batch", "head"),
        P("batch", "head"),
        P("batch", "head"),
        P(),
        P(),
        P(),
        P(),
        P(),
        P(),
        P(),
    )
    out_specs = (
        P("batch", None, None, None),
        P("batch", "head", None, None),
        P("batch", "head", None),
        P("batch", None, "head"),
        P("batch", "head"),
        P("batch", "head"),
        P("batch", "head"),
        P("batch", None, "head"),
        P("batch", "head"),
        P("batch", "head"),
        P("batch", "head"),
        P(),
        P(),
        P(),
        P(),
        P(),
        P(),
        P(),
    )
    return jax.shard_map(
        per_device, mesh=mesh, in_specs=in_specs, out_specs=out_specs, check_vma=False
    )
```

```python
import functools

import jax
import jax.numpy as jnp
from jax import lax
from jax.experimental import pallas as pl
from jax.experimental.layout import Layout, with_layout_constraint
from jax.experimental.pallas import tpu as pltpu
from jax.sharding import PartitionSpec as P

BUCKETS = 32
HEAD_DIM = 64
WIDEST_DOC = 256
EPSILON = 1e-05
MASKED = -1e30
BF = jnp.bfloat16
F32 = jnp.float32
VMEM_BYTES = 56 * 1024 * 1024


def params():
    return pltpu.CompilerParams(vmem_limit_bytes=VMEM_BYTES)


def dot(a, b, ca, cb):
    return lax.dot_general(a, b, (((ca,), (cb,)), ((), ())), preferred_element_type=F32)


def whole(shape):
    return pl.BlockSpec(shape, lambda *_: (0,) * len(shape))


def swap(array_in, axis, bit):
    count = lax.axis_size(axis)
    return lax.ppermute(array_in, axis, [(i, i ^ bit) for i in range(count)])


def bits_of(axis):
    return (lax.axis_size(axis) - 1).bit_length()


def after(value, *earlier):
    return lax.optimization_barrier((value,) + earlier)[0]


def pin(value):
    return with_layout_constraint(value, Layout(tuple(range(value.ndim))))


class Line:
    def __init__(self):
        self.last = ()

    def tie(self, value):
        return after(value, *self.last) if self.last else value

    def mark(self, *values):
        self.last = values
        return values[0]


def chunk_of(rows):
    return rows // 4 if rows % 64 == 0 else rows


def stack_rows(*arrays):
    rows = [array.shape[0] for array in arrays]

    def body(*refs):
        at = 0
        for ref, count in zip(refs, rows):
            refs[-1][at : at + count] = ref[...]
            at += count

    return pl.pallas_call(
        body,
        out_shape=jax.ShapeDtypeStruct((sum(rows), arrays[0].shape[1]), arrays[0].dtype),
        compiler_params=params(),
        name="stack_rows",
    )(*arrays)


def add_blocks(parts, outs, dtype):
    rows = parts[0][0].shape[1]
    chunk = chunk_of(rows) if parts[0][0].size >= 1 << 20 else rows
    widths = [mine.shape[2] for mine, _ in parts]

    def body(*refs):
        ins, out_refs = refs[: 2 * len(parts)], refs[2 * len(parts) :]
        for out_ref, (members, chosen) in zip(out_refs, outs):
            at = 0
            for part in chosen:
                mine_ref, came_ref = ins[2 * part], ins[2 * part + 1]
                for place, block in enumerate(members):
                    total = mine_ref[block].astype(F32) + came_ref[block].astype(F32)
                    out_ref[place, :, at : at + widths[part]] = total.astype(dtype)
                at += widths[part]

    def spec(count, width):
        return pl.BlockSpec((count, chunk, width), lambda i: (0, i, 0))

    shapes = [(len(members), sum(widths[part] for part in chosen)) for members, chosen in outs]
    return pl.pallas_call(
        body,
        grid=(rows // chunk,),
        in_specs=[spec(array.shape[0], array.shape[2]) for pair in parts for array in pair],
        out_specs=[spec(*shape) for shape in shapes],
        out_shape=[jax.ShapeDtypeStruct((count, rows, width), dtype) for count, width in shapes],
        compiler_params=params(),
        name="add_blocks",
    )(*[array for pair in parts for array in pair])


class Gather:
    def __init__(self, line, shard):
        self.line = line
        self.nb, self.nz = bits_of("batch"), bits_of("head")
        self.buf = pin(shard).reshape((1,) * (self.nb + self.nz) + shard.shape)

    def send(self, axis_name, bit):
        self.axis = self.nb + self.nz - 1 - bit if axis_name == "head" else bit
        self.came = swap(self.line.tie(self.buf), axis_name, 1 << bit)

    def take(self):
        mine = self.line.tie(self.buf)
        self.buf = self.line.mark(jnp.concatenate([mine, after(self.came, mine)], self.axis))

    def columns(self, first, count):
        part = Gather.__new__(Gather)
        part.line, part.nb, part.nz = self.line, self.nb, self.nz
        part.buf = pin(self.buf[..., first : first + count])
        return part

    def close(self):
        shape = (1 << (self.nb - 1), 1 << self.nz) + self.buf.shape[-2:]
        return (self.buf.reshape(shape), self.came.reshape(shape))


class Scatter:
    def __init__(self, line, parts, orders, natural=False):
        self.natural = natural
        nb, self.nz = bits_of("batch"), bits_of("head")
        self.line = line
        self.groups, self.blk = parts[0][1].shape[1:3]
        self.left = [list(order) for order in orders]
        self.names = [sorted(order) for order in orders]
        self.heads = list(range(self.nz))
        self.mine, self.came = [None] * len(parts), [None] * len(parts)
        for number, (theirs, mine) in enumerate(parts):
            self.send(number, theirs, mine)

    def send(self, number, theirs, mine):
        bit = self.left[number].pop(0)
        self.names[number].remove(bit)
        self.mine[number] = mine
        self.came[number] = swap(theirs, "batch", 1 << bit)

    def step(self):
        tied = [self.line.tie(mine) for mine in self.mine]
        came = [after(came, mine) for came, mine in zip(self.came, tied)]
        pairs = [
            (one.reshape(-1, self.blk, one.shape[-1]), two.reshape(-1, self.blk, one.shape[-1]))
            for one, two in zip(tied, came)
        ]
        blocks = range(pairs[0][0].shape[0])
        everyone = list(range(len(pairs)))
        if self.left[0]:
            outs = []
            for number in everyone:
                place = self.names[number].index(self.left[number][0])
                bit = len(self.names[number]) - 1 - place
                for side in (1, 0):
                    chosen = [k for k in blocks if (k // self.groups >> bit & 1) == side]
                    outs.append((chosen, [number]))
            sums = add_blocks(pairs, outs, BF)
            self.line.mark(*sums)
            for number in everyone:
                self.send(number, sums[2 * number], sums[2 * number + 1])
            return
        if self.natural:
            (total,) = add_blocks(pairs, [(list(blocks), everyone)], BF)
            total = lax.psum_scatter(
                self.line.mark(total), "head", scatter_dimension=0, tiled=False
            )
            self.total = total.astype(F32)
            return
        if not self.heads:
            (total,) = add_blocks(pairs, [([0], everyone)], F32)
            self.total = self.line.mark(total).reshape(self.blk, -1)
            return
        bit = self.heads.pop(0)
        sides = [[k for k in blocks if (k & 1) == side] for side in (1, 0)]
        theirs, mine = add_blocks(pairs, [(side, everyone) for side in sides], BF)
        self.line.mark(theirs, mine)
        self.mine = [mine]
        self.came = [swap(theirs, "head", 1 << bit)]


def add_halo(own, one, two):
    count = one.shape[0]

    def body(own_ref, one_ref, two_ref, out_ref):
        out_ref[count:] = own_ref[count:]
        came = one_ref[...].astype(F32) + two_ref[...].astype(F32)
        out_ref[0:count] = own_ref[0:count] + came

    return pl.pallas_call(
        body,
        out_shape=jax.ShapeDtypeStruct(own.shape, own.dtype),
        compiler_params=params(),
        name="add_halo",
    )(own, one, two)


def bit_reverse(number, width):
    turned = 0
    for bit in range(width):
        turned |= ((number >> bit) & 1) << (width - 1 - bit)
    return turned


def reorder_blocks(array_in, table):
    count = table.shape[0]
    rows, features = array_in.shape
    blk = features // count
    if blk % 128:
        return jnp.take(array_in.reshape(rows, count, blk), table, axis=1).reshape(rows, features)

    def body(table_ref, in_ref, out_ref):
        for p in range(count):
            start = pl.multiple_of(table_ref[p] * blk, blk)
            out_ref[:, p * blk : (p + 1) * blk] = in_ref[:, pl.ds(start, blk)]

    return pl.pallas_call(
        body,
        out_shape=jax.ShapeDtypeStruct(array_in.shape, array_in.dtype),
        grid_spec=pltpu.PrefetchScalarGridSpec(
            num_scalar_prefetch=1,
            grid=(1,),
            in_specs=[pl.BlockSpec((rows, features), lambda p, table_ref: (0, 0))],
            out_specs=pl.BlockSpec((rows, features), lambda p, table_ref: (0, 0)),
        ),
        name="reorder",
    )(table, array_in)


def piece_specs(pieces, cols, col_block, step=None):
    count, _, blk, _ = pieces[0].shape
    return [
        pl.BlockSpec((count, 1, blk, cols), lambda j, *c: (0, j, 0, col_block + (c[0] if c else 0)))
        for _ in pieces
    ]


def flat_piece(ref):
    count, _, blk, cols = ref.shape
    return ref[...].reshape(count * blk, cols)


def over_features(x, piece_refs):
    depth = x.shape[1] // len(piece_refs)
    total = None
    for number, ref in enumerate(piece_refs):
        term = dot(x[:, number * depth : (number + 1) * depth], flat_piece(ref), 1, 0)
        total = term if total is None else total + term
    return total


def project(x, pieces, first_col, cols, tile, affine, out_dtype, name):
    rows, features = x.shape
    groups = pieces[0].shape[1]
    per = cols // tile

    def body(x_ref, *refs):
        *piece_refs, affine_ref, out_ref = refs
        acc = over_features(x_ref[...], piece_refs)
        out_ref[...] = ((acc + affine_ref[0:1]) * affine_ref[1:2]).astype(out_ref.dtype)

    return pl.pallas_call(
        body,
        grid=(groups, per),
        in_specs=[whole((rows, features))]
        + piece_specs(pieces, tile, first_col // tile)
        + [pl.BlockSpec((2, tile), lambda j, c: (0, j * per + c))],
        out_specs=pl.BlockSpec((rows, tile), lambda j, c: (0, j * per + c)),
        out_shape=jax.ShapeDtypeStruct((rows, groups * cols), out_dtype),
        compiler_params=params(),
        name=name,
    )(x, *pieces, affine)


def project_plain(x, pieces, first_col, cols, name):
    groups = pieces[0].shape[1]
    affine = jnp.stack([jnp.zeros((groups * cols,), F32), jnp.ones((groups * cols,), F32)])
    return project(x, pieces, first_col, cols, cols, affine, BF, name)


def add_rows(acc_ref, left, piece_refs):
    depth = acc_ref.shape[1] // len(piece_refs)
    for number, ref in enumerate(piece_refs):
        where = slice(number * depth, (number + 1) * depth)
        acc_ref[:, where] += dot(left, flat_piece(ref), 1, 1)


def row_mean(v):
    return jnp.mean(v, -1, keepdims=True)


def column_sum(v):
    return jnp.sum(v, 0, keepdims=True)


def normalize(v):
    centered = v - row_mean(v)
    spread = lax.rsqrt(row_mean(centered * centered) + EPSILON)
    return centered * spread, spread


def normalize_back(upstream, unit, spread, gain):
    a = upstream * gain
    return spread * (a - row_mean(a) - unit * row_mean(a * unit))


def close_sublayer(left, pieces, first_col, cols, residual, vectors, name):
    rows, features = residual.shape
    groups = pieces[0].shape[1]
    count = len(pieces)

    def body(left_ref, *refs):
        piece_refs = refs[:count]
        residual_ref, vectors_ref, normed_ref, low_ref, unit_ref, spread_ref, acc_ref = refs[count:]
        step = pl.program_id(0)

        @pl.when(step == 0)
        def _():
            acc_ref[...] = jnp.zeros_like(acc_ref)

        add_rows(acc_ref, left_ref[...], piece_refs)

        @pl.when(step == groups - 1)
        def _():
            v = residual_ref[...].astype(F32) + (acc_ref[...] + vectors_ref[2:3])
            unit, spread = normalize(v)
            normed = unit * vectors_ref[0:1] + vectors_ref[1:2]
            normed_ref[...] = normed
            low_ref[...] = normed.astype(BF)
            unit_ref[...] = unit
            spread_ref[...] = spread

    return pl.pallas_call(
        body,
        grid=(groups,),
        in_specs=[pl.BlockSpec((rows, cols), lambda j: (0, j))]
        + piece_specs(pieces, cols, first_col // cols)
        + [whole((rows, features)), whole((3, features))],
        out_specs=[whole((rows, features))] * 3 + [whole((rows, 1))],
        out_shape=[
            jax.ShapeDtypeStruct((rows, features), F32),
            jax.ShapeDtypeStruct((rows, features), BF),
            jax.ShapeDtypeStruct((rows, features), F32),
            jax.ShapeDtypeStruct((rows, 1), F32),
        ],
        scratch_shapes=[pltpu.VMEM((rows, features), F32)],
        compiler_params=params(),
        name=name,
    )(left, *pieces, residual, vectors)


def natural_from_exchange(order_ref, first, from_ref, to_ref, blk):
    if blk % 128:
        to_ref[...] = from_ref[...]
        return
    for p in range(from_ref.shape[1] // blk):
        start = pl.multiple_of(order_ref[first + p] * blk, blk)
        to_ref[:, pl.ds(start, blk)] = from_ref[:, p * blk : (p + 1) * blk]


def exchange_from_natural(order_ref, first, from_ref, to_ref, blk):
    if blk % 128:
        to_ref[...] = from_ref[...]
        return
    for p in range(from_ref.shape[1] // blk):
        start = pl.multiple_of(order_ref[first + p] * blk, blk)
        to_ref[:, p * blk : (p + 1) * blk] = from_ref[:, pl.ds(start, blk)]


def flat_natural(ref):
    count, _, blk, cols = ref.shape
    return ref[...].reshape(count * blk, cols)


def feed_forward(order, low, normed, weights, up_bias, vectors, grad_out):
    rows, features = normed.shape
    batches, groups, blk, both = weights.shape
    cols = both // 2

    def body(
        order_ref, low_ref, normed_ref, up_ref, down_ref, bias_ref, vectors_ref, grad_ref,
        active_ref, slope_ref, out_ref, third_ref, third_low_ref, sums_ref,
        natural_ref, acc_ref, turned_ref,
    ):
        step = pl.program_id(0)

        @pl.when(step == 0)
        def _():
            natural_from_exchange(order_ref, groups, low_ref, natural_ref, blk)
            acc_ref[...] = jnp.zeros_like(acc_ref)

        upper = dot(natural_ref[...], flat_natural(up_ref), 1, 0) + bias_ref[...]
        cdf = 0.5 * (1.0 + lax.erf(upper * 0.7071067811865476))
        active = (upper * cdf).astype(BF)
        slope = cdf + upper * jnp.exp(-0.5 * upper * upper) * 0.3989422804014327
        active_ref[...] = active
        slope_ref[...] = slope.astype(BF)
        acc_ref[...] += dot(active, flat_natural(down_ref), 1, 1)

        @pl.when(step == groups - 1)
        def _():
            exchange_from_natural(order_ref, groups, acc_ref, turned_ref, blk)
            v = normed_ref[...] + (turned_ref[...] + vectors_ref[2:3])
            unit, spread = normalize(v)
            gain = vectors_ref[0:1]
            out_ref[...] = (unit * gain + vectors_ref[1:2]).astype(BF)
            upstream = grad_ref[...]
            third = normalize_back(upstream, unit, spread, gain)
            third_ref[...] = third
            third_low_ref[...] = third.astype(BF)
            sums_ref[0:1] = column_sum(upstream * unit)
            sums_ref[1:2] = column_sum(upstream)
            sums_ref[2:3] = column_sum(third)

    return pl.pallas_call(
        body,
        grid_spec=pltpu.PrefetchScalarGridSpec(
            num_scalar_prefetch=1,
            grid=(groups,),
            in_specs=[
                whole((rows, features)),
                whole((rows, features)),
                pl.BlockSpec((batches, 1, blk, cols), lambda j, order: (0, j, 0, 0)),
                pl.BlockSpec((batches, 1, blk, cols), lambda j, order: (0, j, 0, 1)),
                pl.BlockSpec((1, cols), lambda j, order: (0, j)),
                whole((3, features)),
                whole((rows, features)),
            ],
            out_specs=[
                pl.BlockSpec((rows, cols), lambda j, order: (0, j)),
                pl.BlockSpec((rows, cols), lambda j, order: (0, j)),
                whole((rows, features)),
                whole((rows, features)),
                whole((rows, features)),
                whole((3, features)),
            ],
            scratch_shapes=[
                pltpu.VMEM((rows, features), BF),
                pltpu.VMEM((rows, features), F32),
                pltpu.VMEM((rows, features), F32),
            ],
        ),
        out_shape=[
            jax.ShapeDtypeStruct((rows, groups * cols), BF),
            jax.ShapeDtypeStruct((rows, groups * cols), BF),
            jax.ShapeDtypeStruct((rows, features), BF),
            jax.ShapeDtypeStruct((rows, features), F32),
            jax.ShapeDtypeStruct((rows, features), BF),
            jax.ShapeDtypeStruct((3, features), F32),
        ],
        compiler_params=params(),
        name="feed_forward",
    )(order, low, normed, weights, weights, up_bias, vectors, grad_out)


def norm_back_outputs(upstream, unit, spread, gain, grad_ref, grad_low_ref, sums_ref):
    grad = normalize_back(upstream, unit, spread, gain)
    grad_ref[...] = grad
    grad_low_ref[...] = grad.astype(BF)
    sums_ref[0:1] = column_sum(upstream * unit)
    sums_ref[1:2] = column_sum(upstream)
    sums_ref[2:3] = column_sum(grad)


def feed_forward_back(order, third_low, third, slope, weights, unit, spread, gain):
    rows, features = third.shape
    batches, groups, blk, both = weights.shape
    cols = both // 2

    def body(
        order_ref, third_low_ref, third_ref, slope_ref, up_ref, down_ref, unit_ref, spread_ref, gain_ref,
        upper_ref, bias_ref, grad_ref, grad_low_ref, sums_ref,
        natural_ref, acc_ref, turned_ref,
    ):
        step = pl.program_id(0)

        @pl.when(step == 0)
        def _():
            natural_from_exchange(order_ref, groups, third_low_ref, natural_ref, blk)
            acc_ref[...] = jnp.zeros_like(acc_ref)

        grad_upper = dot(natural_ref[...], flat_natural(down_ref), 1, 0)
        grad_upper = grad_upper * slope_ref[...].astype(F32)
        bias_ref[...] = column_sum(grad_upper)
        low = grad_upper.astype(BF)
        upper_ref[...] = low
        acc_ref[...] += dot(low, flat_natural(up_ref), 1, 1)

        @pl.when(step == groups - 1)
        def _():
            exchange_from_natural(order_ref, groups, acc_ref, turned_ref, blk)
            norm_back_outputs(
                turned_ref[...] + third_ref[...],
                unit_ref[...],
                spread_ref[...],
                gain_ref[...],
                grad_ref,
                grad_low_ref,
                sums_ref,
            )

    return pl.pallas_call(
        body,
        grid_spec=pltpu.PrefetchScalarGridSpec(
            num_scalar_prefetch=1,
            grid=(groups,),
            in_specs=[
                whole((rows, features)),
                whole((rows, features)),
                pl.BlockSpec((rows, cols), lambda j, order: (0, j)),
                pl.BlockSpec((batches, 1, blk, cols), lambda j, order: (0, j, 0, 0)),
                pl.BlockSpec((batches, 1, blk, cols), lambda j, order: (0, j, 0, 1)),
                whole((rows, features)),
                whole((rows, 1)),
                whole((1, features)),
            ],
            out_specs=[
                pl.BlockSpec((rows, cols), lambda j, order: (0, j)),
                pl.BlockSpec((1, cols), lambda j, order: (0, j)),
                whole((rows, features)),
                whole((rows, features)),
                whole((3, features)),
            ],
            scratch_shapes=[
                pltpu.VMEM((rows, features), BF),
                pltpu.VMEM((rows, features), F32),
                pltpu.VMEM((rows, features), F32),
            ],
        ),
        out_shape=[
            jax.ShapeDtypeStruct((rows, groups * cols), BF),
            jax.ShapeDtypeStruct((1, groups * cols), F32),
            jax.ShapeDtypeStruct((rows, features), F32),
            jax.ShapeDtypeStruct((rows, features), BF),
            jax.ShapeDtypeStruct((3, features), F32),
        ],
        compiler_params=params(),
        name="feed_forward_back",
    )(order, third_low, third, slope, weights, weights, unit, spread, gain)


def cross_query_back(grad_query, pieces, first_col, cols, second, unit, spread, gain):
    rows, features = second.shape
    groups = pieces[0].shape[1]
    count = len(pieces)

    def body(left_ref, *refs):
        piece_refs = refs[:count]
        second_ref, unit_ref, spread_ref, gain_ref, grad_ref, grad_low_ref, sums_ref, acc_ref = refs[
            count:
        ]
        step = pl.program_id(0)

        @pl.when(step == 0)
        def _():
            acc_ref[...] = second_ref[...]

        add_rows(acc_ref, left_ref[...], piece_refs)

        @pl.when(step == groups - 1)
        def _():
            norm_back_outputs(
                acc_ref[...],
                unit_ref[...],
                spread_ref[...],
                gain_ref[...],
                grad_ref,
                grad_low_ref,
                sums_ref,
            )

    return pl.pallas_call(
        body,
        grid=(groups,),
        in_specs=[pl.BlockSpec((rows, cols), lambda j: (0, j))]
        + piece_specs(pieces, cols, first_col // cols)
        + [whole((rows, features)), whole((rows, features)), whole((rows, 1)), whole((1, features))],
        out_specs=[whole((rows, features)), whole((rows, features)), whole((3, features))],
        out_shape=[
            jax.ShapeDtypeStruct((rows, features), F32),
            jax.ShapeDtypeStruct((rows, features), BF),
            jax.ShapeDtypeStruct((3, features), F32),
        ],
        scratch_shapes=[pltpu.VMEM((rows, features), F32)],
        compiler_params=params(),
        name="cross_query_back",
    )(grad_query, *pieces, second, unit, spread, gain)


def rows_back(left, pieces, first_col, cols, name):
    rows = left.shape[0]
    count = len(pieces)
    groups = pieces[0].shape[1]
    features = count * pieces[0].shape[0] * pieces[0].shape[2]

    def body(left_ref, *refs):
        piece_refs = refs[:count]
        low_ref, high_ref, acc_ref = refs[count:]
        step = pl.program_id(0)

        @pl.when(step == 0)
        def _():
            acc_ref[...] = jnp.zeros_like(acc_ref)

        add_rows(acc_ref, left_ref[...], piece_refs)

        @pl.when(step == groups - 1)
        def _():
            low_ref[...] = acc_ref[0 : rows // 2].astype(BF)
            high_ref[...] = acc_ref[rows // 2 :].astype(BF)

    return pl.pallas_call(
        body,
        grid=(groups,),
        in_specs=[pl.BlockSpec((rows, cols), lambda j: (0, j))]
        + piece_specs(pieces, cols, first_col // cols),
        out_specs=[whole((rows // 2, features))] * 2,
        out_shape=[jax.ShapeDtypeStruct((rows // 2, features), BF)] * 2,
        scratch_shapes=[pltpu.VMEM((rows, features), F32)],
        compiler_params=params(),
        name=name,
    )(left, *pieces)


def input_back(grad_query, grad_kv, grad_rel, pieces, others, first):
    rows, features = first.shape
    long_rows = grad_kv.shape[0]
    halo = long_rows - rows
    groups = pieces[0].shape[1]
    count = len(pieces)
    width = grad_query.shape[1] // groups
    rel_width = grad_rel.shape[1] // groups

    def body(query_ref, kv_ref, rel_ref, *refs):
        parts = [refs[count * k : count * (k + 1)] for k in range(4)]
        first_ref, two_ref, one_ref, own_ref, acc_ref = refs[4 * count :]
        step = pl.program_id(0)

        @pl.when(step == 0)
        def _():
            acc_ref[0:halo] = jnp.zeros((halo, features), F32)
            acc_ref[halo:] = first_ref[...]

        own_acc = acc_ref.at[halo:]
        add_rows(own_acc, query_ref[...], parts[0])
        add_rows(acc_ref, kv_ref[:, 0:width], parts[1])
        add_rows(acc_ref, kv_ref[:, width : 2 * width], parts[2])
        add_rows(own_acc, rel_ref[...], parts[3])

        @pl.when(step == groups - 1)
        def _():
            two_ref[...] = acc_ref[0 : halo // 2].astype(BF)
            one_ref[...] = acc_ref[halo // 2 : halo].astype(BF)
            own_ref[...] = acc_ref[halo:]

    return pl.pallas_call(
        body,
        grid=(groups,),
        in_specs=[
            pl.BlockSpec((rows, width), lambda j: (0, j)),
            pl.BlockSpec((long_rows, 2 * width), lambda j: (0, j)),
            pl.BlockSpec((rows, rel_width), lambda j: (0, j)),
        ]
        + piece_specs(pieces, width, 0)
        + piece_specs(pieces, width, 1)
        + piece_specs(others, width, 0)
        + piece_specs(others, rel_width, width // rel_width)
        + [whole((rows, features))],
        out_specs=[whole((halo // 2, features))] * 2 + [whole((rows, features))],
        out_shape=[
            jax.ShapeDtypeStruct((halo // 2, features), BF),
            jax.ShapeDtypeStruct((halo // 2, features), BF),
            jax.ShapeDtypeStruct((rows, features), F32),
        ],
        scratch_shapes=[pltpu.VMEM((long_rows, features), F32)],
        compiler_params=params(),
        name="input_back",
    )(grad_query, grad_kv, grad_rel, *pieces, *pieces, *others, *others, first)


def weight_products(order, entries, half, extra, parts, pieces, groups, name):
    features = entries[0][0].shape[1]
    depth = features // 2
    blk = depth // pieces
    widths = [right.shape[1] // groups for _, right in entries]
    total = sum(widths)
    count = len(entries)
    outs = []
    if parts is None:
        outs.append((0, total, list(range(pieces))))
    else:
        at = 0
        for width, bit in parts:
            for side in (1, 0):
                outs.append((at, width, [p for p in range(pieces) if (p >> bit & 1) == side]))
            at += width

    def body(order_ref, *refs):
        lefts, rights = refs[:count], refs[count : 2 * count]
        out_refs = refs[len(refs) - len(outs) :]
        at = 0
        for left_ref, right_ref, width in zip(lefts, rights, widths):
            term = dot(left_ref[...], right_ref[...], 0, 0).reshape(pieces, blk, width)
            if extra is not None:
                term = term + refs[2 * count][:, 0, :, at : at + width].astype(F32)
            term = term.astype(BF)
            for out_ref, (first, size, members) in zip(out_refs, outs):
                low, high = max(at, first), min(at + width, first + size)
                if low >= high:
                    continue
                for place, piece in enumerate(members):
                    out_ref[place, 0, :, low - first : high - first] = term[
                        piece, :, low - at : high - at
                    ]
            at += width

    def block(number, width):
        return pl.BlockSpec((number, 1, blk, width), lambda j, order: (0, j, 0, 0))

    in_specs = [
        pl.BlockSpec((left.shape[0], depth), lambda j, order: (0, half)) for left, _ in entries
    ]
    in_specs += [
        pl.BlockSpec((right.shape[0], width), lambda j, order: (0, order[j]))
        for (_, right), width in zip(entries, widths)
    ]
    operands = [left for left, _ in entries] + [right for _, right in entries]
    if extra is not None:
        in_specs.append(block(pieces, total))
        operands.append(extra)
    return pl.pallas_call(
        body,
        grid_spec=pltpu.PrefetchScalarGridSpec(
            num_scalar_prefetch=1,
            grid=(groups,),
            in_specs=in_specs,
            out_specs=[block(len(members), width) for _, width, members in outs],
        ),
        out_shape=[
            jax.ShapeDtypeStruct((len(members), groups, blk, width), BF)
            for _, width, members in outs
        ],
        compiler_params=params(),
        name=name,
    )(order, *operands)


def half_masks(rows):
    lane = lax.broadcasted_iota(jnp.int32, (rows, 128), 1)
    return [
        jnp.where((lane >= 64 * half) & (lane < 64 * half + 64), 1.0, 0.0).astype(F32)
        for half in range(2)
    ]


def lanes_and_rows(share):
    lane = lax.broadcasted_iota(jnp.int32, (share, share), 1)
    row = lax.broadcasted_iota(jnp.int32, (share, share), 0)
    return lane > row


def turn_right(block):
    return pltpu.roll(block, 1, 1, stride=1, stride_axis=0)


def skew(distance, later):
    share = later.shape[0]
    tracks = []
    for n in range(distance.shape[0] // share):
        rows = slice(n * share, (n + 1) * share)
        far, near = turn_right(distance[rows, 0:share]), turn_right(distance[rows, share:])
        tracks.append(jnp.concatenate([far, jnp.where(later, near, far), near], 1))
    return jnp.concatenate(tracks, 0)


def unskew_sources(grid, later):
    share = later.shape[0]
    tracks = []
    for n in range(grid.shape[0] // share):
        old, mid, new = [
            grid[n * share : (n + 1) * share, c * share : (c + 1) * share] for c in range(3)
        ]
        tracks.append(jnp.concatenate([jnp.where(later, old, mid), jnp.where(later, mid, new)], 1))
    return jnp.concatenate(tracks, 0)


def turn_blocks(array_in, share):
    rows = array_in.shape[0]
    return jnp.concatenate(
        [
            jnp.concatenate(
                [turn_right(array_in[r : r + share, c : c + share]) for c in (0, share)], 1
            )
            for r in range(0, rows, share)
        ],
        0,
    )


def self_attention(qk, values, relpos, mask, turned, share):
    rows, window = 3 * share, 3 * share
    groups = values.shape[1] // 256
    long_rows = qk.shape[0]
    halo = long_rows - rows

    def body(q_ref, k_ref, v_ref, rel_ref, mask_ref, turned_ref, ctx_ref, raised_ref, own_ref):
        halves = half_masks(rows)
        later = lanes_and_rows(share)
        lane = lax.broadcasted_iota(jnp.int32, (rows, 128), 1)
        rel = rel_ref[...]
        high = rel.astype(BF)
        split = jnp.concatenate([high, (rel - high.astype(F32)).astype(BF)], 1)
        row_id = lax.broadcasted_iota(jnp.int32, (256, 2 * share), 0) & 127
        track = lax.broadcasted_iota(jnp.int32, (rows, 1), 0) >= share
        own_all = jnp.zeros((rows, 128), F32)
        for pair in range(2):
            cols = slice(128 * pair, 128 * pair + 128)
            q = q_ref[halo:, cols]
            k, v = k_ref[0:window, cols], v_ref[0:window, cols]
            own_k = k_ref[halo:, cols].astype(F32)
            own_v = v_ref[halo:, cols].astype(F32)
            product = q.astype(F32) * own_k
            mixed = jnp.zeros((rows, 128), F32)
            for half in range(2):
                head = 2 * pair + half
                scores = dot(q * halves[half].astype(BF), k, 1, 1)
                table = jnp.where(row_id == turned_ref[...] + 32 * head, 1.0, 0.0).astype(BF)
                scores = scores + skew(dot(split, table, 1, 0), later) + mask_ref[...]
                own = jnp.sum(
                    product * halves[half] + jnp.where(lane == 32 * head, rel, 0.0), -1, keepdims=True
                )
                own = jnp.where(track, own, MASKED)
                top = jnp.maximum(jnp.max(scores, -1, keepdims=True), own)
                raised = jnp.exp(scores - top)
                own_raised = jnp.exp(own - top)
                scale = 1.0 / (jnp.sum(raised, -1, keepdims=True) + own_raised)
                raised = raised.astype(BF)
                raised_ref[head] = raised
                own_all = jnp.where(lane == head, own_raised, own_all)
                own_all = jnp.where(lane == head + 4, scale, own_all)
                mixed = mixed + (dot(raised, v, 1, 0) + own_raised * own_v) * (scale * halves[half])
            ctx_ref[:, cols] = mixed.astype(BF)
        own_ref[...] = own_all

    return pl.pallas_call(
        body,
        grid=(groups,),
        in_specs=[
            pl.BlockSpec((long_rows, 256), lambda j: (0, 2 * j)),
            pl.BlockSpec((long_rows, 256), lambda j: (0, 2 * j + 1)),
            pl.BlockSpec((long_rows, 256), lambda j: (0, j)),
            pl.BlockSpec((rows, 128), lambda j: (0, j)),
            whole((rows, window)),
            whole((1, 2 * share)),
        ],
        out_specs=[
            pl.BlockSpec((rows, 256), lambda j: (0, j)),
            pl.BlockSpec((4, rows, window), lambda j: (j, 0, 0)),
            pl.BlockSpec((rows, 128), lambda j: (0, j)),
        ],
        out_shape=[
            jax.ShapeDtypeStruct((rows, groups * 256), BF),
            jax.ShapeDtypeStruct((4 * groups, rows, window), BF),
            jax.ShapeDtypeStruct((rows, groups * 128), F32),
        ],
        compiler_params=params(),
        name="self_attention",
    )(qk, qk, values, relpos, mask, turned)


def self_attention_back(qk, values, raised, own_raised, grad_ctx, straight, share):
    rows, window = 3 * share, 3 * share
    groups = values.shape[1] // 256
    long_rows = qk.shape[0]
    halo = long_rows - rows

    def body(
        q_ref, k_ref, v_ref, raised_ref, own_ref, grad_ref, straight_ref,
        gq_ref, gkv_ref, grel_ref, sums_ref, rel_sums_ref,
    ):
        halves = half_masks(rows)
        later = lanes_and_rows(share)
        lane = lax.broadcasted_iota(jnp.int32, (rows, 128), 1)
        turn = jnp.where(
            lax.broadcasted_iota(jnp.int32, (2 * share, 2 * share), 0)
            + lax.broadcasted_iota(jnp.int32, (2 * share, 2 * share), 1)
            == 2 * share - 1,
            1.0,
            0.0,
        ).astype(BF)
        column = lax.broadcasted_iota(jnp.int32, (2 * share, 128), 1)
        grel = jnp.zeros((rows, 128), F32)
        own_all = own_ref[...]

        def pick(number):
            return jnp.sum(jnp.where(lane == number, own_all, 0.0), -1, keepdims=True)

        for pair in range(2):
            cols = slice(128 * pair, 128 * pair + 128)
            q = q_ref[halo:, cols]
            k, v = k_ref[0:window, cols], v_ref[0:window, cols]
            own_k = k_ref[halo:, cols].astype(F32)
            own_v = v_ref[halo:, cols].astype(F32)
            scales = [pick(2 * pair + half + 4) for half in range(2)]
            grad_wide = grad_ref[:, cols].astype(F32)
            grad_wide = grad_wide * (scales[0] * halves[0] + scales[1] * halves[1])
            grad = grad_wide.astype(BF)
            own_product = grad_wide * own_v
            gq = jnp.zeros((rows, 128), F32)
            own_spread = jnp.zeros((rows, 128), F32)
            own_weight = jnp.zeros((rows, 128), F32)
            score_parts, prob_parts, q_parts, g_parts = [], [], [], []
            for half in range(2):
                head = 2 * pair + half
                low_half = halves[half].astype(BF)
                p = raised_ref[head]
                p_wide = p.astype(F32)
                grad_half = grad * low_half
                grad_probs = dot(grad_half, v, 1, 1)
                own_p = pick(head)
                own_grad = jnp.sum(own_product * halves[half], -1, keepdims=True)
                row_dot = jnp.sum(p_wide * grad_probs, -1, keepdims=True) + own_p * own_grad
                row_dot = row_dot * scales[half]
                grad_scores = p_wide * (grad_probs - row_dot)
                source = unskew_sources(grad_scores, later).astype(BF)
                grad_scores = grad_scores.astype(BF)
                grad_own = (own_p * (own_grad - row_dot)).astype(BF).astype(F32)
                gq = gq + (dot(grad_scores, k, 1, 0) + grad_own * own_k) * halves[half]
                own_spread = own_spread + grad_own * halves[half]
                own_weight = own_weight + own_p * halves[half]
                score_parts.append(grad_scores)
                prob_parts.append(p)
                q_parts.append(q * low_half)
                g_parts.append(grad_half)
                turned = turn_blocks(dot(source, turn, 1, 0), share).astype(BF)
                table = jnp.where(column == straight_ref[...] + 32 * head, 1.0, 0.0).astype(BF)
                grel = grel + dot(turned, table, 1, 0) + jnp.where(lane == 32 * head, grad_own, 0.0)
            gk = dot(
                jnp.concatenate(q_parts, 0), jnp.concatenate(score_parts, 0), 0, 0
            ).T
            gv = dot(
                jnp.concatenate(g_parts, 0), jnp.concatenate(prob_parts, 0), 0, 0
            ).T
            gq = gq * 0.125
            gq_ref[:, cols] = gq.astype(BF)
            own_gk = own_spread * q.astype(F32)
            own_gv = own_weight * grad_wide
            vcols = slice(256 + 128 * pair, 256 + 128 * pair + 128)
            gkv_ref[0:window, cols] = gk.astype(BF)
            gkv_ref[0:window, vcols] = gv.astype(BF)
            gkv_ref[window:, cols] = own_gk[share:].astype(BF)
            gkv_ref[window:, vcols] = own_gv[share:].astype(BF)
            sums_ref[0:1, cols] = column_sum(gq)
            sums_ref[1:2, cols] = column_sum(gv) + column_sum(own_gv[share:])
        grel_ref[...] = grel.astype(BF)
        rel_sums_ref[...] = column_sum(grel)

    return pl.pallas_call(
        body,
        grid=(groups,),
        in_specs=[
            pl.BlockSpec((long_rows, 256), lambda j: (0, 2 * j)),
            pl.BlockSpec((long_rows, 256), lambda j: (0, 2 * j + 1)),
            pl.BlockSpec((long_rows, 256), lambda j: (0, j)),
            pl.BlockSpec((4, rows, window), lambda j: (j, 0, 0)),
            pl.BlockSpec((rows, 128), lambda j: (0, j)),
            pl.BlockSpec((rows, 256), lambda j: (0, j)),
            whole((2 * share, 1)),
        ],
        out_specs=[
            pl.BlockSpec((rows, 256), lambda j: (0, j)),
            pl.BlockSpec((long_rows, 512), lambda j: (0, j)),
            pl.BlockSpec((rows, 128), lambda j: (0, j)),
            pl.BlockSpec((2, 256), lambda j: (0, j)),
            pl.BlockSpec((1, 128), lambda j: (0, j)),
        ],
        out_shape=[
            jax.ShapeDtypeStruct((rows, groups * 256), BF),
            jax.ShapeDtypeStruct((long_rows, groups * 512), BF),
            jax.ShapeDtypeStruct((rows, groups * 128), BF),
            jax.ShapeDtypeStruct((2, groups * 256), F32),
            jax.ShapeDtypeStruct((1, groups * 128), F32),
        ],
        compiler_params=params(),
        name="self_attention_back",
    )(qk, qk, values, raised, own_raised, grad_ctx, straight)


def cross_attention(queries, kv):
    rows, places = queries.shape[0], kv.shape[0]
    groups = queries.shape[1] // 256

    def body(q_ref, k_ref, v_ref, ctx_ref, raised_ref, scale_ref):
        halves = half_masks(rows)
        lane = lax.broadcasted_iota(jnp.int32, (rows, 128), 1)
        scales = jnp.zeros((rows, 128), F32)
        for pair in range(2):
            cols = slice(128 * pair, 128 * pair + 128)
            q, k, v = q_ref[:, cols], k_ref[:, cols], v_ref[:, cols]
            mixed = jnp.zeros((rows, 128), F32)
            for half in range(2):
                head = 2 * pair + half
                scores = dot(q * halves[half].astype(BF), k, 1, 1)
                raised = jnp.exp(scores - jnp.max(scores, -1, keepdims=True))
                scale = 1.0 / jnp.sum(raised, -1, keepdims=True)
                raised = raised.astype(BF)
                raised_ref[head] = raised
                scales = jnp.where(lane == head, scale, scales)
                mixed = mixed + dot(raised, v, 1, 0) * (scale * halves[half])
            ctx_ref[:, cols] = mixed.astype(BF)
        scale_ref[...] = scales

    return pl.pallas_call(
        body,
        grid=(groups,),
        in_specs=[
            pl.BlockSpec((rows, 256), lambda j: (0, j)),
            pl.BlockSpec((places, 256), lambda j: (0, 2 * j)),
            pl.BlockSpec((places, 256), lambda j: (0, 2 * j + 1)),
        ],
        out_specs=[
            pl.BlockSpec((rows, 256), lambda j: (0, j)),
            pl.BlockSpec((4, rows, places), lambda j: (j, 0, 0)),
            pl.BlockSpec((rows, 128), lambda j: (0, j)),
        ],
        out_shape=[
            jax.ShapeDtypeStruct((rows, groups * 256), BF),
            jax.ShapeDtypeStruct((4 * groups, rows, places), BF),
            jax.ShapeDtypeStruct((rows, groups * 128), F32),
        ],
        compiler_params=params(),
        name="cross_attention",
    )(queries, kv, kv)


def cross_attention_back(queries, kv, raised, scales, grad_ctx):
    rows, places = queries.shape[0], kv.shape[0]
    groups = queries.shape[1] // 256

    def body(q_ref, k_ref, v_ref, raised_ref, scale_ref, grad_ref, gq_ref, gkv_ref, sums_ref):
        halves = half_masks(rows)
        lane = lax.broadcasted_iota(jnp.int32, (rows, 128), 1)
        scale_all = scale_ref[...]
        for pair in range(2):
            cols = slice(128 * pair, 128 * pair + 128)
            q, k, v = q_ref[:, cols], k_ref[:, cols], v_ref[:, cols]
            scale = [
                jnp.sum(jnp.where(lane == 2 * pair + half, scale_all, 0.0), -1, keepdims=True)
                for half in range(2)
            ]
            grad = grad_ref[:, cols].astype(F32) * (scale[0] * halves[0] + scale[1] * halves[1])
            grad = grad.astype(BF)
            gq = jnp.zeros((rows, 128), F32)
            score_parts, prob_parts, q_parts, g_parts = [], [], [], []
            for half in range(2):
                low_half = halves[half].astype(BF)
                p = raised_ref[2 * pair + half]
                p_wide = p.astype(F32)
                grad_half = grad * low_half
                grad_probs = dot(grad_half, v, 1, 1)
                row_dot = jnp.sum(p_wide * grad_probs, -1, keepdims=True) * scale[half]
                grad_scores = (p_wide * (grad_probs - row_dot)).astype(BF)
                gq = gq + dot(grad_scores, k, 1, 0) * halves[half]
                score_parts.append(grad_scores)
                prob_parts.append(p)
                q_parts.append(q * low_half)
                g_parts.append(grad_half)
            gk = dot(
                jnp.concatenate(q_parts, 0), jnp.concatenate(score_parts, 0), 0, 0
            ).T
            gv = dot(
                jnp.concatenate(g_parts, 0), jnp.concatenate(prob_parts, 0), 0, 0
            ).T
            gq = gq * 0.125
            gq_ref[:, cols] = gq.astype(BF)
            vcols = slice(256 + 128 * pair, 256 + 128 * pair + 128)
            gkv_ref[:, cols] = gk.astype(BF)
            gkv_ref[:, vcols] = gv.astype(BF)
            sums_ref[0:1, cols] = column_sum(gq)
            sums_ref[1:2, cols] = column_sum(gv)

    return pl.pallas_call(
        body,
        grid=(groups,),
        in_specs=[
            pl.BlockSpec((rows, 256), lambda j: (0, j)),
            pl.BlockSpec((places, 256), lambda j: (0, 2 * j)),
            pl.BlockSpec((places, 256), lambda j: (0, 2 * j + 1)),
            pl.BlockSpec((4, rows, places), lambda j: (j, 0, 0)),
            pl.BlockSpec((rows, 128), lambda j: (0, j)),
            pl.BlockSpec((rows, 256), lambda j: (0, j)),
        ],
        out_specs=[
            pl.BlockSpec((rows, 256), lambda j: (0, j)),
            pl.BlockSpec((places, 512), lambda j: (0, j)),
            pl.BlockSpec((2, 256), lambda j: (0, j)),
        ],
        out_shape=[
            jax.ShapeDtypeStruct((rows, groups * 256), BF),
            jax.ShapeDtypeStruct((places, groups * 512), BF),
            jax.ShapeDtypeStruct((2, groups * 256), F32),
        ],
        compiler_params=params(),
        name="cross_attention_back",
    )(queries, kv, kv, raised, scales, grad_ctx)


def per_device(
    hidden,
    memory,
    grad_out,
    lengths,
    key_mask,
    buckets,
    self_weight,
    relpos_weight,
    selfout_weight,
    crossq_weight,
    crosskv_weight,
    crossout_weight,
    up_weight,
    down_weight,
    self_bias,
    relpos_bias,
    cross_bias,
    up_bias,
    norm_gain,
    norm_bias,
    out_bias,
):
    batches, groups = lax.axis_size("batch"), lax.axis_size("head")
    b, z = lax.axis_index("batch"), lax.axis_index("head")
    nb = bits_of("batch")
    share, features = hidden.shape[1], hidden.shape[3]
    length = share * groups
    rows, window = 3 * share, 3 * share
    assert share == 128 and hidden.shape[0] == 1 and WIDEST_DOC <= 2 * share
    assert batches == 1 << nb and features % batches == 0 and groups == 4
    near, far = list(range(1, nb)), list(reversed(range(1, nb)))

    turned_ids = jnp.array([bit_reverse(p, nb) for p in range(batches)], jnp.int32)
    to_exchange = b ^ turned_ids
    natural = lax.iota(jnp.int32, batches) ^ b
    to_natural = jnp.zeros_like(natural)
    for bit in range(nb):
        to_natural = to_natural | (((natural >> bit) & 1) << (nb - 1 - bit))
    group_order = z ^ lax.iota(jnp.int32, groups)

    def small_features(stack):
        count = stack.shape[0]
        blocks = stack.reshape(count, batches, features // batches)
        return jnp.take(blocks, to_exchange, axis=1).reshape(count, features)

    blk = self_weight.shape[0]
    assert nb >= 2 and bits_of("head") == 2
    line = Line()
    self_shard = jnp.concatenate([self_weight.reshape(blk, -1), relpos_weight], 1).astype(BF)
    gather_self = Gather(line, line.mark(pin(self_shard)))
    gather_self.send("head", 1)
    ffn_shard = line.mark(
        pin(jnp.concatenate([line.tie(up_weight), down_weight], 1).astype(BF))
    )
    gather_ffn = Gather(line, ffn_shard)

    columns = jnp.concatenate(
        [
            self_bias[0].reshape(groups, -1),
            self_bias[1].reshape(groups, -1),
            cross_bias[0].reshape(groups, -1),
            cross_bias[1].reshape(groups, -1),
            relpos_bias.reshape(groups, -1),
            up_bias.reshape(groups, -1),
        ],
        1,
    )
    columns = jnp.take(columns, group_order, axis=0)
    query_bias, value_bias = columns[:, 0:256], columns[:, 256:512]
    cross_query_bias, cross_value_bias = columns[:, 512:768], columns[:, 768:1024]
    rel_row = columns[:, 1024:1152].reshape(1, -1)
    up_row = columns[:, 1152:].reshape(1, -1)

    memory_own = line.mark(reorder_blocks(line.tie(memory[0]), to_exchange))
    own = jnp.transpose(line.tie(hidden[0]), (1, 0, 2)).reshape(rows, features)
    own = line.mark(reorder_blocks(own, to_exchange))
    upstream = lax.dynamic_slice_in_dim(line.tie(grad_out[0]), z * share, share, 0)
    upstream = jnp.transpose(upstream, (1, 0, 2)).reshape(rows, features)
    upstream = line.mark(reorder_blocks(upstream, to_exchange))
    chain = list(range(groups))

    vectors = small_features(jnp.concatenate([norm_gain, norm_bias, out_bias], 0))
    vectors = vectors.reshape(3, 3, features).transpose(1, 0, 2)
    none = jnp.zeros((groups, 256), F32)

    def affine(bias, scale):
        return jnp.stack([bias, jnp.full(bias.shape, scale, F32)])

    scales = jnp.concatenate([none + 0.125, none + 1.0], 1).reshape(-1)
    qk_affine = jnp.stack([jnp.concatenate([query_bias, none], 1).reshape(-1), scales])
    value_affine = affine(value_bias.reshape(-1), 1.0)
    rel_affine = affine(rel_row[0], 1.0)
    cross_query_affine = affine(cross_query_bias.reshape(-1), 0.125)
    cross_kv_affine = affine(jnp.concatenate([none, cross_value_bias], 1).reshape(-1), 1.0)

    places = lax.iota(jnp.int32, length)
    doc_ends = jnp.cumsum(lengths[0])
    segment = jnp.sum((places[:, None] >= doc_ends[None, :]).astype(jnp.int32), -1)
    lead = window - share
    padded_segment = jnp.concatenate([jnp.full((lead,), -1, jnp.int32), segment])
    padded_mask = jnp.concatenate([jnp.zeros((lead,), jnp.int32), key_mask[0]])
    key_segment = lax.dynamic_slice_in_dim(padded_segment, z * share, window)
    key_open = lax.dynamic_slice_in_dim(padded_mask, z * share, window)
    query_segment = lax.dynamic_slice_in_dim(segment, z * share, share)
    query_at = lax.iota(jnp.int32, share)[:, None] + lead
    key_at = lax.iota(jnp.int32, window)[None, :]
    joined = (query_segment[:, None] == key_segment[None, :]) & (
        (key_open[None, :] == 1) | (query_at == key_at)
    )
    allowed_main = joined & (key_at <= query_at)
    allowed_pred = joined & (key_at < query_at)
    mask = jnp.where(jnp.stack([allowed_main, allowed_pred, allowed_pred]), 0.0, MASKED)
    mask = mask.reshape(rows, window).astype(F32)
    straight = buckets[0 : 2 * share]
    turned = straight[::-1]

    mask = line.mark(line.tie(mask))
    assert nb >= 2 and bits_of("head") == 2
    gather_cross = Gather(
        line,
        jnp.concatenate(
            [selfout_weight, crossq_weight, crosskv_weight.reshape(blk, -1), crossout_weight], 1
        ).astype(BF),
    )
    gather_self.take()
    gather_self.send("head", 0)
    gather_ffn.send("head", 1)
    gather_self.take()
    parts_self = [gather_self.columns(0, 512), gather_self.columns(512, 384)]
    orders_self = [near, far]
    for part, part_order in zip(parts_self, orders_self):
        part.send("batch", part_order[0])
    gather_ffn.take()
    gather_ffn.send("head", 0)
    for number in range(1, nb - 1):
        for part, part_order in zip(parts_self, orders_self):
            part.take()
            part.send("batch", part_order[number])
    gather_cross.send("head", 1)
    gather_ffn.take()
    for part in parts_self:
        part.take()
        part.send("batch", 0)
    gather_cross.take()
    gather_cross.send("head", 0)
    main = line.tie(own[0:share])
    before_one = lax.ppermute(main, "head", [(i, i + 1) for i in chain[:-1]])
    before_two = lax.ppermute(main, "head", [(i, i + 2) for i in chain[:-2]])
    gather_cross.take()
    parts_cross = [gather_cross.columns(0, 512), gather_cross.columns(512, 768)]
    orders_cross = [far, near]
    for part, part_order in zip(parts_cross, orders_cross):
        part.send("batch", part_order[0])
    extended = line.mark(stack_rows(before_two, before_one, line.tie(own)))
    memory_came = swap(line.tie(memory_own), "head", 2)
    weights_qk, weights_vr = [part.close() for part in parts_self]

    order = jnp.concatenate([group_order, to_exchange]).astype(jnp.int32)
    values = line.mark(
        project(line.tie(extended), weights_vr, 0, 256, 256, value_affine, BF, "self_v")
    )
    relpos = line.mark(
        project(line.tie(own), weights_vr, 256, 128, 128, rel_affine, F32, "self_rel")
    )
    for number in range(1, nb - 1):
        for part, part_order in zip(parts_cross, orders_cross):
            part.take()
            part.send("batch", part_order[number])
    weights_ffn = line.tie(gather_ffn.buf).reshape((groups,) + ffn_shard.shape)
    weights_ffn = lax.all_gather(weights_ffn, "batch", axis=0)
    if blk % 128:
        weights_ffn = jnp.take(weights_ffn, to_exchange, axis=0)
    qk = line.mark(project(line.tie(extended), weights_qk, 0, 512, 512, qk_affine, BF, "self_qk"))
    memory_half = line.mark(jnp.concatenate([line.tie(memory_own), memory_came], 0))
    memory_came = swap(memory_half, "head", 1)
    context, self_probs, self_own = self_attention(
        line.tie(qk), values, relpos, mask, turned.reshape(1, -1), share
    )
    line.mark(context)
    for part in parts_cross:
        part.take()
        part.send("batch", 0)
    weights_out, weights_kv = [part.close() for part in parts_cross]
    normed1, normed1_low, unit1, spread1 = close_sublayer(
        line.tie(context), weights_out, 0, 256, own, vectors[0], "self_out"
    )
    line.mark(normed1)
    cross_q = line.mark(
        project(
            line.tie(normed1_low), weights_out, 256, 256, 256, cross_query_affine, BF, "cross_q"
        )
    )
    memory_all = line.mark(jnp.concatenate([line.tie(memory_half), memory_came], 0))
    cross_kv = line.mark(
        project(line.tie(memory_all), weights_kv, 0, 512, 512, cross_kv_affine, BF, "cross_kv")
    )
    cross_context, cross_probs, cross_scales = cross_attention(line.tie(cross_q), cross_kv)
    line.mark(cross_context)
    normed2, normed2_low, unit2, spread2 = close_sublayer(
        line.tie(cross_context), weights_kv, 512, 256, normed1, vectors[1], "cross_out"
    )
    line.mark(normed2)
    active, slope, out_low, third, third_low, sums_third = feed_forward(
        order, line.tie(normed2_low), normed2, weights_ffn, up_row, vectors[2], upstream
    )
    line.mark(third)

    straight_order = lax.iota(jnp.int32, groups)

    def send(entries, name, natural=False):
        left, right = entries[0]
        entries = [(line.tie(left), right)] + entries[1:]
        turn = group_order if natural else straight_order
        (sent,) = weight_products(
            turn, entries, 1, None, None, batches // 2, groups, name + "_send"
        )
        return swap(line.mark(sent), "batch", 1)

    def keep(entries, came, parts, name, natural=False):
        left, right = entries[0]
        entries = [(line.tie(left), right)] + entries[1:]
        parts = [(width, nb - 1 - part_order[0]) for width, part_order in parts]
        turn = group_order if natural else straight_order
        outs = weight_products(
            turn, entries, 0, came, parts, batches // 2, groups, name + "_keep"
        )
        line.mark(outs[0])
        return [outs[k : k + 2] for k in range(0, len(outs), 2)]

    def natural_groups(block):
        return jnp.take(block.reshape(-1, groups, block.shape[1] // groups), group_order, axis=1)

    def pack_sums(earlier):
        feature_sums = jnp.concatenate([after(sums_first, earlier), sums_second, sums_third], 0)
        feature_sums = jnp.take(
            feature_sums.reshape(9, batches, features // batches), to_natural, axis=1
        )
        return jnp.concatenate(
            [
                natural_groups(self_sums).reshape(-1),
                natural_groups(rel_sums).reshape(-1),
                natural_groups(cross_sums).reshape(-1),
                natural_groups(up_sums).reshape(-1),
                feature_sums.reshape(-1),
            ]
        )

    down_entries = [(third_low, active)]
    out_low = line.mark(reorder_blocks(line.tie(out_low), to_natural))
    out_low = out_low.reshape(3, share, features)
    layer_out = lax.all_gather(jnp.transpose(out_low, (1, 0, 2)), "head", axis=0, tiled=True)[None]
    down_came = send(down_entries, "down_grad", True)
    upper_low, up_sums, second, second_low, sums_second = feed_forward_back(
        order, line.tie(third_low), third, slope, weights_ffn, unit2, spread2, vectors[1][0:1]
    )
    line.mark(second)
    up_entries = [(normed2_low, upper_low)]
    up_came = send(up_entries, "up_grad", True)
    grad_cross_ctx = project_plain(line.tie(second_low), weights_kv, 512, 256, "cross_ctx_back")
    line.mark(grad_cross_ctx)
    down_halves = keep(down_entries, down_came, [(1024, near)], "down_grad", True)
    up_halves = keep(up_entries, up_came, [(1024, far)], "up_grad", True)
    scatter_ffn = Scatter(line, down_halves + up_halves, (near, far), True)
    grad_cross_q, grad_cross_kv, cross_sums = cross_attention_back(
        cross_q, cross_kv, cross_probs, cross_scales, line.tie(grad_cross_ctx)
    )
    line.mark(grad_cross_q)
    memory_part = rows_back(line.tie(grad_cross_kv), weights_kv, 0, 512, "memory_back")
    span = memory.shape[1]
    line.mark(*memory_part)
    memory_mine, memory_came = memory_part[0], swap(memory_part[1], "head", 1)
    first, first_low, sums_first = cross_query_back(
        line.tie(grad_cross_q), weights_out, 256, 256, second, unit1, spread1, vectors[0][0:1]
    )
    line.mark(first)
    grad_context = project_plain(line.tie(first_low), weights_out, 0, 256, "self_ctx_back")
    line.mark(grad_context)
    layer_out = line.tie(layer_out)
    line.mark(layer_out, grad_context)
    scatter_ffn.step()
    grad_q, grad_kv, grad_rel, self_sums, rel_sums = self_attention_back(
        qk, values, self_probs, self_own, line.tie(grad_context), straight.reshape(-1, 1), share
    )
    line.mark(grad_q)
    scatter_ffn.step()
    memory_mine, memory_came = line.tie(memory_mine), after(memory_came, *line.last)
    pair = (memory_mine.reshape(2, span, features), memory_came.reshape(2, span, features))
    theirs, memory_mine = add_blocks([pair], [([1], [0]), ([0], [0])], BF)
    line.mark(theirs, memory_mine)
    memory_came = swap(theirs, "head", 2)
    cross_entries = [
        (normed1_low, grad_cross_q),
        (memory_all, grad_cross_kv),
        (second_low, cross_context),
        (first_low, context),
    ]
    cross_came = send(cross_entries, "cross_grad")
    self_entries = [(own, grad_q), (extended, grad_kv), (own, grad_rel)]
    self_came = send(self_entries, "self_grad")
    halves = keep(cross_entries, cross_came, [(640, near), (640, far)], "cross_grad")
    scatter_cross = Scatter(line, halves, (near, far))
    halves = keep(self_entries, self_came, [(512, near), (384, far)], "self_grad")
    scatter_self = Scatter(line, halves, (near, far))
    while not hasattr(scatter_ffn, "total"):
        scatter_ffn.step()
    two_grad, one_grad, own_grad = input_back(
        line.tie(grad_q), grad_kv, grad_rel, weights_qk, weights_vr, first
    )
    line.mark(own_grad)
    from_two = lax.ppermute(two_grad, "head", [(i + 2, i) for i in chain[:-2]])
    from_one = lax.ppermute(one_grad, "head", [(i + 1, i) for i in chain[:-1]])
    scatter_ffn.total = line.tie(scatter_ffn.total)
    line.mark(scatter_ffn.total, *line.last)
    scatter_cross.step()
    scatter_self.step()
    packed = line.mark(pack_sums(line.last[0]))
    packed_bits = [("batch", bit) for bit in range(nb)] + [("head", 0), ("head", 1)]

    def add_packed(packed):
        axis_name, bit = packed_bits.pop(0)
        came = swap(packed, axis_name, 1 << bit)
        packed = line.tie(packed)
        return line.mark(packed + after(came, packed))

    own_grad = line.mark(add_halo(line.tie(own_grad), from_one, from_two))
    own_grad = line.mark(reorder_blocks(line.tie(own_grad), to_natural)).reshape(
        3, share, features
    )
    grad_hidden = jnp.transpose(own_grad, (1, 0, 2))[None]
    scatter_cross.step()
    packed = add_packed(packed)
    scatter_self.step()
    packed = add_packed(packed)
    memory_mine, memory_came = line.tie(memory_mine), after(memory_came, *line.last)
    (memory_grad,) = add_blocks([(memory_mine, memory_came)], [([0], [0])], F32)
    memory_grad = line.mark(memory_grad)[0]
    grad_memory = line.mark(reorder_blocks(line.tie(memory_grad), to_natural))[None]
    scatter_cross.step()
    packed = add_packed(packed)
    scatter_self.step()
    packed = add_packed(packed)
    scatter_cross.step()
    scatter_self.step()
    while packed_bits:
        packed = add_packed(packed)
    scatters = (scatter_ffn, scatter_cross, scatter_self)
    for scatter in scatters:
        while not hasattr(scatter, "total"):
            scatter.step()
    grads_ffn, grads_cross, grads_self = [scatter.total for scatter in scatters]

    ends = [0]
    for size in (2 * features, groups * 128, 2 * features, up_bias.shape[0], 9 * features):
        ends.append(ends[-1] + size)
    self_bias_grad = packed[ends[0] : ends[1]].reshape(2, -1)
    relpos_bias_grad = packed[ends[1] : ends[2]]
    cross_bias_grad = packed[ends[2] : ends[3]].reshape(2, -1)
    up_bias_grad = packed[ends[3] : ends[4]]
    feature_sums = packed[ends[4] : ends[5]].reshape(3, 3, features)

    return (
        layer_out,
        grad_hidden,
        grad_memory,
        grads_self[:, 0:768].reshape(blk, 3, 256),
        grads_self[:, 768:896],
        grads_cross[:, 1024:1280],
        grads_cross[:, 0:256],
        grads_cross[:, 256:768].reshape(blk, 2, 256),
        grads_cross[:, 768:1024],
        grads_ffn[:, 1024:],
        grads_ffn[:, 0:1024],
        self_bias_grad,
        relpos_bias_grad,
        cross_bias_grad,
        up_bias_grad,
        feature_sums[:, 0],
        feature_sums[:, 1],
        feature_sums[:, 2],
    )


def solution(mesh):
    in_specs = (
        P("batch", "head", None, None),
        P("batch", "head", None),
        P("batch", None, None, None),
        P("batch", None),
        P("batch", None),
        P(),
        P("batch", None, "head"),
        P("batch", "head"),
        P("batch", "head"),
        P("batch", "head"),
        P("batch", None, "head"),
        P("batch", "head"),
        P("batch", "head"),
        P("batch", "head"),
        P(),
        P(),
        P(),
        P(),
        P(),
        P(),
        P(),
    )
    out_specs = (
        P("batch", None, None, None),
        P("batch", "head", None, None),
        P("batch", "head", None),
        P("batch", None, "head"),
        P("batch", "head"),
        P("batch", "head"),
        P("batch", "head"),
        P("batch", None, "head"),
        P("batch", "head"),
        P("batch", "head"),
        P("batch", "head"),
        P(),
        P(),
        P(),
        P(),
        P(),
        P(),
        P(),
    )
    return jax.shard_map(
        per_device, mesh=mesh, in_specs=in_specs, out_specs=out_specs, check_vma=False
    )
```

```python
import functools

import jax
import jax.numpy as jnp
from jax import lax
from jax.experimental import pallas as pl
from jax.experimental.layout import Layout, with_layout_constraint
from jax.experimental.pallas import tpu as pltpu
from jax.sharding import PartitionSpec as P

BUCKETS = 32
HEAD_DIM = 64
WIDEST_DOC = 256
EPSILON = 1e-05
MASKED = -1e30
BF = jnp.bfloat16
F32 = jnp.float32
VMEM_BYTES = 56 * 1024 * 1024


def params():
    return pltpu.CompilerParams(vmem_limit_bytes=VMEM_BYTES)


def dot(a, b, ca, cb):
    return lax.dot_general(a, b, (((ca,), (cb,)), ((), ())), preferred_element_type=F32)


def whole(shape):
    return pl.BlockSpec(shape, lambda *_: (0,) * len(shape))


def swap(array_in, axis, bit):
    count = lax.axis_size(axis)
    return lax.ppermute(array_in, axis, [(i, i ^ bit) for i in range(count)])


def bits_of(axis):
    return (lax.axis_size(axis) - 1).bit_length()


def after(value, *earlier):
    return lax.optimization_barrier((value,) + earlier)[0]


def pin(value):
    return with_layout_constraint(value, Layout(tuple(range(value.ndim))))


class Line:
    def __init__(self):
        self.last = ()

    def tie(self, value):
        return after(value, *self.last) if self.last else value

    def mark(self, *values):
        self.last = values
        return values[0]


def chunk_of(rows):
    return rows // 4 if rows % 64 == 0 else rows


def stack_rows(*arrays):
    rows = [array.shape[0] for array in arrays]

    def body(*refs):
        at = 0
        for ref, count in zip(refs, rows):
            refs[-1][at : at + count] = ref[...]
            at += count

    return pl.pallas_call(
        body,
        out_shape=jax.ShapeDtypeStruct((sum(rows), arrays[0].shape[1]), arrays[0].dtype),
        compiler_params=params(),
        name="stack_rows",
    )(*arrays)


def add_blocks(parts, outs, dtype):
    rows = parts[0][0].shape[1]
    chunk = chunk_of(rows) if parts[0][0].size >= 1 << 20 else rows
    widths = [mine.shape[2] for mine, _ in parts]

    def body(*refs):
        ins, out_refs = refs[: 2 * len(parts)], refs[2 * len(parts) :]
        for out_ref, (members, chosen) in zip(out_refs, outs):
            at = 0
            for part in chosen:
                mine_ref, came_ref = ins[2 * part], ins[2 * part + 1]
                for place, block in enumerate(members):
                    total = mine_ref[block].astype(F32) + came_ref[block].astype(F32)
                    out_ref[place, :, at : at + widths[part]] = total.astype(dtype)
                at += widths[part]

    def spec(count, width):
        return pl.BlockSpec((count, chunk, width), lambda i: (0, i, 0))

    shapes = [(len(members), sum(widths[part] for part in chosen)) for members, chosen in outs]
    return pl.pallas_call(
        body,
        grid=(rows // chunk,),
        in_specs=[spec(array.shape[0], array.shape[2]) for pair in parts for array in pair],
        out_specs=[spec(*shape) for shape in shapes],
        out_shape=[jax.ShapeDtypeStruct((count, rows, width), dtype) for count, width in shapes],
        compiler_params=params(),
        name="add_blocks",
    )(*[array for pair in parts for array in pair])


def split_sum(mine, came, cuts):
    rows = mine.shape[0]

    def body(mine_ref, came_ref, *out_refs):
        for out_ref, (first, width, copies) in zip(out_refs, cuts):
            for k in range(copies):
                cols = slice(first + k * width, first + (k + 1) * width)
                total = mine_ref[:, cols].astype(F32) + came_ref[:, cols].astype(F32)
                if copies > 1:
                    out_ref[k] = total
                else:
                    out_ref[...] = total

    return pl.pallas_call(
        body,
        out_shape=[
            jax.ShapeDtypeStruct((copies, rows, width) if copies > 1 else (rows, width), F32)
            for _, width, copies in cuts
        ],
        compiler_params=params(),
        name="split_sum",
    )(mine, came)


class Gather:
    def __init__(self, line, shard):
        self.line = line
        self.nb, self.nz = bits_of("batch"), bits_of("head")
        self.buf = pin(shard).reshape((1,) * (self.nb + self.nz) + shard.shape)

    def send(self, axis_name, bit):
        self.axis = self.nb + self.nz - 1 - bit if axis_name == "head" else bit
        self.came = swap(self.line.tie(self.buf), axis_name, 1 << bit)

    def take(self):
        mine = self.line.tie(self.buf)
        self.buf = self.line.mark(jnp.concatenate([mine, after(self.came, mine)], self.axis))

    def columns(self, first, count):
        part = Gather.__new__(Gather)
        part.line, part.nb, part.nz = self.line, self.nb, self.nz
        part.buf = pin(self.buf[..., first : first + count])
        return part

    def close(self):
        shape = (1 << (self.nb - 1), 1 << self.nz) + self.buf.shape[-2:]
        return (self.buf.reshape(shape), self.came.reshape(shape))


class Scatter:
    def __init__(self, line, parts, orders, natural=False, cuts=()):
        self.natural, self.cuts = natural, cuts
        nb, self.nz = bits_of("batch"), bits_of("head")
        self.line = line
        self.groups, self.blk = parts[0][1].shape[1:3]
        self.left = [list(order) for order in orders]
        self.names = [sorted(order) for order in orders]
        self.heads = list(range(self.nz))
        self.mine, self.came = [None] * len(parts), [None] * len(parts)
        for number, (theirs, mine) in enumerate(parts):
            self.send(number, theirs, mine)

    def send(self, number, theirs, mine):
        bit = self.left[number].pop(0)
        self.names[number].remove(bit)
        self.mine[number] = mine
        self.came[number] = swap(theirs, "batch", 1 << bit)

    def step(self):
        tied = [self.line.tie(mine) for mine in self.mine]
        came = [after(came, mine) for came, mine in zip(self.came, tied)]
        pairs = [
            (one.reshape(-1, self.blk, one.shape[-1]), two.reshape(-1, self.blk, one.shape[-1]))
            for one, two in zip(tied, came)
        ]
        blocks = range(pairs[0][0].shape[0])
        everyone = list(range(len(pairs)))
        if self.left[0]:
            outs = []
            for number in everyone:
                place = self.names[number].index(self.left[number][0])
                bit = len(self.names[number]) - 1 - place
                for side in (1, 0):
                    chosen = [k for k in blocks if (k // self.groups >> bit & 1) == side]
                    outs.append((chosen, [number]))
            sums = add_blocks(pairs, outs, BF)
            self.line.mark(*sums)
            for number in everyone:
                self.send(number, sums[2 * number], sums[2 * number + 1])
            return
        if self.natural:
            (total,) = add_blocks(pairs, [(list(blocks), everyone)], BF)
            total = lax.psum_scatter(
                self.line.mark(total), "head", scatter_dimension=0, tiled=False
            )
            self.total = total.astype(F32)
            return
        if not self.heads:
            self.total = split_sum(pairs[0][0][0], pairs[0][1][0], self.cuts)
            self.line.mark(*self.total)
            return
        bit = self.heads.pop(0)
        sides = [[k for k in blocks if (k & 1) == side] for side in (1, 0)]
        theirs, mine = add_blocks(pairs, [(side, everyone) for side in sides], BF)
        self.line.mark(theirs, mine)
        self.mine = [mine]
        self.came = [swap(theirs, "head", 1 << bit)]


def add_halo(own, one, two):
    count = one.shape[0]

    def body(own_ref, one_ref, two_ref, out_ref):
        out_ref[count:] = own_ref[count:]
        came = one_ref[...].astype(F32) + two_ref[...].astype(F32)
        out_ref[0:count] = own_ref[0:count] + came

    return pl.pallas_call(
        body,
        out_shape=jax.ShapeDtypeStruct(own.shape, own.dtype),
        compiler_params=params(),
        name="add_halo",
    )(own, one, two)


def bit_reverse(number, width):
    turned = 0
    for bit in range(width):
        turned |= ((number >> bit) & 1) << (width - 1 - bit)
    return turned


def reorder_blocks(array_in, table, dtype=None):
    count = table.shape[0]
    rows, features = array_in.shape
    blk = features // count
    dtype = dtype or array_in.dtype
    if blk % 128:
        blocks = jnp.take(array_in.reshape(rows, count, blk), table, axis=1)
        return blocks.reshape(rows, features).astype(dtype)

    def body(table_ref, in_ref, out_ref):
        for p in range(count):
            start = pl.multiple_of(table_ref[p] * blk, blk)
            out_ref[:, p * blk : (p + 1) * blk] = in_ref[:, pl.ds(start, blk)].astype(dtype)

    return pl.pallas_call(
        body,
        out_shape=jax.ShapeDtypeStruct(array_in.shape, dtype),
        grid_spec=pltpu.PrefetchScalarGridSpec(
            num_scalar_prefetch=1,
            grid=(1,),
            in_specs=[pl.BlockSpec((rows, features), lambda p, table_ref: (0, 0))],
            out_specs=pl.BlockSpec((rows, features), lambda p, table_ref: (0, 0)),
        ),
        name="reorder",
    )(table, array_in)


def piece_specs(pieces, cols, col_block, step=None):
    count, _, blk, _ = pieces[0].shape
    return [
        pl.BlockSpec((count, 1, blk, cols), lambda j, *c: (0, j, 0, col_block + (c[0] if c else 0)))
        for _ in pieces
    ]


def flat_piece(ref):
    count, _, blk, cols = ref.shape
    return ref[...].reshape(count * blk, cols)


def over_features(x, piece_refs):
    depth = x.shape[1] // len(piece_refs)
    total = None
    for number, ref in enumerate(piece_refs):
        term = dot(x[:, number * depth : (number + 1) * depth], flat_piece(ref), 1, 0)
        total = term if total is None else total + term
    return total


def project(x, pieces, first_col, cols, tile, affine, out_dtype, name):
    rows, features = x.shape
    groups = pieces[0].shape[1]
    per = cols // tile

    def body(x_ref, *refs):
        *piece_refs, affine_ref, out_ref = refs
        acc = over_features(x_ref[...], piece_refs)
        out_ref[...] = ((acc + affine_ref[0:1]) * affine_ref[1:2]).astype(out_ref.dtype)

    return pl.pallas_call(
        body,
        grid=(groups, per),
        in_specs=[whole((rows, features))]
        + piece_specs(pieces, tile, first_col // tile)
        + [pl.BlockSpec((2, tile), lambda j, c: (0, j * per + c))],
        out_specs=pl.BlockSpec((rows, tile), lambda j, c: (0, j * per + c)),
        out_shape=jax.ShapeDtypeStruct((rows, groups * cols), out_dtype),
        compiler_params=params(),
        name=name,
    )(x, *pieces, affine)


def project_plain(x, pieces, first_col, cols, name):
    groups = pieces[0].shape[1]
    affine = jnp.stack([jnp.zeros((groups * cols,), F32), jnp.ones((groups * cols,), F32)])
    return project(x, pieces, first_col, cols, cols, affine, BF, name)


def add_rows(acc_ref, left, piece_refs):
    depth = acc_ref.shape[1] // len(piece_refs)
    for number, ref in enumerate(piece_refs):
        where = slice(number * depth, (number + 1) * depth)
        acc_ref[:, where] += dot(left, flat_piece(ref), 1, 1)


def row_mean(v):
    return jnp.mean(v, -1, keepdims=True)


def column_sum(v):
    return jnp.sum(v, 0, keepdims=True)


def normalize(v):
    centered = v - row_mean(v)
    spread = lax.rsqrt(row_mean(centered * centered) + EPSILON)
    return centered * spread, spread


def normalize_back(upstream, unit, spread, gain):
    a = upstream * gain
    return spread * (a - row_mean(a) - unit * row_mean(a * unit))


def close_sublayer(left, pieces, first_col, cols, residual, vectors, name):
    rows, features = residual.shape
    groups = pieces[0].shape[1]
    count = len(pieces)

    def body(left_ref, *refs):
        piece_refs = refs[:count]
        residual_ref, vectors_ref, normed_ref, low_ref, unit_ref, spread_ref, acc_ref = refs[count:]
        step = pl.program_id(0)

        @pl.when(step == 0)
        def _():
            acc_ref[...] = jnp.zeros_like(acc_ref)

        add_rows(acc_ref, left_ref[...], piece_refs)

        @pl.when(step == groups - 1)
        def _():
            v = residual_ref[...].astype(F32) + (acc_ref[...] + vectors_ref[2:3])
            unit, spread = normalize(v)
            normed = unit * vectors_ref[0:1] + vectors_ref[1:2]
            normed_ref[...] = normed
            low_ref[...] = normed.astype(BF)
            unit_ref[...] = unit
            spread_ref[...] = spread

    return pl.pallas_call(
        body,
        grid=(groups,),
        in_specs=[pl.BlockSpec((rows, cols), lambda j: (0, j))]
        + piece_specs(pieces, cols, first_col // cols)
        + [whole((rows, features)), whole((3, features))],
        out_specs=[whole((rows, features))] * 3 + [whole((rows, 1))],
        out_shape=[
            jax.ShapeDtypeStruct((rows, features), F32),
            jax.ShapeDtypeStruct((rows, features), BF),
            jax.ShapeDtypeStruct((rows, features), F32),
            jax.ShapeDtypeStruct((rows, 1), F32),
        ],
        scratch_shapes=[pltpu.VMEM((rows, features), F32)],
        compiler_params=params(),
        name=name,
    )(left, *pieces, residual, vectors)


def natural_from_exchange(order_ref, first, from_ref, to_ref, blk):
    if blk % 128:
        to_ref[...] = from_ref[...]
        return
    for p in range(from_ref.shape[1] // blk):
        start = pl.multiple_of(order_ref[first + p] * blk, blk)
        to_ref[:, pl.ds(start, blk)] = from_ref[:, p * blk : (p + 1) * blk]


def exchange_from_natural(order_ref, first, from_ref, to_ref, blk):
    if blk % 128:
        to_ref[...] = from_ref[...]
        return
    for p in range(from_ref.shape[1] // blk):
        start = pl.multiple_of(order_ref[first + p] * blk, blk)
        to_ref[:, p * blk : (p + 1) * blk] = from_ref[:, pl.ds(start, blk)]


def norm_back_outputs(upstream, unit, spread, gain, grad_ref, grad_low_ref, sums_ref):
    grad = normalize_back(upstream, unit, spread, gain)
    grad_ref[...] = grad
    grad_low_ref[...] = grad.astype(BF)
    sums_ref[0:1] = column_sum(upstream * unit)
    sums_ref[1:2] = column_sum(upstream)
    sums_ref[2:3] = column_sum(grad)


def held(shape):
    return pl.BlockSpec(shape, lambda *_: (0,) * len(shape), pipeline_mode=pl.Buffered(1))


def feed_forward(
    order, low, normed, weights, up_bias, vectors, grad_out, unit, spread, gain, out_pieces, out_col
):
    rows, features = normed.shape
    batches, groups, blk, both = weights.shape
    cols = both // 2
    width = out_pieces[0].shape[3] - out_col
    count = len(out_pieces)

    def body(order_ref, low_ref, normed_ref, weights_ref, bias_ref, vectors_ref, grad_ref, unit_ref,
             spread_ref, gain_ref, *refs):
        piece_refs = refs[:count]
        (
            active_ref, out_ref, third_low_ref, third_sums_ref, upper_ref, bias_sum_ref,
            second_ref, second_low_ref, second_sums_ref, ctx_ref,
            held_ref, natural_ref, acc_ref, turned_ref, third_ref, slope_ref, sems,
        ) = refs[count:]
        step = pl.program_id(0)

        def copy(j):
            return pltpu.make_async_copy(weights_ref.at[:, j], held_ref.at[j], sems.at[j])

        @pl.when(step == 0)
        def _():
            for j in range(groups):
                copy(j).start()
            natural_from_exchange(order_ref, groups, low_ref, natural_ref, blk)
            acc_ref[...] = jnp.zeros_like(acc_ref)

        for j in range(groups):

            @pl.when(step == j)
            def _():
                copy(j).wait()

        @pl.when(step < groups)
        def _():
            up = held_ref[step, :, :, 0:cols].reshape(features, cols)
            upper = dot(natural_ref[...], up, 1, 0) + bias_ref[...]
            cdf = 0.5 * (1.0 + lax.erf(upper * 0.7071067811865476))
            active = (upper * cdf).astype(BF)
            slope = cdf + upper * jnp.exp(-0.5 * upper * upper) * 0.3989422804014327
            active_ref[...] = active
            slope_ref[step] = slope.astype(BF)
            down = held_ref[step, :, :, cols:].reshape(features, cols)
            acc_ref[...] += dot(active, down, 1, 1)

        @pl.when(step == groups - 1)
        def _():
            exchange_from_natural(order_ref, groups, acc_ref, turned_ref, blk)
            v = normed_ref[...] + (turned_ref[...] + vectors_ref[2:3])
            unit3, spread3 = normalize(v)
            gain3 = vectors_ref[0:1]
            turned_ref[...] = unit3 * gain3 + vectors_ref[1:2]
            natural_from_exchange(order_ref, groups, turned_ref, acc_ref, blk)
            out_ref[...] = acc_ref[...].astype(BF)
            upstream = grad_ref[...]
            third = normalize_back(upstream, unit3, spread3, gain3)
            third_ref[...] = third
            third_low_ref[...] = third.astype(BF)
            third_sums_ref[0:1] = column_sum(upstream * unit3)
            third_sums_ref[1:2] = column_sum(upstream)
            third_sums_ref[2:3] = column_sum(third)
            natural_from_exchange(order_ref, groups, third_low_ref, natural_ref, blk)
            acc_ref[...] = jnp.zeros_like(acc_ref)

        @pl.when((step >= groups) & (step < 2 * groups))
        def _():
            j = step - groups
            down = held_ref[j, :, :, cols:].reshape(features, cols)
            grad_upper = dot(natural_ref[...], down, 1, 0) * slope_ref[j].astype(F32)
            bias_sum_ref[...] = column_sum(grad_upper)
            low = grad_upper.astype(BF)
            upper_ref[...] = low
            up = held_ref[j, :, :, 0:cols].reshape(features, cols)
            acc_ref[...] += dot(low, up, 1, 1)

        @pl.when(step == 2 * groups - 1)
        def _():
            exchange_from_natural(order_ref, groups, acc_ref, turned_ref, blk)
            norm_back_outputs(
                turned_ref[...] + third_ref[...],
                unit_ref[...],
                spread_ref[...],
                gain_ref[...],
                second_ref,
                second_low_ref,
                second_sums_ref,
            )

        @pl.when(step == 2 * groups)
        def _():
            low = second_low_ref[...]
            for j in range(groups):
                total = None
                depth = features // count
                for number, ref in enumerate(piece_refs):
                    piece = ref[:, j].reshape(depth, width)
                    term = dot(low[:, number * depth : (number + 1) * depth], piece, 1, 0)
                    total = term if total is None else total + term
                ctx_ref[:, j * width : (j + 1) * width] = total.astype(BF)

    def forward_block(j, order):
        return (0, jnp.minimum(j, groups - 1))

    def backward_block(j, order):
        return (0, jnp.clip(j - groups, 0, groups - 1))

    piece_rows = out_pieces[0].shape[0]
    return pl.pallas_call(
        body,
        grid_spec=pltpu.PrefetchScalarGridSpec(
            num_scalar_prefetch=1,
            grid=(2 * groups + 1,),
            in_specs=[
                held((rows, features)),
                held((rows, features)),
                pl.BlockSpec(memory_space=pl.ANY),
                pl.BlockSpec((1, cols), forward_block),
                held((3, features)),
                held((rows, features)),
                held((rows, features)),
                held((rows, 1)),
                held((1, features)),
            ]
            + [
                pl.BlockSpec(
                    (piece_rows, groups, blk, width),
                    lambda j, order: (0, 0, 0, out_col // width),
                    pipeline_mode=pl.Buffered(1),
                )
                for _ in out_pieces
            ],
            out_specs=[
                pl.BlockSpec((rows, cols), forward_block),
                whole((rows, features)),
                whole((rows, features)),
                whole((3, features)),
                pl.BlockSpec((rows, cols), backward_block),
                pl.BlockSpec((1, cols), backward_block),
                whole((rows, features)),
                whole((rows, features)),
                whole((3, features)),
                whole((rows, groups * width)),
            ],
            scratch_shapes=[
                pltpu.VMEM((groups, batches, blk, both), BF),
                pltpu.VMEM((rows, features), BF),
                pltpu.VMEM((rows, features), F32),
                pltpu.VMEM((rows, features), F32),
                pltpu.VMEM((rows, features), F32),
                pltpu.VMEM((groups, rows, cols), BF),
                pltpu.SemaphoreType.DMA((groups,)),
            ],
        ),
        out_shape=[
            jax.ShapeDtypeStruct((rows, groups * cols), BF),
            jax.ShapeDtypeStruct((rows, features), BF),
            jax.ShapeDtypeStruct((rows, features), BF),
            jax.ShapeDtypeStruct((3, features), F32),
            jax.ShapeDtypeStruct((rows, groups * cols), BF),
            jax.ShapeDtypeStruct((1, groups * cols), F32),
            jax.ShapeDtypeStruct((rows, features), F32),
            jax.ShapeDtypeStruct((rows, features), BF),
            jax.ShapeDtypeStruct((3, features), F32),
            jax.ShapeDtypeStruct((rows, groups * width), BF),
        ],
        compiler_params=params(),
        name="feed_forward",
    )(order, low, normed, weights, up_bias, vectors, grad_out, unit, spread, gain, *out_pieces)


def cross_query_back(grad_query, pieces, first_col, cols, second, unit, spread, gain):
    rows, features = second.shape
    groups = pieces[0].shape[1]
    count = len(pieces)

    def body(left_ref, *refs):
        piece_refs = refs[:count]
        second_ref, unit_ref, spread_ref, gain_ref, grad_ref, grad_low_ref, sums_ref, acc_ref = refs[
            count:
        ]
        step = pl.program_id(0)

        @pl.when(step == 0)
        def _():
            acc_ref[...] = second_ref[...]

        add_rows(acc_ref, left_ref[...], piece_refs)

        @pl.when(step == groups - 1)
        def _():
            norm_back_outputs(
                acc_ref[...],
                unit_ref[...],
                spread_ref[...],
                gain_ref[...],
                grad_ref,
                grad_low_ref,
                sums_ref,
            )

    return pl.pallas_call(
        body,
        grid=(groups,),
        in_specs=[pl.BlockSpec((rows, cols), lambda j: (0, j))]
        + piece_specs(pieces, cols, first_col // cols)
        + [whole((rows, features)), whole((rows, features)), whole((rows, 1)), whole((1, features))],
        out_specs=[whole((rows, features)), whole((rows, features)), whole((3, features))],
        out_shape=[
            jax.ShapeDtypeStruct((rows, features), F32),
            jax.ShapeDtypeStruct((rows, features), BF),
            jax.ShapeDtypeStruct((3, features), F32),
        ],
        scratch_shapes=[pltpu.VMEM((rows, features), F32)],
        compiler_params=params(),
        name="cross_query_back",
    )(grad_query, *pieces, second, unit, spread, gain)


def rows_back(order, left, pieces, first_col, cols, name):
    rows = left.shape[0]
    count = len(pieces)
    groups = pieces[0].shape[1]
    features = count * pieces[0].shape[0] * pieces[0].shape[2]
    span = rows // groups

    def body(order_ref, left_ref, *refs):
        piece_refs = refs[:count]
        out_ref, acc_ref = refs[count:]
        step = pl.program_id(0)

        @pl.when(step == 0)
        def _():
            acc_ref[...] = jnp.zeros_like(acc_ref)

        add_rows(acc_ref, left_ref[...], piece_refs)

        @pl.when(step == groups - 1)
        def _():
            for k in range(groups):
                start = pl.multiple_of(order_ref[k] * span, span)
                out_ref[pl.ds(start, span)] = acc_ref[k * span : (k + 1) * span].astype(BF)

    piece_count, _, blk, _ = pieces[0].shape
    return pl.pallas_call(
        body,
        grid_spec=pltpu.PrefetchScalarGridSpec(
            num_scalar_prefetch=1,
            grid=(groups,),
            in_specs=[pl.BlockSpec((rows, cols), lambda j, order: (0, j))]
            + [
                pl.BlockSpec(
                    (piece_count, 1, blk, cols), lambda j, order: (0, j, 0, first_col // cols)
                )
                for _ in pieces
            ],
            out_specs=whole((rows, features)),
            scratch_shapes=[pltpu.VMEM((rows, features), F32)],
        ),
        out_shape=jax.ShapeDtypeStruct((rows, features), BF),
        compiler_params=params(),
        name=name,
    )(order, left, *pieces)


def input_back(grad_query, grad_kv, grad_rel, pieces, others, first):
    rows, features = first.shape
    long_rows = grad_kv.shape[0]
    halo = long_rows - rows
    groups = pieces[0].shape[1]
    count = len(pieces)
    width = grad_query.shape[1] // groups
    rel_width = grad_rel.shape[1] // groups

    def body(query_ref, kv_ref, rel_ref, *refs):
        parts = [refs[count * k : count * (k + 1)] for k in range(4)]
        first_ref, two_ref, one_ref, own_ref, acc_ref = refs[4 * count :]
        step = pl.program_id(0)

        @pl.when(step == 0)
        def _():
            acc_ref[0:halo] = jnp.zeros((halo, features), F32)
            acc_ref[halo:] = first_ref[...]

        own_acc = acc_ref.at[halo:]
        add_rows(own_acc, query_ref[...], parts[0])
        add_rows(acc_ref, kv_ref[:, 0:width], parts[1])
        add_rows(acc_ref, kv_ref[:, width : 2 * width], parts[2])
        add_rows(own_acc, rel_ref[...], parts[3])

        @pl.when(step == groups - 1)
        def _():
            two_ref[...] = acc_ref[0 : halo // 2].astype(BF)
            one_ref[...] = acc_ref[halo // 2 : halo].astype(BF)
            own_ref[...] = acc_ref[halo:]

    return pl.pallas_call(
        body,
        grid=(groups,),
        in_specs=[
            pl.BlockSpec((rows, width), lambda j: (0, j)),
            pl.BlockSpec((long_rows, 2 * width), lambda j: (0, j)),
            pl.BlockSpec((rows, rel_width), lambda j: (0, j)),
        ]
        + piece_specs(pieces, width, 0)
        + piece_specs(pieces, width, 1)
        + piece_specs(others, width, 0)
        + piece_specs(others, rel_width, width // rel_width)
        + [whole((rows, features))],
        out_specs=[whole((halo // 2, features))] * 2 + [whole((rows, features))],
        out_shape=[
            jax.ShapeDtypeStruct((halo // 2, features), BF),
            jax.ShapeDtypeStruct((halo // 2, features), BF),
            jax.ShapeDtypeStruct((rows, features), F32),
        ],
        scratch_shapes=[pltpu.VMEM((long_rows, features), F32)],
        compiler_params=params(),
        name="input_back",
    )(grad_query, grad_kv, grad_rel, *pieces, *pieces, *others, *others, first)


def weight_products(order, entries, half, extra, parts, pieces, groups, name):
    features = entries[0][0].shape[1]
    depth = features // 2
    blk = depth // pieces
    widths = [right.shape[1] // groups for _, right in entries]
    total = sum(widths)
    count = len(entries)
    outs = []
    if parts is None:
        outs.append((0, total, list(range(pieces))))
    else:
        at = 0
        for width, bit in parts:
            for side in (1, 0):
                outs.append((at, width, [p for p in range(pieces) if (p >> bit & 1) == side]))
            at += width

    def body(order_ref, *refs):
        lefts, rights = refs[:count], refs[count : 2 * count]
        out_refs = refs[len(refs) - len(outs) :]
        at = 0
        for left_ref, right_ref, width in zip(lefts, rights, widths):
            term = dot(left_ref[...], right_ref[...], 0, 0).reshape(pieces, blk, width)
            if extra is not None:
                term = term + refs[2 * count][:, 0, :, at : at + width].astype(F32)
            term = term.astype(BF)
            for out_ref, (first, size, members) in zip(out_refs, outs):
                low, high = max(at, first), min(at + width, first + size)
                if low >= high:
                    continue
                for place, piece in enumerate(members):
                    out_ref[place, 0, :, low - first : high - first] = term[
                        piece, :, low - at : high - at
                    ]
            at += width

    def block(number, width):
        return pl.BlockSpec((number, 1, blk, width), lambda j, order: (0, j, 0, 0))

    in_specs = [
        pl.BlockSpec((left.shape[0], depth), lambda j, order: (0, half)) for left, _ in entries
    ]
    in_specs += [
        pl.BlockSpec((right.shape[0], width), lambda j, order: (0, order[j]))
        for (_, right), width in zip(entries, widths)
    ]
    operands = [left for left, _ in entries] + [right for _, right in entries]
    if extra is not None:
        in_specs.append(block(pieces, total))
        operands.append(extra)
    return pl.pallas_call(
        body,
        grid_spec=pltpu.PrefetchScalarGridSpec(
            num_scalar_prefetch=1,
            grid=(groups,),
            in_specs=in_specs,
            out_specs=[block(len(members), width) for _, width, members in outs],
        ),
        out_shape=[
            jax.ShapeDtypeStruct((len(members), groups, blk, width), BF)
            for _, width, members in outs
        ],
        compiler_params=params(),
        name=name,
    )(order, *operands)


def half_masks(rows):
    lane = lax.broadcasted_iota(jnp.int32, (rows, 128), 1)
    return [
        jnp.where((lane >= 64 * half) & (lane < 64 * half + 64), 1.0, 0.0).astype(F32)
        for half in range(2)
    ]


def lanes_and_rows(share):
    lane = lax.broadcasted_iota(jnp.int32, (share, share), 1)
    row = lax.broadcasted_iota(jnp.int32, (share, share), 0)
    return lane > row


def turn_right(block):
    return pltpu.roll(block, 1, 1, stride=1, stride_axis=0)


def skew(distance, later):
    share = later.shape[0]
    tracks = []
    for n in range(distance.shape[0] // share):
        rows = slice(n * share, (n + 1) * share)
        far, near = turn_right(distance[rows, 0:share]), turn_right(distance[rows, share:])
        tracks.append(jnp.concatenate([far, jnp.where(later, near, far), near], 1))
    return jnp.concatenate(tracks, 0)


def unskew_sources(grid, later):
    share = later.shape[0]
    tracks = []
    for n in range(grid.shape[0] // share):
        old, mid, new = [
            grid[n * share : (n + 1) * share, c * share : (c + 1) * share] for c in range(3)
        ]
        tracks.append(jnp.concatenate([jnp.where(later, old, mid), jnp.where(later, mid, new)], 1))
    return jnp.concatenate(tracks, 0)


def turn_blocks(array_in, share):
    rows = array_in.shape[0]
    return jnp.concatenate(
        [
            jnp.concatenate(
                [turn_right(array_in[r : r + share, c : c + share]) for c in (0, share)], 1
            )
            for r in range(0, rows, share)
        ],
        0,
    )


def self_attention(qk, values, relpos, mask, turned, share):
    rows, window = 3 * share, 3 * share
    groups = values.shape[1] // 256
    long_rows = qk.shape[0]
    halo = long_rows - rows

    def body(q_ref, k_ref, v_ref, rel_ref, mask_ref, turned_ref, ctx_ref, raised_ref, own_ref):
        halves = half_masks(rows)
        later = lanes_and_rows(share)
        lane = lax.broadcasted_iota(jnp.int32, (rows, 128), 1)
        rel = rel_ref[...]
        high = rel.astype(BF)
        split = jnp.concatenate([high, (rel - high.astype(F32)).astype(BF)], 1)
        row_id = lax.broadcasted_iota(jnp.int32, (256, 2 * share), 0) & 127
        track = lax.broadcasted_iota(jnp.int32, (rows, 1), 0) >= share
        own_all = jnp.zeros((rows, 128), F32)
        for pair in range(2):
            cols = slice(128 * pair, 128 * pair + 128)
            q = q_ref[halo:, cols]
            k, v = k_ref[0:window, cols], v_ref[0:window, cols]
            own_k = k_ref[halo:, cols].astype(F32)
            own_v = v_ref[halo:, cols].astype(F32)
            product = q.astype(F32) * own_k
            mixed = jnp.zeros((rows, 128), F32)
            for half in range(2):
                head = 2 * pair + half
                scores = dot(q * halves[half].astype(BF), k, 1, 1)
                table = jnp.where(row_id == turned_ref[...] + 32 * head, 1.0, 0.0).astype(BF)
                scores = scores + skew(dot(split, table, 1, 0), later) + mask_ref[...]
                own = jnp.sum(
                    product * halves[half] + jnp.where(lane == 32 * head, rel, 0.0), -1, keepdims=True
                )
                own = jnp.where(track, own, MASKED)
                top = jnp.maximum(jnp.max(scores, -1, keepdims=True), own)
                raised = jnp.exp(scores - top)
                own_raised = jnp.exp(own - top)
                scale = 1.0 / (jnp.sum(raised, -1, keepdims=True) + own_raised)
                raised = raised.astype(BF)
                raised_ref[head] = raised
                own_all = jnp.where(lane == head, own_raised, own_all)
                own_all = jnp.where(lane == head + 4, scale, own_all)
                mixed = mixed + (dot(raised, v, 1, 0) + own_raised * own_v) * (scale * halves[half])
            ctx_ref[:, cols] = mixed.astype(BF)
        own_ref[...] = own_all

    return pl.pallas_call(
        body,
        grid=(groups,),
        in_specs=[
            pl.BlockSpec((long_rows, 256), lambda j: (0, 2 * j)),
            pl.BlockSpec((long_rows, 256), lambda j: (0, 2 * j + 1)),
            pl.BlockSpec((long_rows, 256), lambda j: (0, j)),
            pl.BlockSpec((rows, 128), lambda j: (0, j)),
            whole((rows, window)),
            whole((1, 2 * share)),
        ],
        out_specs=[
            pl.BlockSpec((rows, 256), lambda j: (0, j)),
            pl.BlockSpec((4, rows, window), lambda j: (j, 0, 0)),
            pl.BlockSpec((rows, 128), lambda j: (0, j)),
        ],
        out_shape=[
            jax.ShapeDtypeStruct((rows, groups * 256), BF),
            jax.ShapeDtypeStruct((4 * groups, rows, window), BF),
            jax.ShapeDtypeStruct((rows, groups * 128), F32),
        ],
        compiler_params=params(),
        name="self_attention",
    )(qk, qk, values, relpos, mask, turned)


def self_attention_back(qk, values, raised, own_raised, grad_ctx, straight, share):
    rows, window = 3 * share, 3 * share
    groups = values.shape[1] // 256
    long_rows = qk.shape[0]
    halo = long_rows - rows

    def body(
        q_ref, k_ref, v_ref, raised_ref, own_ref, grad_ref, straight_ref,
        gq_ref, gkv_ref, grel_ref, sums_ref, rel_sums_ref,
    ):
        halves = half_masks(rows)
        later = lanes_and_rows(share)
        lane = lax.broadcasted_iota(jnp.int32, (rows, 128), 1)
        turn = jnp.where(
            lax.broadcasted_iota(jnp.int32, (2 * share, 2 * share), 0)
            + lax.broadcasted_iota(jnp.int32, (2 * share, 2 * share), 1)
            == 2 * share - 1,
            1.0,
            0.0,
        ).astype(BF)
        column = lax.broadcasted_iota(jnp.int32, (2 * share, 128), 1)
        grel = jnp.zeros((rows, 128), F32)
        own_all = own_ref[...]

        def pick(number):
            return jnp.sum(jnp.where(lane == number, own_all, 0.0), -1, keepdims=True)

        for pair in range(2):
            cols = slice(128 * pair, 128 * pair + 128)
            q = q_ref[halo:, cols]
            k, v = k_ref[0:window, cols], v_ref[0:window, cols]
            own_k = k_ref[halo:, cols].astype(F32)
            own_v = v_ref[halo:, cols].astype(F32)
            scales = [pick(2 * pair + half + 4) for half in range(2)]
            grad_wide = grad_ref[:, cols].astype(F32)
            grad_wide = grad_wide * (scales[0] * halves[0] + scales[1] * halves[1])
            grad = grad_wide.astype(BF)
            own_product = grad_wide * own_v
            gq = jnp.zeros((rows, 128), F32)
            own_spread = jnp.zeros((rows, 128), F32)
            own_weight = jnp.zeros((rows, 128), F32)
            score_parts, prob_parts, q_parts, g_parts = [], [], [], []
            for half in range(2):
                head = 2 * pair + half
                low_half = halves[half].astype(BF)
                p = raised_ref[head]
                p_wide = p.astype(F32)
                grad_half = grad * low_half
                grad_probs = dot(grad_half, v, 1, 1)
                own_p = pick(head)
                own_grad = jnp.sum(own_product * halves[half], -1, keepdims=True)
                row_dot = jnp.sum(p_wide * grad_probs, -1, keepdims=True) + own_p * own_grad
                row_dot = row_dot * scales[half]
                grad_scores = p_wide * (grad_probs - row_dot)
                source = unskew_sources(grad_scores, later).astype(BF)
                grad_scores = grad_scores.astype(BF)
                grad_own = (own_p * (own_grad - row_dot)).astype(BF).astype(F32)
                gq = gq + (dot(grad_scores, k, 1, 0) + grad_own * own_k) * halves[half]
                own_spread = own_spread + grad_own * halves[half]
                own_weight = own_weight + own_p * halves[half]
                score_parts.append(grad_scores)
                prob_parts.append(p)
                q_parts.append(q * low_half)
                g_parts.append(grad_half)
                turned = turn_blocks(dot(source, turn, 1, 0), share).astype(BF)
                table = jnp.where(column == straight_ref[...] + 32 * head, 1.0, 0.0).astype(BF)
                grel = grel + dot(turned, table, 1, 0) + jnp.where(lane == 32 * head, grad_own, 0.0)
            gk = dot(
                jnp.concatenate(q_parts, 0), jnp.concatenate(score_parts, 0), 0, 0
            ).T
            gv = dot(
                jnp.concatenate(g_parts, 0), jnp.concatenate(prob_parts, 0), 0, 0
            ).T
            gq = gq * 0.125
            gq_ref[:, cols] = gq.astype(BF)
            own_gk = own_spread * q.astype(F32)
            own_gv = own_weight * grad_wide
            vcols = slice(256 + 128 * pair, 256 + 128 * pair + 128)
            gkv_ref[0:window, cols] = gk.astype(BF)
            gkv_ref[0:window, vcols] = gv.astype(BF)
            gkv_ref[window:, cols] = own_gk[share:].astype(BF)
            gkv_ref[window:, vcols] = own_gv[share:].astype(BF)
            sums_ref[0:1, cols] = column_sum(gq)
            sums_ref[1:2, cols] = column_sum(gv) + column_sum(own_gv[share:])
        grel_ref[...] = grel.astype(BF)
        rel_sums_ref[...] = column_sum(grel)

    return pl.pallas_call(
        body,
        grid=(groups,),
        in_specs=[
            pl.BlockSpec((long_rows, 256), lambda j: (0, 2 * j)),
            pl.BlockSpec((long_rows, 256), lambda j: (0, 2 * j + 1)),
            pl.BlockSpec((long_rows, 256), lambda j: (0, j)),
            pl.BlockSpec((4, rows, window), lambda j: (j, 0, 0)),
            pl.BlockSpec((rows, 128), lambda j: (0, j)),
            pl.BlockSpec((rows, 256), lambda j: (0, j)),
            whole((2 * share, 1)),
        ],
        out_specs=[
            pl.BlockSpec((rows, 256), lambda j: (0, j)),
            pl.BlockSpec((long_rows, 512), lambda j: (0, j)),
            pl.BlockSpec((rows, 128), lambda j: (0, j)),
            pl.BlockSpec((2, 256), lambda j: (0, j)),
            pl.BlockSpec((1, 128), lambda j: (0, j)),
        ],
        out_shape=[
            jax.ShapeDtypeStruct((rows, groups * 256), BF),
            jax.ShapeDtypeStruct((long_rows, groups * 512), BF),
            jax.ShapeDtypeStruct((rows, groups * 128), BF),
            jax.ShapeDtypeStruct((2, groups * 256), F32),
            jax.ShapeDtypeStruct((1, groups * 128), F32),
        ],
        compiler_params=params(),
        name="self_attention_back",
    )(qk, qk, values, raised, own_raised, grad_ctx, straight)


def cross_attention(queries, kv):
    rows, places = queries.shape[0], kv.shape[0]
    groups = queries.shape[1] // 256

    def body(q_ref, k_ref, v_ref, ctx_ref, raised_ref, scale_ref):
        halves = half_masks(rows)
        lane = lax.broadcasted_iota(jnp.int32, (rows, 128), 1)
        scales = jnp.zeros((rows, 128), F32)
        for pair in range(2):
            cols = slice(128 * pair, 128 * pair + 128)
            q, k, v = q_ref[:, cols], k_ref[:, cols], v_ref[:, cols]
            mixed = jnp.zeros((rows, 128), F32)
            for half in range(2):
                head = 2 * pair + half
                scores = dot(q * halves[half].astype(BF), k, 1, 1)
                raised = jnp.exp(scores - jnp.max(scores, -1, keepdims=True))
                scale = 1.0 / jnp.sum(raised, -1, keepdims=True)
                raised = raised.astype(BF)
                raised_ref[head] = raised
                scales = jnp.where(lane == head, scale, scales)
                mixed = mixed + dot(raised, v, 1, 0) * (scale * halves[half])
            ctx_ref[:, cols] = mixed.astype(BF)
        scale_ref[...] = scales

    return pl.pallas_call(
        body,
        grid=(groups,),
        in_specs=[
            pl.BlockSpec((rows, 256), lambda j: (0, j)),
            pl.BlockSpec((places, 256), lambda j: (0, 2 * j)),
            pl.BlockSpec((places, 256), lambda j: (0, 2 * j + 1)),
        ],
        out_specs=[
            pl.BlockSpec((rows, 256), lambda j: (0, j)),
            pl.BlockSpec((4, rows, places), lambda j: (j, 0, 0)),
            pl.BlockSpec((rows, 128), lambda j: (0, j)),
        ],
        out_shape=[
            jax.ShapeDtypeStruct((rows, groups * 256), BF),
            jax.ShapeDtypeStruct((4 * groups, rows, places), BF),
            jax.ShapeDtypeStruct((rows, groups * 128), F32),
        ],
        compiler_params=params(),
        name="cross_attention",
    )(queries, kv, kv)


def cross_attention_back(queries, kv, raised, scales, grad_ctx):
    rows, places = queries.shape[0], kv.shape[0]
    groups = queries.shape[1] // 256

    def body(q_ref, k_ref, v_ref, raised_ref, scale_ref, grad_ref, gq_ref, gkv_ref, sums_ref):
        halves = half_masks(rows)
        lane = lax.broadcasted_iota(jnp.int32, (rows, 128), 1)
        scale_all = scale_ref[...]
        for pair in range(2):
            cols = slice(128 * pair, 128 * pair + 128)
            q, k, v = q_ref[:, cols], k_ref[:, cols], v_ref[:, cols]
            scale = [
                jnp.sum(jnp.where(lane == 2 * pair + half, scale_all, 0.0), -1, keepdims=True)
                for half in range(2)
            ]
            grad = grad_ref[:, cols].astype(F32) * (scale[0] * halves[0] + scale[1] * halves[1])
            grad = grad.astype(BF)
            gq = jnp.zeros((rows, 128), F32)
            score_parts, prob_parts, q_parts, g_parts = [], [], [], []
            for half in range(2):
                low_half = halves[half].astype(BF)
                p = raised_ref[2 * pair + half]
                p_wide = p.astype(F32)
                grad_half = grad * low_half
                grad_probs = dot(grad_half, v, 1, 1)
                row_dot = jnp.sum(p_wide * grad_probs, -1, keepdims=True) * scale[half]
                grad_scores = (p_wide * (grad_probs - row_dot)).astype(BF)
                gq = gq + dot(grad_scores, k, 1, 0) * halves[half]
                score_parts.append(grad_scores)
                prob_parts.append(p)
                q_parts.append(q * low_half)
                g_parts.append(grad_half)
            gk = dot(
                jnp.concatenate(q_parts, 0), jnp.concatenate(score_parts, 0), 0, 0
            ).T
            gv = dot(
                jnp.concatenate(g_parts, 0), jnp.concatenate(prob_parts, 0), 0, 0
            ).T
            gq = gq * 0.125
            gq_ref[:, cols] = gq.astype(BF)
            vcols = slice(256 + 128 * pair, 256 + 128 * pair + 128)
            gkv_ref[:, cols] = gk.astype(BF)
            gkv_ref[:, vcols] = gv.astype(BF)
            sums_ref[0:1, cols] = column_sum(gq)
            sums_ref[1:2, cols] = column_sum(gv)

    return pl.pallas_call(
        body,
        grid=(groups,),
        in_specs=[
            pl.BlockSpec((rows, 256), lambda j: (0, j)),
            pl.BlockSpec((places, 256), lambda j: (0, 2 * j)),
            pl.BlockSpec((places, 256), lambda j: (0, 2 * j + 1)),
            pl.BlockSpec((4, rows, places), lambda j: (j, 0, 0)),
            pl.BlockSpec((rows, 128), lambda j: (0, j)),
            pl.BlockSpec((rows, 256), lambda j: (0, j)),
        ],
        out_specs=[
            pl.BlockSpec((rows, 256), lambda j: (0, j)),
            pl.BlockSpec((places, 512), lambda j: (0, j)),
            pl.BlockSpec((2, 256), lambda j: (0, j)),
        ],
        out_shape=[
            jax.ShapeDtypeStruct((rows, groups * 256), BF),
            jax.ShapeDtypeStruct((places, groups * 512), BF),
            jax.ShapeDtypeStruct((2, groups * 256), F32),
        ],
        compiler_params=params(),
        name="cross_attention_back",
    )(queries, kv, kv, raised, scales, grad_ctx)


def per_device(
    hidden,
    memory,
    grad_out,
    lengths,
    key_mask,
    buckets,
    self_weight,
    relpos_weight,
    selfout_weight,
    crossq_weight,
    crosskv_weight,
    crossout_weight,
    up_weight,
    down_weight,
    self_bias,
    relpos_bias,
    cross_bias,
    up_bias,
    norm_gain,
    norm_bias,
    out_bias,
):
    batches, groups = lax.axis_size("batch"), lax.axis_size("head")
    b, z = lax.axis_index("batch"), lax.axis_index("head")
    nb = bits_of("batch")
    share, features = hidden.shape[1], hidden.shape[3]
    length = share * groups
    rows, window = 3 * share, 3 * share
    assert share == 128 and hidden.shape[0] == 1 and WIDEST_DOC <= 2 * share
    assert batches == 1 << nb and features % batches == 0 and groups == 4
    near, far = list(range(1, nb)), list(reversed(range(1, nb)))

    turned_ids = jnp.array([bit_reverse(p, nb) for p in range(batches)], jnp.int32)
    to_exchange = b ^ turned_ids
    natural = lax.iota(jnp.int32, batches) ^ b
    to_natural = jnp.zeros_like(natural)
    for bit in range(nb):
        to_natural = to_natural | (((natural >> bit) & 1) << (nb - 1 - bit))
    group_order = z ^ lax.iota(jnp.int32, groups)

    def small_features(stack):
        count = stack.shape[0]
        blocks = stack.reshape(count, batches, features // batches)
        return jnp.take(blocks, to_exchange, axis=1).reshape(count, features)

    blk = self_weight.shape[0]
    assert nb >= 2 and bits_of("head") == 2
    line = Line()
    self_shard = jnp.concatenate([self_weight.reshape(blk, -1), relpos_weight], 1).astype(BF)
    gather_self = Gather(line, line.mark(pin(self_shard)))
    gather_self.send("head", 1)
    ffn_shard = line.mark(
        pin(jnp.concatenate([line.tie(up_weight), down_weight], 1).astype(BF))
    )
    gather_ffn = Gather(line, ffn_shard)

    columns = jnp.concatenate(
        [
            self_bias[0].reshape(groups, -1),
            self_bias[1].reshape(groups, -1),
            cross_bias[0].reshape(groups, -1),
            cross_bias[1].reshape(groups, -1),
            relpos_bias.reshape(groups, -1),
            up_bias.reshape(groups, -1),
        ],
        1,
    )
    columns = jnp.take(columns, group_order, axis=0)
    query_bias, value_bias = columns[:, 0:256], columns[:, 256:512]
    cross_query_bias, cross_value_bias = columns[:, 512:768], columns[:, 768:1024]
    rel_row = columns[:, 1024:1152].reshape(1, -1)
    up_row = columns[:, 1152:].reshape(1, -1)

    memory_own = line.mark(reorder_blocks(line.tie(memory[0]), to_exchange))
    own = jnp.transpose(line.tie(hidden[0]), (1, 0, 2)).reshape(rows, features)
    own = line.mark(reorder_blocks(own, to_exchange))
    upstream = lax.dynamic_slice_in_dim(line.tie(grad_out[0]), z * share, share, 0)
    upstream = jnp.transpose(upstream, (1, 0, 2)).reshape(rows, features)
    upstream = line.mark(reorder_blocks(upstream, to_exchange))
    chain = list(range(groups))

    vectors = small_features(jnp.concatenate([norm_gain, norm_bias, out_bias], 0))
    vectors = vectors.reshape(3, 3, features).transpose(1, 0, 2)
    none = jnp.zeros((groups, 256), F32)

    def affine(bias, scale):
        return jnp.stack([bias, jnp.full(bias.shape, scale, F32)])

    scales = jnp.concatenate([none + 0.125, none + 1.0], 1).reshape(-1)
    qk_affine = jnp.stack([jnp.concatenate([query_bias, none], 1).reshape(-1), scales])
    value_affine = affine(value_bias.reshape(-1), 1.0)
    rel_affine = affine(rel_row[0], 1.0)
    cross_query_affine = affine(cross_query_bias.reshape(-1), 0.125)
    cross_kv_affine = affine(jnp.concatenate([none, cross_value_bias], 1).reshape(-1), 1.0)

    places = lax.iota(jnp.int32, length)
    doc_ends = jnp.cumsum(lengths[0])
    segment = jnp.sum((places[:, None] >= doc_ends[None, :]).astype(jnp.int32), -1)
    lead = window - share
    padded_segment = jnp.concatenate([jnp.full((lead,), -1, jnp.int32), segment])
    padded_mask = jnp.concatenate([jnp.zeros((lead,), jnp.int32), key_mask[0]])
    key_segment = lax.dynamic_slice_in_dim(padded_segment, z * share, window)
    key_open = lax.dynamic_slice_in_dim(padded_mask, z * share, window)
    query_segment = lax.dynamic_slice_in_dim(segment, z * share, share)
    query_at = lax.iota(jnp.int32, share)[:, None] + lead
    key_at = lax.iota(jnp.int32, window)[None, :]
    joined = (query_segment[:, None] == key_segment[None, :]) & (
        (key_open[None, :] == 1) | (query_at == key_at)
    )
    allowed_main = joined & (key_at <= query_at)
    allowed_pred = joined & (key_at < query_at)
    mask = jnp.where(jnp.stack([allowed_main, allowed_pred, allowed_pred]), 0.0, MASKED)
    mask = mask.reshape(rows, window).astype(F32)
    straight = buckets[0 : 2 * share]
    turned = straight[::-1]

    mask = line.mark(line.tie(mask))
    assert nb >= 2 and bits_of("head") == 2
    gather_cross = Gather(
        line,
        jnp.concatenate(
            [selfout_weight, crossq_weight, crosskv_weight.reshape(blk, -1), crossout_weight], 1
        ).astype(BF),
    )
    gather_self.take()
    gather_self.send("head", 0)
    gather_ffn.send("head", 1)
    gather_self.take()
    parts_self = [gather_self.columns(0, 512), gather_self.columns(512, 384)]
    orders_self = [near, far]
    for part, part_order in zip(parts_self, orders_self):
        part.send("batch", part_order[0])
    gather_ffn.take()
    gather_ffn.send("head", 0)
    for number in range(1, nb - 1):
        for part, part_order in zip(parts_self, orders_self):
            part.take()
            part.send("batch", part_order[number])
    gather_cross.send("head", 1)
    gather_ffn.take()
    for part in parts_self:
        part.take()
        part.send("batch", 0)
    gather_cross.take()
    gather_cross.send("head", 0)
    main = line.tie(own[0:share])
    before_one = lax.ppermute(main, "head", [(i, i + 1) for i in chain[:-1]])
    before_two = lax.ppermute(main, "head", [(i, i + 2) for i in chain[:-2]])
    gather_cross.take()
    parts_cross = [gather_cross.columns(0, 512), gather_cross.columns(512, 768)]
    orders_cross = [far, near]
    for part, part_order in zip(parts_cross, orders_cross):
        part.send("batch", part_order[0])
    extended = line.mark(stack_rows(before_two, before_one, line.tie(own)))
    memory_came = swap(line.tie(memory_own), "head", 2)
    weights_qk, weights_vr = [part.close() for part in parts_self]

    order = jnp.concatenate([group_order, to_exchange]).astype(jnp.int32)
    values = line.mark(
        project(line.tie(extended), weights_vr, 0, 256, 256, value_affine, BF, "self_v")
    )
    relpos = line.mark(
        project(line.tie(own), weights_vr, 256, 128, 128, rel_affine, F32, "self_rel")
    )
    for number in range(1, nb - 1):
        for part, part_order in zip(parts_cross, orders_cross):
            part.take()
            part.send("batch", part_order[number])
    weights_ffn = line.tie(gather_ffn.buf).reshape((groups,) + ffn_shard.shape)
    weights_ffn = lax.all_gather(weights_ffn, "batch", axis=0)
    if blk % 128:
        weights_ffn = jnp.take(weights_ffn, to_exchange, axis=0)
    qk = line.mark(project(line.tie(extended), weights_qk, 0, 512, 512, qk_affine, BF, "self_qk"))
    memory_half = line.mark(jnp.concatenate([line.tie(memory_own), memory_came], 0))
    memory_came = swap(memory_half, "head", 1)
    context, self_probs, self_own = self_attention(
        line.tie(qk), values, relpos, mask, turned.reshape(1, -1), share
    )
    line.mark(context)
    for part in parts_cross:
        part.take()
        part.send("batch", 0)
    weights_out, weights_kv = [part.close() for part in parts_cross]
    normed1, normed1_low, unit1, spread1 = close_sublayer(
        line.tie(context), weights_out, 0, 256, own, vectors[0], "self_out"
    )
    line.mark(normed1)
    cross_q = line.mark(
        project(
            line.tie(normed1_low), weights_out, 256, 256, 256, cross_query_affine, BF, "cross_q"
        )
    )
    memory_all = line.mark(jnp.concatenate([line.tie(memory_half), memory_came], 0))
    cross_kv = line.mark(
        project(line.tie(memory_all), weights_kv, 0, 512, 512, cross_kv_affine, BF, "cross_kv")
    )
    cross_context, cross_probs, cross_scales = cross_attention(line.tie(cross_q), cross_kv)
    line.mark(cross_context)
    normed2, normed2_low, unit2, spread2 = close_sublayer(
        line.tie(cross_context), weights_kv, 512, 256, normed1, vectors[1], "cross_out"
    )
    line.mark(normed2)
    (
        active, out_low, third_low, sums_third, upper_low, up_sums,
        second, second_low, sums_second, grad_cross_ctx,
    ) = feed_forward(
        order, line.tie(normed2_low), normed2, weights_ffn, up_row, vectors[2], upstream,
        unit2, spread2, vectors[1][0:1], weights_kv, 512,
    )
    line.mark(second)

    straight_order = lax.iota(jnp.int32, groups)

    def send(entries, name, natural=False):
        left, right = entries[0]
        entries = [(line.tie(left), right)] + entries[1:]
        turn = group_order if natural else straight_order
        (sent,) = weight_products(
            turn, entries, 1, None, None, batches // 2, groups, name + "_send"
        )
        return swap(line.mark(sent), "batch", 1)

    def keep(entries, came, parts, name, natural=False):
        left, right = entries[0]
        entries = [(line.tie(left), right)] + entries[1:]
        parts = [(width, nb - 1 - part_order[0]) for width, part_order in parts]
        turn = group_order if natural else straight_order
        outs = weight_products(
            turn, entries, 0, came, parts, batches // 2, groups, name + "_keep"
        )
        line.mark(outs[0])
        return [outs[k : k + 2] for k in range(0, len(outs), 2)]

    def natural_groups(block):
        return jnp.take(block.reshape(-1, groups, block.shape[1] // groups), group_order, axis=1)

    def pack_sums(earlier):
        feature_sums = jnp.concatenate([after(sums_first, earlier), sums_second, sums_third], 0)
        feature_sums = jnp.take(
            feature_sums.reshape(9, batches, features // batches), to_natural, axis=1
        )
        return jnp.concatenate(
            [
                natural_groups(self_sums).reshape(-1),
                natural_groups(rel_sums).reshape(-1),
                natural_groups(cross_sums).reshape(-1),
                natural_groups(up_sums).reshape(-1),
                feature_sums.reshape(-1),
            ]
        )

    down_entries = [(third_low, active)]
    if blk % 128:
        out_low = reorder_blocks(out_low, to_natural)
    out_low = out_low.reshape(3, share, features)
    layer_out = lax.all_gather(jnp.transpose(out_low, (1, 0, 2)), "head", axis=0, tiled=True)[None]
    down_entries = [(third_low, active)]
    down_came = send(down_entries, "down_grad", True)
    up_entries = [(normed2_low, upper_low)]
    up_came = send(up_entries, "up_grad", True)
    down_halves = keep(down_entries, down_came, [(1024, near)], "down_grad", True)
    up_halves = keep(up_entries, up_came, [(1024, far)], "up_grad", True)
    scatter_ffn = Scatter(line, down_halves + up_halves, (near, far), True)
    grad_cross_q, grad_cross_kv, cross_sums = cross_attention_back(
        cross_q, cross_kv, cross_probs, cross_scales, line.tie(grad_cross_ctx)
    )
    line.mark(grad_cross_q)
    first, first_low, sums_first = cross_query_back(
        line.tie(grad_cross_q), weights_out, 256, 256, second, unit1, spread1, vectors[0][0:1]
    )
    line.mark(first)
    grad_context = project_plain(line.tie(first_low), weights_out, 0, 256, "self_ctx_back")
    line.mark(grad_context)
    scatter_ffn.step()
    grad_q, grad_kv, grad_rel, self_sums, rel_sums = self_attention_back(
        qk, values, self_probs, self_own, line.tie(grad_context), straight.reshape(-1, 1), share
    )
    line.mark(grad_q)
    scatter_ffn.step()
    layer_out = line.tie(layer_out)
    line.mark(layer_out, *line.last)
    memory_order = z ^ jnp.array([0, 2, 1, 3], jnp.int32)
    memory_part = rows_back(
        memory_order, line.tie(grad_cross_kv), weights_kv, 0, 512, "memory_back"
    )
    memory_grad = lax.psum_scatter(
        line.mark(memory_part), "head", scatter_dimension=0, tiled=True
    )
    cross_entries = [
        (normed1_low, grad_cross_q),
        (memory_all, grad_cross_kv),
        (second_low, cross_context),
        (first_low, context),
    ]
    cross_came = send(cross_entries, "cross_grad")
    self_entries = [(own, grad_q), (extended, grad_kv), (own, grad_rel)]
    self_came = send(self_entries, "self_grad")
    halves = keep(cross_entries, cross_came, [(640, near), (640, far)], "cross_grad")
    cross_cuts = ((0, 256, 1), (256, 512, 1), (768, 256, 1), (1024, 256, 1))
    scatter_cross = Scatter(line, halves, (near, far), cuts=cross_cuts)
    halves = keep(self_entries, self_came, [(512, near), (384, far)], "self_grad")
    scatter_self = Scatter(line, halves, (near, far), cuts=((0, 256, 3), (768, 128, 1)))
    while not hasattr(scatter_ffn, "total"):
        scatter_ffn.step()
    two_grad, one_grad, own_grad = input_back(
        line.tie(grad_q), grad_kv, grad_rel, weights_qk, weights_vr, first
    )
    line.mark(own_grad)
    from_two = lax.ppermute(two_grad, "head", [(i + 2, i) for i in chain[:-2]])
    from_one = lax.ppermute(one_grad, "head", [(i + 1, i) for i in chain[:-1]])
    scatter_ffn.total = line.tie(scatter_ffn.total)
    line.mark(scatter_ffn.total, *line.last)
    scatter_cross.step()
    scatter_self.step()
    packed = line.mark(pack_sums(line.last[0]))
    packed_bits = [("batch", bit) for bit in range(nb)] + [("head", 0), ("head", 1)]

    def add_packed(packed):
        axis_name, bit = packed_bits.pop(0)
        came = swap(packed, axis_name, 1 << bit)
        packed = line.tie(packed)
        return line.mark(packed + after(came, packed))

    memory_grad = line.tie(memory_grad)
    line.mark(memory_grad, *line.last)
    own_grad = line.mark(add_halo(line.tie(own_grad), from_one, from_two))
    own_grad = line.mark(reorder_blocks(line.tie(own_grad), to_natural)).reshape(
        3, share, features
    )
    grad_hidden = jnp.transpose(own_grad, (1, 0, 2))[None]
    scatter_cross.step()
    packed = add_packed(packed)
    scatter_self.step()
    packed = add_packed(packed)
    grad_memory = line.mark(reorder_blocks(line.tie(memory_grad), to_natural, F32))[None]
    scatter_cross.step()
    packed = add_packed(packed)
    scatter_self.step()
    packed = add_packed(packed)
    scatter_cross.step()
    scatter_self.step()
    while packed_bits:
        packed = add_packed(packed)
    scatters = (scatter_ffn, scatter_cross, scatter_self)
    for scatter in scatters:
        while not hasattr(scatter, "total"):
            scatter.step()
    grads_ffn, grads_cross, grads_self = [scatter.total for scatter in scatters]

    ends = [0]
    for size in (2 * features, groups * 128, 2 * features, up_bias.shape[0], 9 * features):
        ends.append(ends[-1] + size)
    self_bias_grad = packed[ends[0] : ends[1]].reshape(2, -1)
    relpos_bias_grad = packed[ends[1] : ends[2]]
    cross_bias_grad = packed[ends[2] : ends[3]].reshape(2, -1)
    up_bias_grad = packed[ends[3] : ends[4]]
    feature_sums = packed[ends[4] : ends[5]].reshape(3, 3, features)

    return (
        layer_out,
        grad_hidden,
        grad_memory,
        jnp.transpose(grads_self[0], (1, 0, 2)),
        grads_self[1],
        grads_cross[3],
        grads_cross[0],
        grads_cross[1].reshape(blk, 2, 256),
        grads_cross[2],
        grads_ffn[:, 1024:],
        grads_ffn[:, 0:1024],
        self_bias_grad,
        relpos_bias_grad,
        cross_bias_grad,
        up_bias_grad,
        feature_sums[:, 0],
        feature_sums[:, 1],
        feature_sums[:, 2],
    )


def solution(mesh):
    in_specs = (
        P("batch", "head", None, None),
        P("batch", "head", None),
        P("batch", None, None, None),
        P("batch", None),
        P("batch", None),
        P(),
        P("batch", None, "head"),
        P("batch", "head"),
        P("batch", "head"),
        P("batch", "head"),
        P("batch", None, "head"),
        P("batch", "head"),
        P("batch", "head"),
        P("batch", "head"),
        P(),
        P(),
        P(),
        P(),
        P(),
        P(),
        P(),
    )
    out_specs = (
        P("batch", None, None, None),
        P("batch", "head", None, None),
        P("batch", "head", None),
        P("batch", None, "head"),
        P("batch", "head"),
        P("batch", "head"),
        P("batch", "head"),
        P("batch", None, "head"),
        P("batch", "head"),
        P("batch", "head"),
        P("batch", "head"),
        P(),
        P(),
        P(),
        P(),
        P(),
        P(),
        P(),
    )
    return jax.shard_map(
        per_device, mesh=mesh, in_specs=in_specs, out_specs=out_specs, check_vma=False
    )
```

```python
import functools

import jax
import jax.numpy as jnp
from jax import lax
from jax.experimental import pallas as pl
from jax.experimental.layout import Layout, with_layout_constraint
from jax.experimental.pallas import tpu as pltpu
from jax.sharding import PartitionSpec as P

BUCKETS = 32
HEAD_DIM = 64
WIDEST_DOC = 256
EPSILON = 1e-05
MASKED = -1e30
BF = jnp.bfloat16
F32 = jnp.float32
VMEM_BYTES = 56 * 1024 * 1024


def params():
    return pltpu.CompilerParams(vmem_limit_bytes=VMEM_BYTES)


def dot(a, b, ca, cb):
    return lax.dot_general(a, b, (((ca,), (cb,)), ((), ())), preferred_element_type=F32)


def whole(shape):
    return pl.BlockSpec(shape, lambda *_: (0,) * len(shape))


def swap(array_in, axis, bit):
    count = lax.axis_size(axis)
    return lax.ppermute(array_in, axis, [(i, i ^ bit) for i in range(count)])


def bits_of(axis):
    return (lax.axis_size(axis) - 1).bit_length()


def after(value, *earlier):
    return lax.optimization_barrier((value,) + earlier)[0]


def pin(value):
    return with_layout_constraint(value, Layout(tuple(range(value.ndim))))


class Line:
    def __init__(self):
        self.last = ()

    def tie(self, value):
        return after(value, *self.last) if self.last else value

    def mark(self, *values):
        self.last = values
        return values[0]


def chunk_of(rows):
    return rows // 4 if rows % 64 == 0 else rows


def stack_rows(*arrays):
    rows = [array.shape[0] for array in arrays]

    def body(*refs):
        at = 0
        for ref, count in zip(refs, rows):
            refs[-1][at : at + count] = ref[...]
            at += count

    return pl.pallas_call(
        body,
        out_shape=jax.ShapeDtypeStruct((sum(rows), arrays[0].shape[1]), arrays[0].dtype),
        compiler_params=params(),
        name="stack_rows",
    )(*arrays)


def add_blocks(parts, outs, dtype):
    rows = parts[0][0].shape[1]
    chunk = chunk_of(rows) if parts[0][0].size >= 1 << 20 else rows
    widths = [mine.shape[2] for mine, _ in parts]

    def body(*refs):
        ins, out_refs = refs[: 2 * len(parts)], refs[2 * len(parts) :]
        for out_ref, (members, chosen) in zip(out_refs, outs):
            at = 0
            for part in chosen:
                mine_ref, came_ref = ins[2 * part], ins[2 * part + 1]
                for place, block in enumerate(members):
                    total = mine_ref[block].astype(F32) + came_ref[block].astype(F32)
                    out_ref[place, :, at : at + widths[part]] = total.astype(dtype)
                at += widths[part]

    def spec(count, width):
        return pl.BlockSpec((count, chunk, width), lambda i: (0, i, 0))

    shapes = [(len(members), sum(widths[part] for part in chosen)) for members, chosen in outs]
    return pl.pallas_call(
        body,
        grid=(rows // chunk,),
        in_specs=[spec(array.shape[0], array.shape[2]) for pair in parts for array in pair],
        out_specs=[spec(*shape) for shape in shapes],
        out_shape=[jax.ShapeDtypeStruct((count, rows, width), dtype) for count, width in shapes],
        compiler_params=params(),
        name="add_blocks",
    )(*[array for pair in parts for array in pair])


def split_sum(mine, came, cuts):
    rows = mine.shape[0]

    def body(mine_ref, came_ref, *out_refs):
        for out_ref, (first, width, copies) in zip(out_refs, cuts):
            for k in range(copies):
                cols = slice(first + k * width, first + (k + 1) * width)
                total = mine_ref[:, cols].astype(F32) + came_ref[:, cols].astype(F32)
                if copies > 1:
                    out_ref[k] = total
                else:
                    out_ref[...] = total

    return pl.pallas_call(
        body,
        out_shape=[
            jax.ShapeDtypeStruct((copies, rows, width) if copies > 1 else (rows, width), F32)
            for _, width, copies in cuts
        ],
        compiler_params=params(),
        name="split_sum",
    )(mine, came)


class Gather:
    def __init__(self, line, shard):
        self.line = line
        self.nb, self.nz = bits_of("batch"), bits_of("head")
        self.buf = pin(shard).reshape((1,) * (self.nb + self.nz) + shard.shape)

    def send(self, axis_name, bit):
        self.axis = self.nb + self.nz - 1 - bit if axis_name == "head" else bit
        self.came = swap(self.line.tie(self.buf), axis_name, 1 << bit)

    def take(self):
        mine = self.line.tie(self.buf)
        self.buf = self.line.mark(jnp.concatenate([mine, after(self.came, mine)], self.axis))

    def columns(self, first, count):
        part = Gather.__new__(Gather)
        part.line, part.nb, part.nz = self.line, self.nb, self.nz
        part.buf = pin(self.buf[..., first : first + count])
        return part

    def close(self):
        shape = (1 << (self.nb - 1), 1 << self.nz) + self.buf.shape[-2:]
        return (self.buf.reshape(shape), self.came.reshape(shape))


class Scatter:
    def __init__(self, line, parts, orders, natural=False, cuts=()):
        self.natural, self.cuts = natural, cuts
        nb, self.nz = bits_of("batch"), bits_of("head")
        self.line = line
        self.groups, self.blk = parts[0][1].shape[1:3]
        self.left = [list(order) for order in orders]
        self.names = [sorted(order) for order in orders]
        self.heads = list(range(self.nz))
        self.mine, self.came = [None] * len(parts), [None] * len(parts)
        for number, (theirs, mine) in enumerate(parts):
            self.send(number, theirs, mine)

    def send(self, number, theirs, mine):
        bit = self.left[number].pop(0)
        self.names[number].remove(bit)
        self.mine[number] = mine
        self.came[number] = swap(theirs, "batch", 1 << bit)

    def step(self):
        tied = [self.line.tie(mine) for mine in self.mine]
        came = [after(came, mine) for came, mine in zip(self.came, tied)]
        pairs = [
            (one.reshape(-1, self.blk, one.shape[-1]), two.reshape(-1, self.blk, one.shape[-1]))
            for one, two in zip(tied, came)
        ]
        blocks = range(pairs[0][0].shape[0])
        everyone = list(range(len(pairs)))
        if self.left[0]:
            outs = []
            for number in everyone:
                place = self.names[number].index(self.left[number][0])
                bit = len(self.names[number]) - 1 - place
                for side in (1, 0):
                    chosen = [k for k in blocks if (k // self.groups >> bit & 1) == side]
                    outs.append((chosen, [number]))
            sums = add_blocks(pairs, outs, BF)
            self.line.mark(*sums)
            for number in everyone:
                self.send(number, sums[2 * number], sums[2 * number + 1])
            return
        if self.natural:
            (total,) = add_blocks(pairs, [(list(blocks), everyone)], BF)
            total = lax.psum_scatter(
                self.line.mark(total), "head", scatter_dimension=0, tiled=False
            )
            self.total = total.astype(F32)
            return
        if not self.heads:
            self.total = split_sum(pairs[0][0][0], pairs[0][1][0], self.cuts)
            self.line.mark(*self.total)
            return
        bit = self.heads.pop(0)
        sides = [[k for k in blocks if (k & 1) == side] for side in (1, 0)]
        theirs, mine = add_blocks(pairs, [(side, everyone) for side in sides], BF)
        self.line.mark(theirs, mine)
        self.mine = [mine]
        self.came = [swap(theirs, "head", 1 << bit)]


def add_halo(own, one, two):
    count = one.shape[0]

    def body(own_ref, one_ref, two_ref, out_ref):
        out_ref[count:] = own_ref[count:]
        came = one_ref[...].astype(F32) + two_ref[...].astype(F32)
        out_ref[0:count] = own_ref[0:count] + came

    return pl.pallas_call(
        body,
        out_shape=jax.ShapeDtypeStruct(own.shape, own.dtype),
        compiler_params=params(),
        name="add_halo",
    )(own, one, two)


def copy_tracks(array_in):
    tracks, rows, features = array_in.shape

    def body(in_ref, out_ref):
        out_ref[...] = in_ref[...]

    return pl.pallas_call(
        body,
        grid=(tracks,),
        in_specs=[pl.BlockSpec((1, rows, features), lambda n: (n, 0, 0))],
        out_specs=pl.BlockSpec((1, rows, features), lambda n: (n, 0, 0)),
        out_shape=jax.ShapeDtypeStruct(array_in.shape, array_in.dtype),
        compiler_params=params(),
        name="copy_tracks",
    )(array_in)


def bit_reverse(number, width):
    turned = 0
    for bit in range(width):
        turned |= ((number >> bit) & 1) << (width - 1 - bit)
    return turned


def reorder_blocks(array_in, table, dtype=None):
    count = table.shape[0]
    rows, features = array_in.shape
    blk = features // count
    dtype = dtype or array_in.dtype
    if blk % 128:
        blocks = jnp.take(array_in.reshape(rows, count, blk), table, axis=1)
        return blocks.reshape(rows, features).astype(dtype)

    def body(table_ref, in_ref, out_ref):
        for p in range(count):
            start = pl.multiple_of(table_ref[p] * blk, blk)
            out_ref[:, p * blk : (p + 1) * blk] = in_ref[:, pl.ds(start, blk)].astype(dtype)

    return pl.pallas_call(
        body,
        out_shape=jax.ShapeDtypeStruct(array_in.shape, dtype),
        grid_spec=pltpu.PrefetchScalarGridSpec(
            num_scalar_prefetch=1,
            grid=(1,),
            in_specs=[pl.BlockSpec((rows, features), lambda p, table_ref: (0, 0))],
            out_specs=pl.BlockSpec((rows, features), lambda p, table_ref: (0, 0)),
        ),
        name="reorder",
    )(table, array_in)


def piece_specs(pieces, cols, col_block, step=None):
    count, _, blk, _ = pieces[0].shape
    return [
        pl.BlockSpec((count, 1, blk, cols), lambda j, *c: (0, j, 0, col_block + (c[0] if c else 0)))
        for _ in pieces
    ]


def flat_piece(ref):
    count, _, blk, cols = ref.shape
    return ref[...].reshape(count * blk, cols)


def over_features(x, piece_refs):
    depth = x.shape[1] // len(piece_refs)
    total = None
    for number, ref in enumerate(piece_refs):
        term = dot(x[:, number * depth : (number + 1) * depth], flat_piece(ref), 1, 0)
        total = term if total is None else total + term
    return total


def project(x, pieces, first_col, cols, tile, affine, out_dtype, name):
    rows, features = x.shape
    groups = pieces[0].shape[1]
    per = cols // tile
    paired = per == 1 and tile <= 256

    def body(x_ref, *refs):
        *piece_refs, affine_ref, out_ref = refs
        depth = features // len(pieces)
        for k in range(2 if paired else 1):
            total = None
            for number, ref in enumerate(piece_refs):
                piece = ref[:, k].reshape(depth, tile)
                term = dot(x_ref[:, number * depth : (number + 1) * depth], piece, 1, 0)
                total = term if total is None else total + term
            where = slice(k * tile, (k + 1) * tile)
            total = (total + affine_ref[0:1, where]) * affine_ref[1:2, where]
            out_ref[:, where] = total.astype(out_ref.dtype)

    if paired:
        grid, wide = (groups // 2, 1), 2 * tile
        weight_specs = [
            pl.BlockSpec(
                (pieces[0].shape[0], 2, pieces[0].shape[2], tile),
                lambda j, c: (0, j, 0, first_col // tile),
            )
            for _ in pieces
        ]
    else:
        grid, wide = (groups, per), tile
        weight_specs = piece_specs(pieces, tile, first_col // tile)
    return pl.pallas_call(
        body,
        grid=grid,
        in_specs=[whole((rows, features))]
        + weight_specs
        + [pl.BlockSpec((2, wide), lambda j, c: (0, j * per + c))],
        out_specs=pl.BlockSpec((rows, wide), lambda j, c: (0, j * per + c)),
        out_shape=jax.ShapeDtypeStruct((rows, groups * cols), out_dtype),
        compiler_params=params(),
        name=name,
    )(x, *pieces, affine)


def project_plain(x, pieces, first_col, cols, name):
    groups = pieces[0].shape[1]
    affine = jnp.stack([jnp.zeros((groups * cols,), F32), jnp.ones((groups * cols,), F32)])
    return project(x, pieces, first_col, cols, cols, affine, BF, name)


def paired_specs(pieces, cols, col_block):
    count, _, blk, _ = pieces[0].shape
    return [pl.BlockSpec((count, 2, blk, cols), lambda i: (0, i, 0, col_block)) for _ in pieces]


def add_paired_rows(acc_ref, left_ref, piece_refs, cols):
    depth = acc_ref.shape[1] // len(piece_refs)
    for number, ref in enumerate(piece_refs):
        where = slice(number * depth, (number + 1) * depth)
        total = None
        for k in range(2):
            piece = ref[:, k].reshape(depth, cols)
            term = dot(left_ref[:, k * cols : (k + 1) * cols], piece, 1, 1)
            total = term if total is None else total + term
        acc_ref[:, where] += total


def add_rows(acc_ref, left, piece_refs):
    depth = acc_ref.shape[1] // len(piece_refs)
    for number, ref in enumerate(piece_refs):
        where = slice(number * depth, (number + 1) * depth)
        acc_ref[:, where] += dot(left, flat_piece(ref), 1, 1)


def row_mean(v):
    return jnp.mean(v, -1, keepdims=True)


def column_sum(v):
    return jnp.sum(v, 0, keepdims=True)


def normalize(v):
    centered = v - row_mean(v)
    spread = lax.rsqrt(row_mean(centered * centered) + EPSILON)
    return centered * spread, spread


def normalize_back(upstream, unit, spread, gain):
    a = upstream * gain
    return spread * (a - row_mean(a) - unit * row_mean(a * unit))


def close_sublayer(left, pieces, first_col, cols, residual, vectors, name):
    rows, features = residual.shape
    groups = pieces[0].shape[1]
    count = len(pieces)

    def body(left_ref, *refs):
        piece_refs = refs[:count]
        residual_ref, vectors_ref, normed_ref, low_ref, unit_ref, spread_ref, acc_ref = refs[count:]
        step = pl.program_id(0)

        @pl.when(step == 0)
        def _():
            acc_ref[...] = jnp.zeros_like(acc_ref)

        add_paired_rows(acc_ref, left_ref, piece_refs, cols)

        @pl.when(step == groups // 2 - 1)
        def _():
            v = residual_ref[...].astype(F32) + (acc_ref[...] + vectors_ref[2:3])
            unit, spread = normalize(v)
            normed = unit * vectors_ref[0:1] + vectors_ref[1:2]
            normed_ref[...] = normed
            low_ref[...] = normed.astype(BF)
            unit_ref[...] = unit
            spread_ref[...] = spread

    return pl.pallas_call(
        body,
        grid=(groups // 2,),
        in_specs=[pl.BlockSpec((rows, 2 * cols), lambda j: (0, j))]
        + paired_specs(pieces, cols, first_col // cols)
        + [whole((rows, features)), whole((3, features))],
        out_specs=[whole((rows, features))] * 3 + [whole((rows, 1))],
        out_shape=[
            jax.ShapeDtypeStruct((rows, features), F32),
            jax.ShapeDtypeStruct((rows, features), BF),
            jax.ShapeDtypeStruct((rows, features), F32),
            jax.ShapeDtypeStruct((rows, 1), F32),
        ],
        scratch_shapes=[pltpu.VMEM((rows, features), F32)],
        compiler_params=params(),
        name=name,
    )(left, *pieces, residual, vectors)


def natural_from_exchange(order_ref, first, from_ref, to_ref, blk):
    if blk % 128:
        to_ref[...] = from_ref[...]
        return
    for p in range(from_ref.shape[1] // blk):
        start = pl.multiple_of(order_ref[first + p] * blk, blk)
        to_ref[:, pl.ds(start, blk)] = from_ref[:, p * blk : (p + 1) * blk]


def exchange_from_natural(order_ref, first, from_ref, to_ref, blk):
    if blk % 128:
        to_ref[...] = from_ref[...]
        return
    for p in range(from_ref.shape[1] // blk):
        start = pl.multiple_of(order_ref[first + p] * blk, blk)
        to_ref[:, p * blk : (p + 1) * blk] = from_ref[:, pl.ds(start, blk)]


def norm_back_outputs(upstream, unit, spread, gain, grad_ref, grad_low_ref, sums_ref):
    grad = normalize_back(upstream, unit, spread, gain)
    grad_ref[...] = grad
    grad_low_ref[...] = grad.astype(BF)
    sums_ref[0:1] = column_sum(upstream * unit)
    sums_ref[1:2] = column_sum(upstream)
    sums_ref[2:3] = column_sum(grad)


def held(shape):
    return pl.BlockSpec(shape, lambda *_: (0,) * len(shape), pipeline_mode=pl.Buffered(1))


def feed_forward(
    order, low, normed, weights, up_bias, vectors, grad_out, unit, spread, gain, out_pieces, out_col
):
    rows, features = normed.shape
    batches, groups, blk, both = weights.shape
    cols = both // 2
    width = out_pieces[0].shape[3] - out_col
    count = len(out_pieces)

    def body(order_ref, low_ref, normed_ref, weights_ref, bias_ref, vectors_ref, grad_ref, unit_ref,
             spread_ref, gain_ref, *refs):
        piece_refs = refs[:count]
        (
            active_ref, out_ref, third_low_ref, third_sums_ref, upper_ref, bias_sum_ref,
            second_ref, second_low_ref, second_sums_ref, ctx_ref,
            held_ref, natural_ref, acc_ref, turned_ref, third_ref, slope_ref, sems,
        ) = refs[count:]
        step = pl.program_id(0)

        def copy(j):
            return pltpu.make_async_copy(weights_ref.at[:, j], held_ref.at[j], sems.at[j])

        @pl.when(step == 0)
        def _():
            for j in range(groups):
                copy(j).start()
            natural_from_exchange(order_ref, groups, low_ref, natural_ref, blk)
            acc_ref[...] = jnp.zeros_like(acc_ref)

        for j in range(groups):

            @pl.when(step == j)
            def _():
                copy(j).wait()

        @pl.when(step < groups)
        def _():
            up = held_ref[step, :, :, 0:cols].reshape(features, cols)
            upper = dot(natural_ref[...], up, 1, 0) + bias_ref[...]
            cdf = 0.5 * (1.0 + lax.erf(upper * 0.7071067811865476))
            active = (upper * cdf).astype(BF)
            slope = cdf + upper * jnp.exp(-0.5 * upper * upper) * 0.3989422804014327
            active_ref[...] = active
            slope_ref[step] = slope.astype(BF)
            down = held_ref[step, :, :, cols:].reshape(features, cols)
            acc_ref[...] += dot(active, down, 1, 1)

        @pl.when(step == groups - 1)
        def _():
            exchange_from_natural(order_ref, groups, acc_ref, turned_ref, blk)
            v = normed_ref[...] + (turned_ref[...] + vectors_ref[2:3])
            unit3, spread3 = normalize(v)
            gain3 = vectors_ref[0:1]
            turned_ref[...] = unit3 * gain3 + vectors_ref[1:2]
            natural_from_exchange(order_ref, groups, turned_ref, acc_ref, blk)
            out_ref[...] = acc_ref[...].astype(BF)
            upstream = grad_ref[...]
            third = normalize_back(upstream, unit3, spread3, gain3)
            third_ref[...] = third
            third_low_ref[...] = third.astype(BF)
            third_sums_ref[0:1] = column_sum(upstream * unit3)
            third_sums_ref[1:2] = column_sum(upstream)
            third_sums_ref[2:3] = column_sum(third)
            natural_from_exchange(order_ref, groups, third_low_ref, natural_ref, blk)
            acc_ref[...] = jnp.zeros_like(acc_ref)

        @pl.when((step >= groups) & (step < 2 * groups))
        def _():
            j = step - groups
            down = held_ref[j, :, :, cols:].reshape(features, cols)
            grad_upper = dot(natural_ref[...], down, 1, 0) * slope_ref[j].astype(F32)
            bias_sum_ref[...] = column_sum(grad_upper)
            low = grad_upper.astype(BF)
            upper_ref[...] = low
            up = held_ref[j, :, :, 0:cols].reshape(features, cols)
            acc_ref[...] += dot(low, up, 1, 1)

        @pl.when(step == 2 * groups - 1)
        def _():
            exchange_from_natural(order_ref, groups, acc_ref, turned_ref, blk)
            norm_back_outputs(
                turned_ref[...] + third_ref[...],
                unit_ref[...],
                spread_ref[...],
                gain_ref[...],
                second_ref,
                second_low_ref,
                second_sums_ref,
            )

        @pl.when(step == 2 * groups)
        def _():
            low = second_low_ref[...]
            for j in range(groups):
                total = None
                depth = features // count
                for number, ref in enumerate(piece_refs):
                    piece = ref[:, j].reshape(depth, width)
                    term = dot(low[:, number * depth : (number + 1) * depth], piece, 1, 0)
                    total = term if total is None else total + term
                ctx_ref[:, j * width : (j + 1) * width] = total.astype(BF)

    def forward_block(j, order):
        return (0, jnp.minimum(j, groups - 1))

    def backward_block(j, order):
        return (0, jnp.clip(j - groups, 0, groups - 1))

    piece_rows = out_pieces[0].shape[0]
    return pl.pallas_call(
        body,
        grid_spec=pltpu.PrefetchScalarGridSpec(
            num_scalar_prefetch=1,
            grid=(2 * groups + 1,),
            in_specs=[
                held((rows, features)),
                held((rows, features)),
                pl.BlockSpec(memory_space=pl.ANY),
                pl.BlockSpec((1, cols), forward_block),
                held((3, features)),
                held((rows, features)),
                held((rows, features)),
                held((rows, 1)),
                held((1, features)),
            ]
            + [
                pl.BlockSpec(
                    (piece_rows, groups, blk, width),
                    lambda j, order: (0, 0, 0, out_col // width),
                    pipeline_mode=pl.Buffered(1),
                )
                for _ in out_pieces
            ],
            out_specs=[
                pl.BlockSpec((rows, cols), forward_block),
                whole((rows, features)),
                whole((rows, features)),
                whole((3, features)),
                pl.BlockSpec((rows, cols), backward_block),
                pl.BlockSpec((1, cols), backward_block),
                whole((rows, features)),
                whole((rows, features)),
                whole((3, features)),
                whole((rows, groups * width)),
            ],
            scratch_shapes=[
                pltpu.VMEM((groups, batches, blk, both), BF),
                pltpu.VMEM((rows, features), BF),
                pltpu.VMEM((rows, features), F32),
                pltpu.VMEM((rows, features), F32),
                pltpu.VMEM((rows, features), F32),
                pltpu.VMEM((groups, rows, cols), BF),
                pltpu.SemaphoreType.DMA((groups,)),
            ],
        ),
        out_shape=[
            jax.ShapeDtypeStruct((rows, groups * cols), BF),
            jax.ShapeDtypeStruct((rows, features), BF),
            jax.ShapeDtypeStruct((rows, features), BF),
            jax.ShapeDtypeStruct((3, features), F32),
            jax.ShapeDtypeStruct((rows, groups * cols), BF),
            jax.ShapeDtypeStruct((1, groups * cols), F32),
            jax.ShapeDtypeStruct((rows, features), F32),
            jax.ShapeDtypeStruct((rows, features), BF),
            jax.ShapeDtypeStruct((3, features), F32),
            jax.ShapeDtypeStruct((rows, groups * width), BF),
        ],
        compiler_params=params(),
        name="feed_forward",
    )(order, low, normed, weights, up_bias, vectors, grad_out, unit, spread, gain, *out_pieces)


def cross_query_back(grad_query, pieces, first_col, cols, second, unit, spread, gain):
    rows, features = second.shape
    groups = pieces[0].shape[1]
    count = len(pieces)

    def body(left_ref, *refs):
        piece_refs = refs[:count]
        second_ref, unit_ref, spread_ref, gain_ref, grad_ref, grad_low_ref, sums_ref, acc_ref = refs[
            count:
        ]
        step = pl.program_id(0)

        @pl.when(step == 0)
        def _():
            acc_ref[...] = second_ref[...]

        add_paired_rows(acc_ref, left_ref, piece_refs, cols)

        @pl.when(step == groups // 2 - 1)
        def _():
            norm_back_outputs(
                acc_ref[...],
                unit_ref[...],
                spread_ref[...],
                gain_ref[...],
                grad_ref,
                grad_low_ref,
                sums_ref,
            )

    return pl.pallas_call(
        body,
        grid=(groups // 2,),
        in_specs=[pl.BlockSpec((rows, 2 * cols), lambda j: (0, j))]
        + paired_specs(pieces, cols, first_col // cols)
        + [whole((rows, features)), whole((rows, features)), whole((rows, 1)), whole((1, features))],
        out_specs=[whole((rows, features)), whole((rows, features)), whole((3, features))],
        out_shape=[
            jax.ShapeDtypeStruct((rows, features), F32),
            jax.ShapeDtypeStruct((rows, features), BF),
            jax.ShapeDtypeStruct((3, features), F32),
        ],
        scratch_shapes=[pltpu.VMEM((rows, features), F32)],
        compiler_params=params(),
        name="cross_query_back",
    )(grad_query, *pieces, second, unit, spread, gain)


def rows_back(order, left, pieces, first_col, cols, name):
    rows = left.shape[0]
    count = len(pieces)
    groups = pieces[0].shape[1]
    features = count * pieces[0].shape[0] * pieces[0].shape[2]
    span = rows // groups

    def body(order_ref, left_ref, *refs):
        piece_refs = refs[:count]
        out_ref, acc_ref = refs[count:]
        step = pl.program_id(0)

        @pl.when(step == 0)
        def _():
            acc_ref[...] = jnp.zeros_like(acc_ref)

        add_rows(acc_ref, left_ref[...], piece_refs)

        @pl.when(step == groups - 1)
        def _():
            for k in range(groups):
                start = pl.multiple_of(order_ref[k] * span, span)
                out_ref[pl.ds(start, span)] = acc_ref[k * span : (k + 1) * span].astype(BF)

    piece_count, _, blk, _ = pieces[0].shape
    return pl.pallas_call(
        body,
        grid_spec=pltpu.PrefetchScalarGridSpec(
            num_scalar_prefetch=1,
            grid=(groups,),
            in_specs=[pl.BlockSpec((rows, cols), lambda j, order: (0, j))]
            + [
                pl.BlockSpec(
                    (piece_count, 1, blk, cols), lambda j, order: (0, j, 0, first_col // cols)
                )
                for _ in pieces
            ],
            out_specs=whole((rows, features)),
            scratch_shapes=[pltpu.VMEM((rows, features), F32)],
        ),
        out_shape=jax.ShapeDtypeStruct((rows, features), BF),
        compiler_params=params(),
        name=name,
    )(order, left, *pieces)


def input_back(grad_query, grad_kv, grad_rel, pieces, others, first):
    rows, features = first.shape
    long_rows = grad_kv.shape[0]
    halo = long_rows - rows
    groups = pieces[0].shape[1]
    count = len(pieces)
    width = grad_query.shape[1] // groups
    rel_width = grad_rel.shape[1] // groups

    def body(query_ref, kv_ref, rel_ref, *refs):
        parts = [refs[count * k : count * (k + 1)] for k in range(4)]
        first_ref, two_ref, one_ref, own_ref, acc_ref = refs[4 * count :]
        step = pl.program_id(0)

        @pl.when(step == 0)
        def _():
            acc_ref[0:halo] = jnp.zeros((halo, features), F32)
            acc_ref[halo:] = first_ref[...]

        own_acc = acc_ref.at[halo:]
        add_rows(own_acc, query_ref[...], parts[0])
        add_rows(acc_ref, kv_ref[:, 0:width], parts[1])
        add_rows(acc_ref, kv_ref[:, width : 2 * width], parts[2])
        add_rows(own_acc, rel_ref[...], parts[3])

        @pl.when(step == groups - 1)
        def _():
            two_ref[...] = acc_ref[0 : halo // 2].astype(BF)
            one_ref[...] = acc_ref[halo // 2 : halo].astype(BF)
            own_ref[...] = acc_ref[halo:]

    return pl.pallas_call(
        body,
        grid=(groups,),
        in_specs=[
            pl.BlockSpec((rows, width), lambda j: (0, j)),
            pl.BlockSpec((long_rows, 2 * width), lambda j: (0, j)),
            pl.BlockSpec((rows, rel_width), lambda j: (0, j)),
        ]
        + piece_specs(pieces, width, 0)
        + piece_specs(pieces, width, 1)
        + piece_specs(others, width, 0)
        + piece_specs(others, rel_width, width // rel_width)
        + [whole((rows, features))],
        out_specs=[whole((halo // 2, features))] * 2 + [whole((rows, features))],
        out_shape=[
            jax.ShapeDtypeStruct((halo // 2, features), BF),
            jax.ShapeDtypeStruct((halo // 2, features), BF),
            jax.ShapeDtypeStruct((rows, features), F32),
        ],
        scratch_shapes=[pltpu.VMEM((long_rows, features), F32)],
        compiler_params=params(),
        name="input_back",
    )(grad_query, grad_kv, grad_rel, *pieces, *pieces, *others, *others, first)


def weight_products(order, entries, half, extra, parts, pieces, groups, name):
    features = entries[0][0].shape[1]
    depth = features // 2
    blk = depth // pieces
    widths = [right.shape[1] // groups for _, right in entries]
    total = sum(widths)
    count = len(entries)
    outs = []
    if parts is None:
        outs.append((0, total, list(range(pieces))))
    else:
        at = 0
        for width, bit in parts:
            for side in (1, 0):
                outs.append((at, width, [p for p in range(pieces) if (p >> bit & 1) == side]))
            at += width

    def body(order_ref, *refs):
        lefts, rights = refs[:count], refs[count : 2 * count]
        out_refs = refs[len(refs) - len(outs) :]
        for k in range(2):
            odd = order_ref[2 * pl.program_id(0) + k] & 1
            at = 0
            for left_ref, right_ref, width in zip(lefts, rights, widths):
                right = right_ref[:, pl.ds(pl.multiple_of(odd * width, 128), width)]
                term = dot(left_ref[...], right, 0, 0).reshape(pieces, blk, width)
                if extra is not None:
                    term = term + refs[2 * count][:, k, :, at : at + width].astype(F32)
                term = term.astype(BF)
                for out_ref, (first, size, members) in zip(out_refs, outs):
                    low, high = max(at, first), min(at + width, first + size)
                    if low >= high:
                        continue
                    for place, piece in enumerate(members):
                        out_ref[place, k, :, low - first : high - first] = term[
                            piece, :, low - at : high - at
                        ]
                at += width

    def block(number, width):
        return pl.BlockSpec((number, 2, blk, width), lambda i, order: (0, i, 0, 0))

    in_specs = [
        pl.BlockSpec((left.shape[0], depth), lambda i, order: (0, half)) for left, _ in entries
    ]
    in_specs += [
        pl.BlockSpec((right.shape[0], 2 * width), lambda i, order: (0, order[2 * i] // 2))
        for (_, right), width in zip(entries, widths)
    ]
    operands = [left for left, _ in entries] + [right for _, right in entries]
    if extra is not None:
        in_specs.append(block(pieces, total))
        operands.append(extra)
    return pl.pallas_call(
        body,
        grid_spec=pltpu.PrefetchScalarGridSpec(
            num_scalar_prefetch=1,
            grid=(groups // 2,),
            in_specs=in_specs,
            out_specs=[block(len(members), width) for _, width, members in outs],
        ),
        out_shape=[
            jax.ShapeDtypeStruct((len(members), groups, blk, width), BF)
            for _, width, members in outs
        ],
        compiler_params=params(),
        name=name,
    )(order, *operands)


def half_masks(rows):
    lane = lax.broadcasted_iota(jnp.int32, (rows, 128), 1)
    return [
        jnp.where((lane >= 64 * half) & (lane < 64 * half + 64), 1.0, 0.0).astype(F32)
        for half in range(2)
    ]


def lanes_and_rows(share):
    lane = lax.broadcasted_iota(jnp.int32, (share, share), 1)
    row = lax.broadcasted_iota(jnp.int32, (share, share), 0)
    return lane > row


def turn_right(block):
    return pltpu.roll(block, 1, 1, stride=1, stride_axis=0)


def skew(distance, later):
    share = later.shape[0]
    tracks = []
    for n in range(distance.shape[0] // share):
        rows = slice(n * share, (n + 1) * share)
        far, near = turn_right(distance[rows, 0:share]), turn_right(distance[rows, share:])
        tracks.append(jnp.concatenate([far, jnp.where(later, near, far), near], 1))
    return jnp.concatenate(tracks, 0)


def unskew_sources(grid, later):
    share = later.shape[0]
    tracks = []
    for n in range(grid.shape[0] // share):
        old, mid, new = [
            grid[n * share : (n + 1) * share, c * share : (c + 1) * share] for c in range(3)
        ]
        tracks.append(jnp.concatenate([jnp.where(later, old, mid), jnp.where(later, mid, new)], 1))
    return jnp.concatenate(tracks, 0)


def turn_blocks(array_in, share):
    rows = array_in.shape[0]
    return jnp.concatenate(
        [
            jnp.concatenate(
                [turn_right(array_in[r : r + share, c : c + share]) for c in (0, share)], 1
            )
            for r in range(0, rows, share)
        ],
        0,
    )


def self_attention(qk, values, relpos, mask, turned, share):
    rows, window = 3 * share, 3 * share
    groups = values.shape[1] // 256
    long_rows = qk.shape[0]
    halo = long_rows - rows

    def body(q_ref, k_ref, v_ref, rel_ref, mask_ref, turned_ref, ctx_ref, raised_ref, own_ref):
        halves = half_masks(rows)
        later = lanes_and_rows(share)
        lane = lax.broadcasted_iota(jnp.int32, (rows, 128), 1)
        rel = rel_ref[...]
        high = rel.astype(BF)
        split = jnp.concatenate([high, (rel - high.astype(F32)).astype(BF)], 1)
        row_id = lax.broadcasted_iota(jnp.int32, (256, 2 * share), 0) & 127
        track = lax.broadcasted_iota(jnp.int32, (rows, 1), 0) >= share
        own_all = jnp.zeros((rows, 128), F32)
        for pair in range(2):
            cols = slice(128 * pair, 128 * pair + 128)
            q = q_ref[halo:, cols]
            k, v = k_ref[0:window, cols], v_ref[0:window, cols]
            own_k = k_ref[halo:, cols].astype(F32)
            own_v = v_ref[halo:, cols].astype(F32)
            product = q.astype(F32) * own_k
            mixed = jnp.zeros((rows, 128), F32)
            for half in range(2):
                head = 2 * pair + half
                scores = dot(q * halves[half].astype(BF), k, 1, 1)
                table = jnp.where(row_id == turned_ref[...] + 32 * head, 1.0, 0.0).astype(BF)
                scores = scores + skew(dot(split, table, 1, 0), later) + mask_ref[...]
                own = jnp.sum(
                    product * halves[half] + jnp.where(lane == 32 * head, rel, 0.0), -1, keepdims=True
                )
                own = jnp.where(track, own, MASKED)
                top = jnp.maximum(jnp.max(scores, -1, keepdims=True), own)
                raised = jnp.exp(scores - top)
                own_raised = jnp.exp(own - top)
                scale = 1.0 / (jnp.sum(raised, -1, keepdims=True) + own_raised)
                raised = raised.astype(BF)
                raised_ref[head] = raised
                own_all = jnp.where(lane == head, own_raised, own_all)
                own_all = jnp.where(lane == head + 4, scale, own_all)
                mixed = mixed + (dot(raised, v, 1, 0) + own_raised * own_v) * (scale * halves[half])
            ctx_ref[:, cols] = mixed.astype(BF)
        own_ref[...] = own_all

    return pl.pallas_call(
        body,
        grid=(groups,),
        in_specs=[
            pl.BlockSpec((long_rows, 256), lambda j: (0, 2 * j)),
            pl.BlockSpec((long_rows, 256), lambda j: (0, 2 * j + 1)),
            pl.BlockSpec((long_rows, 256), lambda j: (0, j)),
            pl.BlockSpec((rows, 128), lambda j: (0, j)),
            whole((rows, window)),
            whole((1, 2 * share)),
        ],
        out_specs=[
            pl.BlockSpec((rows, 256), lambda j: (0, j)),
            pl.BlockSpec((4, rows, window), lambda j: (j, 0, 0)),
            pl.BlockSpec((rows, 128), lambda j: (0, j)),
        ],
        out_shape=[
            jax.ShapeDtypeStruct((rows, groups * 256), BF),
            jax.ShapeDtypeStruct((4 * groups, rows, window), BF),
            jax.ShapeDtypeStruct((rows, groups * 128), F32),
        ],
        compiler_params=params(),
        name="self_attention",
    )(qk, qk, values, relpos, mask, turned)


def self_attention_back(qk, values, raised, own_raised, grad_ctx, straight, share):
    rows, window = 3 * share, 3 * share
    groups = values.shape[1] // 256
    long_rows = qk.shape[0]
    halo = long_rows - rows

    def body(
        q_ref, k_ref, v_ref, raised_ref, own_ref, grad_ref, straight_ref,
        gq_ref, gkv_ref, grel_ref, sums_ref, rel_sums_ref,
    ):
        halves = half_masks(rows)
        later = lanes_and_rows(share)
        lane = lax.broadcasted_iota(jnp.int32, (rows, 128), 1)
        turn = jnp.where(
            lax.broadcasted_iota(jnp.int32, (2 * share, 2 * share), 0)
            + lax.broadcasted_iota(jnp.int32, (2 * share, 2 * share), 1)
            == 2 * share - 1,
            1.0,
            0.0,
        ).astype(BF)
        column = lax.broadcasted_iota(jnp.int32, (2 * share, 128), 1)
        grel = jnp.zeros((rows, 128), F32)
        own_all = own_ref[...]

        def pick(number):
            return jnp.sum(jnp.where(lane == number, own_all, 0.0), -1, keepdims=True)

        for pair in range(2):
            cols = slice(128 * pair, 128 * pair + 128)
            q = q_ref[halo:, cols]
            k, v = k_ref[0:window, cols], v_ref[0:window, cols]
            own_k = k_ref[halo:, cols].astype(F32)
            own_v = v_ref[halo:, cols].astype(F32)
            scales = [pick(2 * pair + half + 4) for half in range(2)]
            grad_wide = grad_ref[:, cols].astype(F32)
            grad_wide = grad_wide * (scales[0] * halves[0] + scales[1] * halves[1])
            grad = grad_wide.astype(BF)
            own_product = grad_wide * own_v
            gq = jnp.zeros((rows, 128), F32)
            own_spread = jnp.zeros((rows, 128), F32)
            own_weight = jnp.zeros((rows, 128), F32)
            score_parts, prob_parts, q_parts, g_parts = [], [], [], []
            for half in range(2):
                head = 2 * pair + half
                low_half = halves[half].astype(BF)
                p = raised_ref[head]
                p_wide = p.astype(F32)
                grad_half = grad * low_half
                grad_probs = dot(grad_half, v, 1, 1)
                own_p = pick(head)
                own_grad = jnp.sum(own_product * halves[half], -1, keepdims=True)
                row_dot = jnp.sum(p_wide * grad_probs, -1, keepdims=True) + own_p * own_grad
                row_dot = row_dot * scales[half]
                grad_scores = p_wide * (grad_probs - row_dot)
                source = unskew_sources(grad_scores, later).astype(BF)
                grad_scores = grad_scores.astype(BF)
                grad_own = (own_p * (own_grad - row_dot)).astype(BF).astype(F32)
                gq = gq + (dot(grad_scores, k, 1, 0) + grad_own * own_k) * halves[half]
                own_spread = own_spread + grad_own * halves[half]
                own_weight = own_weight + own_p * halves[half]
                score_parts.append(grad_scores)
                prob_parts.append(p)
                q_parts.append(q * low_half)
                g_parts.append(grad_half)
                turned = turn_blocks(dot(source, turn, 1, 0), share).astype(BF)
                table = jnp.where(column == straight_ref[...] + 32 * head, 1.0, 0.0).astype(BF)
                grel = grel + dot(turned, table, 1, 0) + jnp.where(lane == 32 * head, grad_own, 0.0)
            gk = dot(
                jnp.concatenate(q_parts, 0), jnp.concatenate(score_parts, 0), 0, 0
            ).T
            gv = dot(
                jnp.concatenate(g_parts, 0), jnp.concatenate(prob_parts, 0), 0, 0
            ).T
            gq = gq * 0.125
            gq_ref[:, cols] = gq.astype(BF)
            own_gk = own_spread * q.astype(F32)
            own_gv = own_weight * grad_wide
            vcols = slice(256 + 128 * pair, 256 + 128 * pair + 128)
            gkv_ref[0:window, cols] = gk.astype(BF)
            gkv_ref[0:window, vcols] = gv.astype(BF)
            gkv_ref[window:, cols] = own_gk[share:].astype(BF)
            gkv_ref[window:, vcols] = own_gv[share:].astype(BF)
            sums_ref[0:1, cols] = column_sum(gq)
            sums_ref[1:2, cols] = column_sum(gv) + column_sum(own_gv[share:])
        grel_ref[...] = grel.astype(BF)
        rel_sums_ref[...] = column_sum(grel)

    return pl.pallas_call(
        body,
        grid=(groups,),
        in_specs=[
            pl.BlockSpec((long_rows, 256), lambda j: (0, 2 * j)),
            pl.BlockSpec((long_rows, 256), lambda j: (0, 2 * j + 1)),
            pl.BlockSpec((long_rows, 256), lambda j: (0, j)),
            pl.BlockSpec((4, rows, window), lambda j: (j, 0, 0)),
            pl.BlockSpec((rows, 128), lambda j: (0, j)),
            pl.BlockSpec((rows, 256), lambda j: (0, j)),
            whole((2 * share, 1)),
        ],
        out_specs=[
            pl.BlockSpec((rows, 256), lambda j: (0, j)),
            pl.BlockSpec((long_rows, 512), lambda j: (0, j)),
            pl.BlockSpec((rows, 128), lambda j: (0, j)),
            pl.BlockSpec((2, 256), lambda j: (0, j)),
            pl.BlockSpec((1, 128), lambda j: (0, j)),
        ],
        out_shape=[
            jax.ShapeDtypeStruct((rows, groups * 256), BF),
            jax.ShapeDtypeStruct((long_rows, groups * 512), BF),
            jax.ShapeDtypeStruct((rows, groups * 128), BF),
            jax.ShapeDtypeStruct((2, groups * 256), F32),
            jax.ShapeDtypeStruct((1, groups * 128), F32),
        ],
        compiler_params=params(),
        name="self_attention_back",
    )(qk, qk, values, raised, own_raised, grad_ctx, straight)


def cross_attention(queries, kv):
    rows, places = queries.shape[0], kv.shape[0]
    groups = queries.shape[1] // 256

    def body(q_ref, k_ref, v_ref, ctx_ref, raised_ref, scale_ref):
        halves = half_masks(rows)
        lane = lax.broadcasted_iota(jnp.int32, (rows, 128), 1)
        scales = jnp.zeros((rows, 128), F32)
        for pair in range(2):
            cols = slice(128 * pair, 128 * pair + 128)
            q, k, v = q_ref[:, cols], k_ref[:, cols], v_ref[:, cols]
            mixed = jnp.zeros((rows, 128), F32)
            for half in range(2):
                head = 2 * pair + half
                scores = dot(q * halves[half].astype(BF), k, 1, 1)
                raised = jnp.exp(scores - jnp.max(scores, -1, keepdims=True))
                scale = 1.0 / jnp.sum(raised, -1, keepdims=True)
                raised = raised.astype(BF)
                raised_ref[head] = raised
                scales = jnp.where(lane == head, scale, scales)
                mixed = mixed + dot(raised, v, 1, 0) * (scale * halves[half])
            ctx_ref[:, cols] = mixed.astype(BF)
        scale_ref[...] = scales

    return pl.pallas_call(
        body,
        grid=(groups,),
        in_specs=[
            pl.BlockSpec((rows, 256), lambda j: (0, j)),
            pl.BlockSpec((places, 256), lambda j: (0, 2 * j)),
            pl.BlockSpec((places, 256), lambda j: (0, 2 * j + 1)),
        ],
        out_specs=[
            pl.BlockSpec((rows, 256), lambda j: (0, j)),
            pl.BlockSpec((4, rows, places), lambda j: (j, 0, 0)),
            pl.BlockSpec((rows, 128), lambda j: (0, j)),
        ],
        out_shape=[
            jax.ShapeDtypeStruct((rows, groups * 256), BF),
            jax.ShapeDtypeStruct((4 * groups, rows, places), BF),
            jax.ShapeDtypeStruct((rows, groups * 128), F32),
        ],
        compiler_params=params(),
        name="cross_attention",
    )(queries, kv, kv)


def cross_attention_back(queries, kv, raised, scales, grad_ctx):
    rows, places = queries.shape[0], kv.shape[0]
    groups = queries.shape[1] // 256

    def body(q_ref, k_ref, v_ref, raised_ref, scale_ref, grad_ref, gq_ref, gkv_ref, sums_ref):
        halves = half_masks(rows)
        lane = lax.broadcasted_iota(jnp.int32, (rows, 128), 1)
        scale_all = scale_ref[...]
        for pair in range(2):
            cols = slice(128 * pair, 128 * pair + 128)
            q, k, v = q_ref[:, cols], k_ref[:, cols], v_ref[:, cols]
            scale = [
                jnp.sum(jnp.where(lane == 2 * pair + half, scale_all, 0.0), -1, keepdims=True)
                for half in range(2)
            ]
            grad = grad_ref[:, cols].astype(F32) * (scale[0] * halves[0] + scale[1] * halves[1])
            grad = grad.astype(BF)
            gq = jnp.zeros((rows, 128), F32)
            score_parts, prob_parts, q_parts, g_parts = [], [], [], []
            for half in range(2):
                low_half = halves[half].astype(BF)
                p = raised_ref[2 * pair + half]
                p_wide = p.astype(F32)
                grad_half = grad * low_half
                grad_probs = dot(grad_half, v, 1, 1)
                row_dot = jnp.sum(p_wide * grad_probs, -1, keepdims=True) * scale[half]
                grad_scores = (p_wide * (grad_probs - row_dot)).astype(BF)
                gq = gq + dot(grad_scores, k, 1, 0) * halves[half]
                score_parts.append(grad_scores)
                prob_parts.append(p)
                q_parts.append(q * low_half)
                g_parts.append(grad_half)
            gk = dot(
                jnp.concatenate(q_parts, 0), jnp.concatenate(score_parts, 0), 0, 0
            ).T
            gv = dot(
                jnp.concatenate(g_parts, 0), jnp.concatenate(prob_parts, 0), 0, 0
            ).T
            gq = gq * 0.125
            gq_ref[:, cols] = gq.astype(BF)
            vcols = slice(256 + 128 * pair, 256 + 128 * pair + 128)
            gkv_ref[:, cols] = gk.astype(BF)
            gkv_ref[:, vcols] = gv.astype(BF)
            sums_ref[0:1, cols] = column_sum(gq)
            sums_ref[1:2, cols] = column_sum(gv)

    return pl.pallas_call(
        body,
        grid=(groups,),
        in_specs=[
            pl.BlockSpec((rows, 256), lambda j: (0, j)),
            pl.BlockSpec((places, 256), lambda j: (0, 2 * j)),
            pl.BlockSpec((places, 256), lambda j: (0, 2 * j + 1)),
            pl.BlockSpec((4, rows, places), lambda j: (j, 0, 0)),
            pl.BlockSpec((rows, 128), lambda j: (0, j)),
            pl.BlockSpec((rows, 256), lambda j: (0, j)),
        ],
        out_specs=[
            pl.BlockSpec((rows, 256), lambda j: (0, j)),
            pl.BlockSpec((places, 512), lambda j: (0, j)),
            pl.BlockSpec((2, 256), lambda j: (0, j)),
        ],
        out_shape=[
            jax.ShapeDtypeStruct((rows, groups * 256), BF),
            jax.ShapeDtypeStruct((places, groups * 512), BF),
            jax.ShapeDtypeStruct((2, groups * 256), F32),
        ],
        compiler_params=params(),
        name="cross_attention_back",
    )(queries, kv, kv, raised, scales, grad_ctx)


def per_device(
    hidden,
    memory,
    grad_out,
    lengths,
    key_mask,
    buckets,
    self_weight,
    relpos_weight,
    selfout_weight,
    crossq_weight,
    crosskv_weight,
    crossout_weight,
    up_weight,
    down_weight,
    self_bias,
    relpos_bias,
    cross_bias,
    up_bias,
    norm_gain,
    norm_bias,
    out_bias,
):
    batches, groups = lax.axis_size("batch"), lax.axis_size("head")
    b, z = lax.axis_index("batch"), lax.axis_index("head")
    nb = bits_of("batch")
    share, features = hidden.shape[1], hidden.shape[3]
    length = share * groups
    rows, window = 3 * share, 3 * share
    assert share == 128 and hidden.shape[0] == 1 and WIDEST_DOC <= 2 * share
    assert batches == 1 << nb and features % batches == 0 and groups == 4
    near, far = list(range(1, nb)), list(reversed(range(1, nb)))

    turned_ids = jnp.array([bit_reverse(p, nb) for p in range(batches)], jnp.int32)
    to_exchange = b ^ turned_ids
    natural = lax.iota(jnp.int32, batches) ^ b
    to_natural = jnp.zeros_like(natural)
    for bit in range(nb):
        to_natural = to_natural | (((natural >> bit) & 1) << (nb - 1 - bit))
    group_order = z ^ lax.iota(jnp.int32, groups)

    def small_features(stack):
        count = stack.shape[0]
        blocks = stack.reshape(count, batches, features // batches)
        return jnp.take(blocks, to_exchange, axis=1).reshape(count, features)

    blk = self_weight.shape[0]
    assert nb >= 2 and bits_of("head") == 2
    line = Line()
    self_shard = jnp.concatenate([self_weight.reshape(blk, -1), relpos_weight], 1).astype(BF)
    gather_self = Gather(line, line.mark(pin(self_shard)))
    gather_self.send("head", 1)
    ffn_shard = line.mark(
        pin(jnp.concatenate([line.tie(up_weight), down_weight], 1).astype(BF))
    )
    gather_ffn = Gather(line, ffn_shard)

    columns = jnp.concatenate(
        [
            self_bias[0].reshape(groups, -1),
            self_bias[1].reshape(groups, -1),
            cross_bias[0].reshape(groups, -1),
            cross_bias[1].reshape(groups, -1),
            relpos_bias.reshape(groups, -1),
            up_bias.reshape(groups, -1),
        ],
        1,
    )
    columns = jnp.take(columns, group_order, axis=0)
    query_bias, value_bias = columns[:, 0:256], columns[:, 256:512]
    cross_query_bias, cross_value_bias = columns[:, 512:768], columns[:, 768:1024]
    rel_row = columns[:, 1024:1152].reshape(1, -1)
    up_row = columns[:, 1152:].reshape(1, -1)

    memory_own = line.mark(reorder_blocks(line.tie(memory[0]), to_exchange))
    own = jnp.transpose(line.tie(hidden[0]), (1, 0, 2)).reshape(rows, features)
    own = line.mark(reorder_blocks(own, to_exchange))
    upstream = lax.dynamic_slice_in_dim(line.tie(grad_out[0]), z * share, share, 0)
    upstream = jnp.transpose(upstream, (1, 0, 2)).reshape(rows, features)
    upstream = line.mark(reorder_blocks(upstream, to_exchange))
    chain = list(range(groups))

    vectors = small_features(jnp.concatenate([norm_gain, norm_bias, out_bias], 0))
    vectors = vectors.reshape(3, 3, features).transpose(1, 0, 2)
    none = jnp.zeros((groups, 256), F32)

    def affine(bias, scale):
        return jnp.stack([bias, jnp.full(bias.shape, scale, F32)])

    scales = jnp.concatenate([none + 0.125, none + 1.0], 1).reshape(-1)
    qk_affine = jnp.stack([jnp.concatenate([query_bias, none], 1).reshape(-1), scales])
    value_affine = affine(value_bias.reshape(-1), 1.0)
    rel_affine = affine(rel_row[0], 1.0)
    cross_query_affine = affine(cross_query_bias.reshape(-1), 0.125)
    cross_kv_affine = affine(jnp.concatenate([none, cross_value_bias], 1).reshape(-1), 1.0)

    places = lax.iota(jnp.int32, length)
    doc_ends = jnp.cumsum(lengths[0])
    segment = jnp.sum((places[:, None] >= doc_ends[None, :]).astype(jnp.int32), -1)
    lead = window - share
    padded_segment = jnp.concatenate([jnp.full((lead,), -1, jnp.int32), segment])
    padded_mask = jnp.concatenate([jnp.zeros((lead,), jnp.int32), key_mask[0]])
    key_segment = lax.dynamic_slice_in_dim(padded_segment, z * share, window)
    key_open = lax.dynamic_slice_in_dim(padded_mask, z * share, window)
    query_segment = lax.dynamic_slice_in_dim(segment, z * share, share)
    query_at = lax.iota(jnp.int32, share)[:, None] + lead
    key_at = lax.iota(jnp.int32, window)[None, :]
    joined = (query_segment[:, None] == key_segment[None, :]) & (
        (key_open[None, :] == 1) | (query_at == key_at)
    )
    allowed_main = joined & (key_at <= query_at)
    allowed_pred = joined & (key_at < query_at)
    mask = jnp.where(jnp.stack([allowed_main, allowed_pred, allowed_pred]), 0.0, MASKED)
    mask = mask.reshape(rows, window).astype(F32)
    straight = buckets[0 : 2 * share]
    turned = straight[::-1]

    mask = line.mark(line.tie(mask))
    assert nb >= 2 and bits_of("head") == 2
    gather_cross = Gather(
        line,
        jnp.concatenate(
            [selfout_weight, crossq_weight, crosskv_weight.reshape(blk, -1), crossout_weight], 1
        ).astype(BF),
    )
    gather_self.take()
    gather_self.send("head", 0)
    gather_ffn.send("head", 1)
    gather_self.take()
    parts_self = [gather_self.columns(0, 512), gather_self.columns(512, 384)]
    orders_self = [near, far]
    for part, part_order in zip(parts_self, orders_self):
        part.send("batch", part_order[0])
    gather_ffn.take()
    gather_ffn.send("head", 0)
    for number in range(1, nb - 1):
        for part, part_order in zip(parts_self, orders_self):
            part.take()
            part.send("batch", part_order[number])
    gather_cross.send("head", 1)
    gather_ffn.take()
    for part in parts_self:
        part.take()
        part.send("batch", 0)
    gather_cross.take()
    gather_cross.send("head", 0)
    main = line.tie(own[0:share])
    before_one = lax.ppermute(main, "head", [(i, i + 1) for i in chain[:-1]])
    before_two = lax.ppermute(main, "head", [(i, i + 2) for i in chain[:-2]])
    gather_cross.take()
    parts_cross = [gather_cross.columns(0, 512), gather_cross.columns(512, 768)]
    orders_cross = [far, near]
    for part, part_order in zip(parts_cross, orders_cross):
        part.send("batch", part_order[0])
    extended = line.mark(stack_rows(before_two, before_one, line.tie(own)))
    memory_came = swap(line.tie(memory_own), "head", 2)
    weights_qk, weights_vr = [part.close() for part in parts_self]

    order = jnp.concatenate([group_order, to_exchange]).astype(jnp.int32)
    values = line.mark(
        project(line.tie(extended), weights_vr, 0, 256, 256, value_affine, BF, "self_v")
    )
    relpos = line.mark(
        project(line.tie(own), weights_vr, 256, 128, 128, rel_affine, F32, "self_rel")
    )
    for number in range(1, nb - 1):
        for part, part_order in zip(parts_cross, orders_cross):
            part.take()
            part.send("batch", part_order[number])
    weights_ffn = line.tie(gather_ffn.buf).reshape((groups,) + ffn_shard.shape)
    weights_ffn = lax.all_gather(weights_ffn, "batch", axis=0)
    if blk % 128:
        weights_ffn = jnp.take(weights_ffn, to_exchange, axis=0)
    qk = line.mark(project(line.tie(extended), weights_qk, 0, 512, 512, qk_affine, BF, "self_qk"))
    memory_half = line.mark(jnp.concatenate([line.tie(memory_own), memory_came], 0))
    memory_came = swap(memory_half, "head", 1)
    context, self_probs, self_own = self_attention(
        line.tie(qk), values, relpos, mask, turned.reshape(1, -1), share
    )
    line.mark(context)
    for part in parts_cross:
        part.take()
        part.send("batch", 0)
    weights_out, weights_kv = [part.close() for part in parts_cross]
    normed1, normed1_low, unit1, spread1 = close_sublayer(
        line.tie(context), weights_out, 0, 256, own, vectors[0], "self_out"
    )
    line.mark(normed1)
    cross_q = line.mark(
        project(
            line.tie(normed1_low), weights_out, 256, 256, 256, cross_query_affine, BF, "cross_q"
        )
    )
    memory_all = line.mark(jnp.concatenate([line.tie(memory_half), memory_came], 0))
    cross_kv = line.mark(
        project(line.tie(memory_all), weights_kv, 0, 512, 512, cross_kv_affine, BF, "cross_kv")
    )
    cross_context, cross_probs, cross_scales = cross_attention(line.tie(cross_q), cross_kv)
    line.mark(cross_context)
    normed2, normed2_low, unit2, spread2 = close_sublayer(
        line.tie(cross_context), weights_kv, 512, 256, normed1, vectors[1], "cross_out"
    )
    line.mark(normed2)
    (
        active, out_low, third_low, sums_third, upper_low, up_sums,
        second, second_low, sums_second, grad_cross_ctx,
    ) = feed_forward(
        order, line.tie(normed2_low), normed2, weights_ffn, up_row, vectors[2], upstream,
        unit2, spread2, vectors[1][0:1], weights_kv, 512,
    )
    line.mark(second)

    straight_order = lax.iota(jnp.int32, groups)

    def send(entries, name, natural=False):
        left, right = entries[0]
        entries = [(line.tie(left), right)] + entries[1:]
        turn = group_order if natural else straight_order
        (sent,) = weight_products(
            turn, entries, 1, None, None, batches // 2, groups, name + "_send"
        )
        return swap(line.mark(sent), "batch", 1)

    def keep(entries, came, parts, name, natural=False):
        left, right = entries[0]
        entries = [(line.tie(left), right)] + entries[1:]
        parts = [(width, nb - 1 - part_order[0]) for width, part_order in parts]
        turn = group_order if natural else straight_order
        outs = weight_products(
            turn, entries, 0, came, parts, batches // 2, groups, name + "_keep"
        )
        line.mark(outs[0])
        return [outs[k : k + 2] for k in range(0, len(outs), 2)]

    def natural_groups(block):
        return jnp.take(block.reshape(-1, groups, block.shape[1] // groups), group_order, axis=1)

    def pack_sums(earlier):
        feature_sums = jnp.concatenate([after(sums_first, earlier), sums_second, sums_third], 0)
        feature_sums = jnp.take(
            feature_sums.reshape(9, batches, features // batches), to_natural, axis=1
        )
        return jnp.concatenate(
            [
                natural_groups(self_sums).reshape(-1),
                natural_groups(rel_sums).reshape(-1),
                natural_groups(cross_sums).reshape(-1),
                natural_groups(up_sums).reshape(-1),
                feature_sums.reshape(-1),
            ]
        )

    down_entries = [(third_low, active)]
    if blk % 128:
        out_low = reorder_blocks(out_low, to_natural)
    out_low = out_low.reshape(3, share, features)
    layer_out = lax.all_gather(out_low, "head", axis=1, tiled=True)
    down_entries = [(third_low, active)]
    down_came = send(down_entries, "down_grad", True)
    up_entries = [(normed2_low, upper_low)]
    up_came = send(up_entries, "up_grad", True)
    down_halves = keep(down_entries, down_came, [(1024, near)], "down_grad", True)
    up_halves = keep(up_entries, up_came, [(1024, far)], "up_grad", True)
    scatter_ffn = Scatter(line, down_halves + up_halves, (near, far), True)
    grad_cross_q, grad_cross_kv, cross_sums = cross_attention_back(
        cross_q, cross_kv, cross_probs, cross_scales, line.tie(grad_cross_ctx)
    )
    line.mark(grad_cross_q)
    first, first_low, sums_first = cross_query_back(
        line.tie(grad_cross_q), weights_out, 256, 256, second, unit1, spread1, vectors[0][0:1]
    )
    line.mark(first)
    grad_context = project_plain(line.tie(first_low), weights_out, 0, 256, "self_ctx_back")
    line.mark(grad_context)
    grad_q, grad_kv, grad_rel, self_sums, rel_sums = self_attention_back(
        qk, values, self_probs, self_own, line.tie(grad_context), straight.reshape(-1, 1), share
    )
    line.mark(grad_q)
    layer_out = line.tie(layer_out)
    line.mark(layer_out, *line.last)
    scatter_ffn.step()
    memory_order = z ^ jnp.array([0, 2, 1, 3], jnp.int32)
    memory_part = rows_back(
        memory_order, line.tie(grad_cross_kv), weights_kv, 0, 512, "memory_back"
    )
    memory_grad = lax.psum_scatter(
        line.mark(memory_part), "head", scatter_dimension=0, tiled=True
    )
    cross_entries = [
        (normed1_low, grad_cross_q),
        (memory_all, grad_cross_kv),
        (second_low, cross_context),
        (first_low, context),
    ]
    cross_came = send(cross_entries, "cross_grad")
    self_entries = [(own, grad_q), (extended, grad_kv), (own, grad_rel)]
    self_came = send(self_entries, "self_grad")
    halves = keep(cross_entries, cross_came, [(640, near), (640, far)], "cross_grad")
    cross_cuts = ((0, 256, 1), (256, 512, 1), (768, 256, 1), (1024, 256, 1))
    scatter_cross = Scatter(line, halves, (near, far), cuts=cross_cuts)
    halves = keep(self_entries, self_came, [(512, near), (384, far)], "self_grad")
    scatter_self = Scatter(line, halves, (near, far), cuts=((0, 256, 3), (768, 128, 1)))
    while not hasattr(scatter_ffn, "total"):
        scatter_ffn.step()
    memory_grad = line.tie(memory_grad)
    line.mark(memory_grad, *line.last)
    packed = line.mark(pack_sums(line.last[0]))
    packed_bits = [("batch", bit) for bit in range(nb)] + [("head", 0), ("head", 1)]

    def add_packed(packed):
        axis_name, bit = packed_bits.pop(0)
        came = swap(packed, axis_name, 1 << bit)
        packed = line.tie(packed)
        return line.mark(packed + after(came, packed))

    two_grad, one_grad, own_grad = input_back(
        line.tie(grad_q), grad_kv, grad_rel, weights_qk, weights_vr, first
    )
    line.mark(own_grad)
    from_two = lax.ppermute(two_grad, "head", [(i + 2, i) for i in chain[:-2]])
    from_one = lax.ppermute(one_grad, "head", [(i + 1, i) for i in chain[:-1]])
    scatter_cross.step()
    scatter_self.step()
    scatter_ffn.total = line.tie(scatter_ffn.total)
    line.mark(scatter_ffn.total, *line.last)
    own_grad = line.mark(add_halo(line.tie(own_grad), from_one, from_two))
    own_grad = line.mark(reorder_blocks(line.tie(own_grad), to_natural)).reshape(
        3, share, features
    )
    grad_hidden = jnp.transpose(own_grad, (1, 0, 2))[None]
    scatter_cross.step()
    scatter_self.step()
    packed = add_packed(packed)
    grad_memory = line.mark(reorder_blocks(line.tie(memory_grad), to_natural, F32))[None]
    packed = add_packed(packed)
    layer_out = line.mark(copy_tracks(line.tie(layer_out)))
    layer_out = jnp.transpose(layer_out, (1, 0, 2))[None]
    scatter_cross.step()
    packed = add_packed(packed)
    scatter_self.step()
    while packed_bits:
        packed = add_packed(packed)
    ends = [0]
    for size in (2 * features, groups * 128, 2 * features, up_bias.shape[0], 9 * features):
        ends.append(ends[-1] + size)
    self_bias_grad = packed[ends[0] : ends[1]].reshape(2, -1)
    relpos_bias_grad = packed[ends[1] : ends[2]]
    cross_bias_grad = packed[ends[2] : ends[3]].reshape(2, -1)
    up_bias_grad = packed[ends[3] : ends[4]]
    feature_sums = packed[ends[4] : ends[5]].reshape(3, 3, features)
    small = (
        self_bias_grad,
        relpos_bias_grad,
        cross_bias_grad,
        up_bias_grad,
        feature_sums[:, 0],
        feature_sums[:, 1],
        feature_sums[:, 2],
    )
    small = lax.optimization_barrier(small + line.last)[: len(small)]
    line.mark(*small)
    while not hasattr(scatter_cross, "total"):
        scatter_cross.step()
    cross_kv_grad = line.mark(line.tie(scatter_cross.total[1]).reshape(blk, 2, 256))
    while not hasattr(scatter_self, "total"):
        scatter_self.step()
    grads_ffn, grads_cross, grads_self = [
        scatter.total for scatter in (scatter_ffn, scatter_cross, scatter_self)
    ]

    return (
        layer_out,
        grad_hidden,
        grad_memory,
        jnp.transpose(grads_self[0], (1, 0, 2)),
        grads_self[1],
        grads_cross[3],
        grads_cross[0],
        cross_kv_grad,
        grads_cross[2],
        grads_ffn[:, 1024:],
        grads_ffn[:, 0:1024],
    ) + tuple(small)


def solution(mesh):
    in_specs = (
        P("batch", "head", None, None),
        P("batch", "head", None),
        P("batch", None, None, None),
        P("batch", None),
        P("batch", None),
        P(),
        P("batch", None, "head"),
        P("batch", "head"),
        P("batch", "head"),
        P("batch", "head"),
        P("batch", None, "head"),
        P("batch", "head"),
        P("batch", "head"),
        P("batch", "head"),
        P(),
        P(),
        P(),
        P(),
        P(),
        P(),
        P(),
    )
    out_specs = (
        P("batch", None, None, None),
        P("batch", "head", None, None),
        P("batch", "head", None),
        P("batch", None, "head"),
        P("batch", "head"),
        P("batch", "head"),
        P("batch", "head"),
        P("batch", None, "head"),
        P("batch", "head"),
        P("batch", "head"),
        P("batch", "head"),
        P(),
        P(),
        P(),
        P(),
        P(),
        P(),
        P(),
    )
    return jax.shard_map(
        per_device, mesh=mesh, in_specs=in_specs, out_specs=out_specs, check_vma=False
    )
```

```python
import functools

import jax
import jax.numpy as jnp
from jax import lax
from jax.experimental import pallas as pl
from jax.experimental.layout import Layout, with_layout_constraint
from jax.experimental.pallas import tpu as pltpu
from jax.sharding import PartitionSpec as P

BUCKETS = 32
HEAD_DIM = 64
WIDEST_DOC = 256
EPSILON = 1e-05
MASKED = -1e30
BF = jnp.bfloat16
F32 = jnp.float32
VMEM_BYTES = 56 * 1024 * 1024


def params():
    return pltpu.CompilerParams(vmem_limit_bytes=VMEM_BYTES)


def dot(a, b, ca, cb):
    return lax.dot_general(a, b, (((ca,), (cb,)), ((), ())), preferred_element_type=F32)


def whole(shape):
    return pl.BlockSpec(shape, lambda *_: (0,) * len(shape))


def swap(array_in, axis, bit):
    count = lax.axis_size(axis)
    return lax.ppermute(array_in, axis, [(i, i ^ bit) for i in range(count)])


def bits_of(axis):
    return (lax.axis_size(axis) - 1).bit_length()


def after(value, *earlier):
    return lax.optimization_barrier((value,) + earlier)[0]


def pin(value):
    return with_layout_constraint(value, Layout(tuple(range(value.ndim))))


class Line:
    def __init__(self):
        self.last = ()

    def tie(self, value):
        return after(value, *self.last) if self.last else value

    def mark(self, *values):
        self.last = values
        return values[0]


def chunk_of(rows):
    return rows // 4 if rows % 64 == 0 else rows


def stack_rows(*arrays):
    rows = [array.shape[0] for array in arrays]

    def body(*refs):
        at = 0
        for ref, count in zip(refs, rows):
            refs[-1][at : at + count] = ref[...]
            at += count

    return pl.pallas_call(
        body,
        out_shape=jax.ShapeDtypeStruct((sum(rows), arrays[0].shape[1]), arrays[0].dtype),
        compiler_params=params(),
        name="stack_rows",
    )(*arrays)


def add_blocks(parts, outs, dtype):
    rows = parts[0][0].shape[1]
    chunk = chunk_of(rows) if parts[0][0].size >= 1 << 20 else rows
    widths = [mine.shape[2] for mine, _ in parts]

    def body(*refs):
        ins, out_refs = refs[: 2 * len(parts)], refs[2 * len(parts) :]
        for out_ref, (members, chosen) in zip(out_refs, outs):
            at = 0
            for part in chosen:
                mine_ref, came_ref = ins[2 * part], ins[2 * part + 1]
                for place, block in enumerate(members):
                    total = mine_ref[block].astype(F32) + came_ref[block].astype(F32)
                    out_ref[place, :, at : at + widths[part]] = total.astype(dtype)
                at += widths[part]

    def spec(count, width):
        return pl.BlockSpec((count, chunk, width), lambda i: (0, i, 0))

    shapes = [(len(members), sum(widths[part] for part in chosen)) for members, chosen in outs]
    return pl.pallas_call(
        body,
        grid=(rows // chunk,),
        in_specs=[spec(array.shape[0], array.shape[2]) for pair in parts for array in pair],
        out_specs=[spec(*shape) for shape in shapes],
        out_shape=[jax.ShapeDtypeStruct((count, rows, width), dtype) for count, width in shapes],
        compiler_params=params(),
        name="add_blocks",
    )(*[array for pair in parts for array in pair])


def split_sum(mine, came, cuts):
    rows = mine.shape[0]

    def body(mine_ref, came_ref, *out_refs):
        for out_ref, (first, width, copies) in zip(out_refs, cuts):
            for k in range(copies):
                cols = slice(first + k * width, first + (k + 1) * width)
                total = mine_ref[:, cols].astype(F32) + came_ref[:, cols].astype(F32)
                if copies > 1:
                    out_ref[k] = total
                else:
                    out_ref[...] = total

    return pl.pallas_call(
        body,
        out_shape=[
            jax.ShapeDtypeStruct((copies, rows, width) if copies > 1 else (rows, width), F32)
            for _, width, copies in cuts
        ],
        compiler_params=params(),
        name="split_sum",
    )(mine, came)


class Gather:
    def __init__(self, line, shard):
        self.line = line
        self.nb, self.nz = bits_of("batch"), bits_of("head")
        self.buf = pin(shard).reshape((1,) * (self.nb + self.nz) + shard.shape)

    def send(self, axis_name, bit):
        self.axis = self.nb + self.nz - 1 - bit if axis_name == "head" else bit
        self.came = swap(self.line.tie(self.buf), axis_name, 1 << bit)

    def take(self):
        mine = self.line.tie(self.buf)
        self.buf = self.line.mark(jnp.concatenate([mine, after(self.came, mine)], self.axis))

    def columns(self, first, count):
        part = Gather.__new__(Gather)
        part.line, part.nb, part.nz = self.line, self.nb, self.nz
        part.buf = pin(self.buf[..., first : first + count])
        return part

    def close(self):
        shape = (1 << (self.nb - 1), 1 << self.nz) + self.buf.shape[-2:]
        return (self.buf.reshape(shape), self.came.reshape(shape))


class Scatter:
    def __init__(self, line, parts, orders, natural=False, cuts=()):
        self.natural, self.cuts = natural, cuts
        nb, self.nz = bits_of("batch"), bits_of("head")
        self.line = line
        self.groups, self.blk = parts[0][1].shape[1:3]
        self.left = [list(order) for order in orders]
        self.names = [sorted(order) for order in orders]
        self.heads = list(range(self.nz))
        self.mine, self.came = [None] * len(parts), [None] * len(parts)
        for number, (theirs, mine) in enumerate(parts):
            self.send(number, theirs, mine)

    def send(self, number, theirs, mine):
        bit = self.left[number].pop(0)
        self.names[number].remove(bit)
        self.mine[number] = mine
        self.came[number] = swap(theirs, "batch", 1 << bit)

    def step(self):
        tied = [self.line.tie(mine) for mine in self.mine]
        came = [after(came, mine) for came, mine in zip(self.came, tied)]
        pairs = [
            (one.reshape(-1, self.blk, one.shape[-1]), two.reshape(-1, self.blk, one.shape[-1]))
            for one, two in zip(tied, came)
        ]
        blocks = range(pairs[0][0].shape[0])
        everyone = list(range(len(pairs)))
        if self.left[0]:
            outs = []
            for number in everyone:
                place = self.names[number].index(self.left[number][0])
                bit = len(self.names[number]) - 1 - place
                for side in (1, 0):
                    chosen = [k for k in blocks if (k // self.groups >> bit & 1) == side]
                    outs.append((chosen, [number]))
            sums = add_blocks(pairs, outs, BF)
            self.line.mark(*sums)
            for number in everyone:
                self.send(number, sums[2 * number], sums[2 * number + 1])
            return
        if self.natural:
            (total,) = add_blocks(pairs, [(list(blocks), everyone)], BF)
            total = lax.psum_scatter(
                self.line.mark(total), "head", scatter_dimension=0, tiled=False
            )
            self.total = total.astype(F32)
            return
        if not self.heads:
            self.total = split_sum(pairs[0][0][0], pairs[0][1][0], self.cuts)
            self.line.mark(*self.total)
            return
        bit = self.heads.pop(0)
        sides = [[k for k in blocks if (k & 1) == side] for side in (1, 0)]
        theirs, mine = add_blocks(pairs, [(side, everyone) for side in sides], BF)
        self.line.mark(theirs, mine)
        self.mine = [mine]
        self.came = [swap(theirs, "head", 1 << bit)]


def add_halo(own, one, two):
    count = one.shape[0]

    def body(own_ref, one_ref, two_ref, out_ref):
        out_ref[count:] = own_ref[count:]
        came = one_ref[...].astype(F32) + two_ref[...].astype(F32)
        out_ref[0:count] = own_ref[0:count] + came

    return pl.pallas_call(
        body,
        out_shape=jax.ShapeDtypeStruct(own.shape, own.dtype),
        compiler_params=params(),
        name="add_halo",
    )(own, one, two)


def copy_tracks(array_in):
    tracks, rows, features = array_in.shape

    def body(in_ref, out_ref):
        out_ref[...] = in_ref[...]

    return pl.pallas_call(
        body,
        grid=(tracks,),
        in_specs=[pl.BlockSpec((1, rows, features), lambda n: (n, 0, 0))],
        out_specs=pl.BlockSpec((1, rows, features), lambda n: (n, 0, 0)),
        out_shape=jax.ShapeDtypeStruct(array_in.shape, array_in.dtype),
        compiler_params=params(),
        name="copy_tracks",
    )(array_in)


def bit_reverse(number, width):
    turned = 0
    for bit in range(width):
        turned |= ((number >> bit) & 1) << (width - 1 - bit)
    return turned


def reorder_blocks(array_in, table, dtype=None):
    count = table.shape[0]
    rows, features = array_in.shape
    blk = features // count
    dtype = dtype or array_in.dtype
    if blk % 128:
        blocks = jnp.take(array_in.reshape(rows, count, blk), table, axis=1)
        return blocks.reshape(rows, features).astype(dtype)

    def body(table_ref, in_ref, out_ref):
        for p in range(count):
            start = pl.multiple_of(table_ref[p] * blk, blk)
            out_ref[:, p * blk : (p + 1) * blk] = in_ref[:, pl.ds(start, blk)].astype(dtype)

    return pl.pallas_call(
        body,
        out_shape=jax.ShapeDtypeStruct(array_in.shape, dtype),
        grid_spec=pltpu.PrefetchScalarGridSpec(
            num_scalar_prefetch=1,
            grid=(1,),
            in_specs=[pl.BlockSpec((rows, features), lambda p, table_ref: (0, 0))],
            out_specs=pl.BlockSpec((rows, features), lambda p, table_ref: (0, 0)),
        ),
        name="reorder",
    )(table, array_in)


def piece_specs(pieces, cols, col_block, step=None):
    count, _, blk, _ = pieces[0].shape
    return [
        pl.BlockSpec((count, 1, blk, cols), lambda j, *c: (0, j, 0, col_block + (c[0] if c else 0)))
        for _ in pieces
    ]


def flat_piece(ref):
    count, _, blk, cols = ref.shape
    return ref[...].reshape(count * blk, cols)


def over_features(x, piece_refs):
    depth = x.shape[1] // len(piece_refs)
    total = None
    for number, ref in enumerate(piece_refs):
        term = dot(x[:, number * depth : (number + 1) * depth], flat_piece(ref), 1, 0)
        total = term if total is None else total + term
    return total


def project(x, pieces, first_col, cols, tile, affine, out_dtype, name):
    rows, features = x.shape
    groups = pieces[0].shape[1]
    per = cols // tile
    paired = per == 1 and tile <= 256

    def body(x_ref, *refs):
        *piece_refs, affine_ref, out_ref = refs
        depth = features // len(pieces)
        for k in range(2 if paired else 1):
            total = None
            for number, ref in enumerate(piece_refs):
                piece = ref[:, k].reshape(depth, tile)
                term = dot(x_ref[:, number * depth : (number + 1) * depth], piece, 1, 0)
                total = term if total is None else total + term
            where = slice(k * tile, (k + 1) * tile)
            total = (total + affine_ref[0:1, where]) * affine_ref[1:2, where]
            out_ref[:, where] = total.astype(out_ref.dtype)

    if paired:
        grid, wide = (groups // 2, 1), 2 * tile
        weight_specs = [
            pl.BlockSpec(
                (pieces[0].shape[0], 2, pieces[0].shape[2], tile),
                lambda j, c: (0, j, 0, first_col // tile),
            )
            for _ in pieces
        ]
    else:
        grid, wide = (groups, per), tile
        weight_specs = piece_specs(pieces, tile, first_col // tile)
    return pl.pallas_call(
        body,
        grid=grid,
        in_specs=[whole((rows, features))]
        + weight_specs
        + [pl.BlockSpec((2, wide), lambda j, c: (0, j * per + c))],
        out_specs=pl.BlockSpec((rows, wide), lambda j, c: (0, j * per + c)),
        out_shape=jax.ShapeDtypeStruct((rows, groups * cols), out_dtype),
        compiler_params=params(),
        name=name,
    )(x, *pieces, affine)


def project_plain(x, pieces, first_col, cols, name):
    groups = pieces[0].shape[1]
    affine = jnp.stack([jnp.zeros((groups * cols,), F32), jnp.ones((groups * cols,), F32)])
    return project(x, pieces, first_col, cols, cols, affine, BF, name)


def paired_specs(pieces, cols, col_block):
    count, _, blk, _ = pieces[0].shape
    return [pl.BlockSpec((count, 2, blk, cols), lambda i: (0, i, 0, col_block)) for _ in pieces]


def add_paired_rows(acc_ref, left_ref, piece_refs, cols):
    depth = acc_ref.shape[1] // len(piece_refs)
    for number, ref in enumerate(piece_refs):
        where = slice(number * depth, (number + 1) * depth)
        total = None
        for k in range(2):
            piece = ref[:, k].reshape(depth, cols)
            term = dot(left_ref[:, k * cols : (k + 1) * cols], piece, 1, 1)
            total = term if total is None else total + term
        acc_ref[:, where] += total


def add_rows(acc_ref, left, piece_refs):
    depth = acc_ref.shape[1] // len(piece_refs)
    for number, ref in enumerate(piece_refs):
        where = slice(number * depth, (number + 1) * depth)
        acc_ref[:, where] += dot(left, flat_piece(ref), 1, 1)


def row_mean(v):
    return jnp.mean(v, -1, keepdims=True)


def column_sum(v):
    return jnp.sum(v, 0, keepdims=True)


def normalize(v):
    centered = v - row_mean(v)
    spread = lax.rsqrt(row_mean(centered * centered) + EPSILON)
    return centered * spread, spread


def normalize_back(upstream, unit, spread, gain):
    a = upstream * gain
    return spread * (a - row_mean(a) - unit * row_mean(a * unit))


def close_sublayer(left, pieces, first_col, cols, residual, vectors, name):
    rows, features = residual.shape
    groups = pieces[0].shape[1]
    count = len(pieces)

    def body(left_ref, *refs):
        piece_refs = refs[:count]
        residual_ref, vectors_ref, normed_ref, low_ref, unit_ref, spread_ref, acc_ref = refs[count:]
        step = pl.program_id(0)

        @pl.when(step == 0)
        def _():
            acc_ref[...] = jnp.zeros_like(acc_ref)

        add_paired_rows(acc_ref, left_ref, piece_refs, cols)

        @pl.when(step == groups // 2 - 1)
        def _():
            v = residual_ref[...].astype(F32) + (acc_ref[...] + vectors_ref[2:3])
            unit, spread = normalize(v)
            normed = unit * vectors_ref[0:1] + vectors_ref[1:2]
            normed_ref[...] = normed
            low_ref[...] = normed.astype(BF)
            unit_ref[...] = unit
            spread_ref[...] = spread

    return pl.pallas_call(
        body,
        grid=(groups // 2,),
        in_specs=[pl.BlockSpec((rows, 2 * cols), lambda j: (0, j))]
        + paired_specs(pieces, cols, first_col // cols)
        + [whole((rows, features)), whole((3, features))],
        out_specs=[whole((rows, features))] * 3 + [whole((rows, 1))],
        out_shape=[
            jax.ShapeDtypeStruct((rows, features), F32),
            jax.ShapeDtypeStruct((rows, features), BF),
            jax.ShapeDtypeStruct((rows, features), F32),
            jax.ShapeDtypeStruct((rows, 1), F32),
        ],
        scratch_shapes=[pltpu.VMEM((rows, features), F32)],
        compiler_params=params(),
        name=name,
    )(left, *pieces, residual, vectors)


def natural_from_exchange(order_ref, first, from_ref, to_ref, blk):
    if blk % 128:
        to_ref[...] = from_ref[...]
        return
    for p in range(from_ref.shape[1] // blk):
        start = pl.multiple_of(order_ref[first + p] * blk, blk)
        to_ref[:, pl.ds(start, blk)] = from_ref[:, p * blk : (p + 1) * blk]


def exchange_from_natural(order_ref, first, from_ref, to_ref, blk):
    if blk % 128:
        to_ref[...] = from_ref[...]
        return
    for p in range(from_ref.shape[1] // blk):
        start = pl.multiple_of(order_ref[first + p] * blk, blk)
        to_ref[:, p * blk : (p + 1) * blk] = from_ref[:, pl.ds(start, blk)]


def norm_back_outputs(upstream, unit, spread, gain, grad_ref, grad_low_ref, sums_ref):
    grad = normalize_back(upstream, unit, spread, gain)
    grad_ref[...] = grad
    grad_low_ref[...] = grad.astype(BF)
    sums_ref[0:1] = column_sum(upstream * unit)
    sums_ref[1:2] = column_sum(upstream)
    sums_ref[2:3] = column_sum(grad)


def held(shape):
    return pl.BlockSpec(shape, lambda *_: (0,) * len(shape), pipeline_mode=pl.Buffered(1))


def feed_forward(
    order, low, normed, weights, up_bias, vectors, grad_out, unit, spread, gain, out_pieces, out_col
):
    rows, features = normed.shape
    batches, groups, blk, both = weights.shape
    cols = both // 2
    width = out_pieces[0].shape[3] - out_col
    count = len(out_pieces)

    def body(order_ref, low_ref, normed_ref, weights_ref, bias_ref, vectors_ref, grad_ref, unit_ref,
             spread_ref, gain_ref, *refs):
        piece_refs = refs[:count]
        (
            active_ref, out_ref, third_low_ref, third_sums_ref, upper_ref, bias_sum_ref,
            second_ref, second_low_ref, second_sums_ref, ctx_ref,
            held_ref, natural_ref, acc_ref, turned_ref, third_ref, slope_ref, sems,
        ) = refs[count:]
        step = pl.program_id(0)

        def copy(j):
            return pltpu.make_async_copy(weights_ref.at[:, j], held_ref.at[j], sems.at[j])

        @pl.when(step == 0)
        def _():
            for j in range(groups):
                copy(j).start()
            natural_from_exchange(order_ref, groups, low_ref, natural_ref, blk)
            acc_ref[...] = jnp.zeros_like(acc_ref)

        for j in range(groups):

            @pl.when(step == j)
            def _():
                copy(j).wait()

        @pl.when(step < groups)
        def _():
            up = held_ref[step, :, :, 0:cols].reshape(features, cols)
            upper = dot(natural_ref[...], up, 1, 0) + bias_ref[...]
            cdf = 0.5 * (1.0 + lax.erf(upper * 0.7071067811865476))
            active = (upper * cdf).astype(BF)
            slope = cdf + upper * jnp.exp(-0.5 * upper * upper) * 0.3989422804014327
            active_ref[...] = active
            slope_ref[step] = slope.astype(BF)
            down = held_ref[step, :, :, cols:].reshape(features, cols)
            acc_ref[...] += dot(active, down, 1, 1)

        @pl.when(step == groups - 1)
        def _():
            exchange_from_natural(order_ref, groups, acc_ref, turned_ref, blk)
            v = normed_ref[...] + (turned_ref[...] + vectors_ref[2:3])
            unit3, spread3 = normalize(v)
            gain3 = vectors_ref[0:1]
            turned_ref[...] = unit3 * gain3 + vectors_ref[1:2]
            natural_from_exchange(order_ref, groups, turned_ref, acc_ref, blk)
            out_ref[...] = acc_ref[...].astype(BF)
            upstream = grad_ref[...]
            third = normalize_back(upstream, unit3, spread3, gain3)
            third_ref[...] = third
            third_low_ref[...] = third.astype(BF)
            third_sums_ref[0:1] = column_sum(upstream * unit3)
            third_sums_ref[1:2] = column_sum(upstream)
            third_sums_ref[2:3] = column_sum(third)
            natural_from_exchange(order_ref, groups, third_low_ref, natural_ref, blk)
            acc_ref[...] = jnp.zeros_like(acc_ref)

        @pl.when((step >= groups) & (step < 2 * groups))
        def _():
            j = step - groups
            down = held_ref[j, :, :, cols:].reshape(features, cols)
            grad_upper = dot(natural_ref[...], down, 1, 0) * slope_ref[j].astype(F32)
            bias_sum_ref[...] = column_sum(grad_upper)
            low = grad_upper.astype(BF)
            upper_ref[...] = low
            up = held_ref[j, :, :, 0:cols].reshape(features, cols)
            acc_ref[...] += dot(low, up, 1, 1)

        @pl.when(step == 2 * groups - 1)
        def _():
            exchange_from_natural(order_ref, groups, acc_ref, turned_ref, blk)
            norm_back_outputs(
                turned_ref[...] + third_ref[...],
                unit_ref[...],
                spread_ref[...],
                gain_ref[...],
                second_ref,
                second_low_ref,
                second_sums_ref,
            )

        @pl.when(step == 2 * groups - 1)
        def _():
            low = second_low_ref[...]
            for j in range(groups):
                total = None
                depth = features // count
                for number, ref in enumerate(piece_refs):
                    piece = ref[:, j].reshape(depth, width)
                    term = dot(low[:, number * depth : (number + 1) * depth], piece, 1, 0)
                    total = term if total is None else total + term
                ctx_ref[:, j * width : (j + 1) * width] = total.astype(BF)

    def forward_block(j, order):
        return (0, jnp.minimum(j, groups - 1))

    def backward_block(j, order):
        return (0, jnp.clip(j - groups, 0, groups - 1))

    piece_rows = out_pieces[0].shape[0]
    return pl.pallas_call(
        body,
        grid_spec=pltpu.PrefetchScalarGridSpec(
            num_scalar_prefetch=1,
            grid=(2 * groups,),
            in_specs=[
                held((rows, features)),
                held((rows, features)),
                pl.BlockSpec(memory_space=pl.ANY),
                pl.BlockSpec((1, cols), forward_block),
                held((3, features)),
                held((rows, features)),
                held((rows, features)),
                held((rows, 1)),
                held((1, features)),
            ]
            + [
                pl.BlockSpec(
                    (piece_rows, groups, blk, width),
                    lambda j, order: (0, 0, 0, out_col // width),
                    pipeline_mode=pl.Buffered(1),
                )
                for _ in out_pieces
            ],
            out_specs=[
                pl.BlockSpec((rows, cols), forward_block),
                whole((rows, features)),
                whole((rows, features)),
                whole((3, features)),
                pl.BlockSpec((rows, cols), backward_block),
                pl.BlockSpec((1, cols), backward_block),
                whole((rows, features)),
                whole((rows, features)),
                whole((3, features)),
                whole((rows, groups * width)),
            ],
            scratch_shapes=[
                pltpu.VMEM((groups, batches, blk, both), BF),
                pltpu.VMEM((rows, features), BF),
                pltpu.VMEM((rows, features), F32),
                pltpu.VMEM((rows, features), F32),
                pltpu.VMEM((rows, features), F32),
                pltpu.VMEM((groups, rows, cols), BF),
                pltpu.SemaphoreType.DMA((groups,)),
            ],
        ),
        out_shape=[
            jax.ShapeDtypeStruct((rows, groups * cols), BF),
            jax.ShapeDtypeStruct((rows, features), BF),
            jax.ShapeDtypeStruct((rows, features), BF),
            jax.ShapeDtypeStruct((3, features), F32),
            jax.ShapeDtypeStruct((rows, groups * cols), BF),
            jax.ShapeDtypeStruct((1, groups * cols), F32),
            jax.ShapeDtypeStruct((rows, features), F32),
            jax.ShapeDtypeStruct((rows, features), BF),
            jax.ShapeDtypeStruct((3, features), F32),
            jax.ShapeDtypeStruct((rows, groups * width), BF),
        ],
        compiler_params=params(),
        name="feed_forward",
    )(order, low, normed, weights, up_bias, vectors, grad_out, unit, spread, gain, *out_pieces)


def cross_query_back(grad_query, pieces, first_col, cols, second, unit, spread, gain):
    rows, features = second.shape
    groups = pieces[0].shape[1]
    count = len(pieces)

    def body(left_ref, *refs):
        piece_refs = refs[:count]
        second_ref, unit_ref, spread_ref, gain_ref, grad_ref, grad_low_ref, sums_ref, acc_ref = refs[
            count:
        ]
        step = pl.program_id(0)

        @pl.when(step == 0)
        def _():
            acc_ref[...] = second_ref[...]

        add_paired_rows(acc_ref, left_ref, piece_refs, cols)

        @pl.when(step == groups // 2 - 1)
        def _():
            norm_back_outputs(
                acc_ref[...],
                unit_ref[...],
                spread_ref[...],
                gain_ref[...],
                grad_ref,
                grad_low_ref,
                sums_ref,
            )

    return pl.pallas_call(
        body,
        grid=(groups // 2,),
        in_specs=[pl.BlockSpec((rows, 2 * cols), lambda j: (0, j))]
        + paired_specs(pieces, cols, first_col // cols)
        + [whole((rows, features)), whole((rows, features)), whole((rows, 1)), whole((1, features))],
        out_specs=[whole((rows, features)), whole((rows, features)), whole((3, features))],
        out_shape=[
            jax.ShapeDtypeStruct((rows, features), F32),
            jax.ShapeDtypeStruct((rows, features), BF),
            jax.ShapeDtypeStruct((3, features), F32),
        ],
        scratch_shapes=[pltpu.VMEM((rows, features), F32)],
        compiler_params=params(),
        name="cross_query_back",
    )(grad_query, *pieces, second, unit, spread, gain)


def rows_back(order, left, pieces, first_col, cols, name):
    rows = left.shape[0]
    count = len(pieces)
    groups = pieces[0].shape[1]
    features = count * pieces[0].shape[0] * pieces[0].shape[2]
    span = rows // groups

    def body(order_ref, left_ref, *refs):
        piece_refs = refs[:count]
        out_ref, acc_ref = refs[count:]
        step = pl.program_id(0)

        @pl.when(step == 0)
        def _():
            acc_ref[...] = jnp.zeros_like(acc_ref)

        add_paired_rows(acc_ref, left_ref, piece_refs, cols)

        @pl.when(step == groups // 2 - 1)
        def _():
            for k in range(groups):
                start = pl.multiple_of(order_ref[k] * span, span)
                out_ref[pl.ds(start, span)] = acc_ref[k * span : (k + 1) * span].astype(BF)

    piece_count, _, blk, _ = pieces[0].shape
    return pl.pallas_call(
        body,
        grid_spec=pltpu.PrefetchScalarGridSpec(
            num_scalar_prefetch=1,
            grid=(groups // 2,),
            in_specs=[pl.BlockSpec((rows, 2 * cols), lambda j, order: (0, j))]
            + [
                pl.BlockSpec(
                    (piece_count, 2, blk, cols), lambda j, order: (0, j, 0, first_col // cols)
                )
                for _ in pieces
            ],
            out_specs=whole((rows, features)),
            scratch_shapes=[pltpu.VMEM((rows, features), F32)],
        ),
        out_shape=jax.ShapeDtypeStruct((rows, features), BF),
        compiler_params=params(),
        name=name,
    )(order, left, *pieces)


def input_back(grad_query, grad_kv, grad_rel, pieces, others, first):
    rows, features = first.shape
    long_rows = grad_kv.shape[0]
    halo = long_rows - rows
    groups = pieces[0].shape[1]
    count = len(pieces)
    width = grad_query.shape[1] // groups
    rel_width = grad_rel.shape[1] // groups

    def body(query_ref, kv_ref, rel_ref, *refs):
        parts = [refs[count * k : count * (k + 1)] for k in range(4)]
        first_ref, two_ref, one_ref, own_ref, acc_ref = refs[4 * count :]
        step = pl.program_id(0)

        @pl.when(step == 0)
        def _():
            acc_ref[0:halo] = jnp.zeros((halo, features), F32)
            acc_ref[halo:] = first_ref[...]

        own_acc = acc_ref.at[halo:]
        add_paired_rows(own_acc, query_ref, parts[0], width)
        keys = jnp.concatenate([kv_ref[:, 0:width], kv_ref[:, 2 * width : 3 * width]], 1)
        add_paired_rows(acc_ref, keys, parts[1], width)
        values = jnp.concatenate([kv_ref[:, width : 2 * width], kv_ref[:, 3 * width :]], 1)
        add_paired_rows(acc_ref, values, parts[2], width)
        add_paired_rows(own_acc, rel_ref, parts[3], rel_width)

        @pl.when(step == groups // 2 - 1)
        def _():
            two_ref[...] = acc_ref[0 : halo // 2].astype(BF)
            one_ref[...] = acc_ref[halo // 2 : halo].astype(BF)
            own_ref[...] = acc_ref[halo:]

    return pl.pallas_call(
        body,
        grid=(groups // 2,),
        in_specs=[
            pl.BlockSpec((rows, 2 * width), lambda j: (0, j)),
            pl.BlockSpec((long_rows, 4 * width), lambda j: (0, j)),
            pl.BlockSpec((rows, 2 * rel_width), lambda j: (0, j)),
        ]
        + paired_specs(pieces, width, 0)
        + paired_specs(pieces, width, 1)
        + paired_specs(others, width, 0)
        + paired_specs(others, rel_width, width // rel_width)
        + [whole((rows, features))],
        out_specs=[whole((halo // 2, features))] * 2 + [whole((rows, features))],
        out_shape=[
            jax.ShapeDtypeStruct((halo // 2, features), BF),
            jax.ShapeDtypeStruct((halo // 2, features), BF),
            jax.ShapeDtypeStruct((rows, features), F32),
        ],
        scratch_shapes=[pltpu.VMEM((long_rows, features), F32)],
        compiler_params=params(),
        name="input_back",
    )(grad_query, grad_kv, grad_rel, *pieces, *pieces, *others, *others, first)


def weight_products(order, entries, half, extra, parts, pieces, groups, name):
    features = entries[0][0].shape[1]
    depth = features // 2
    blk = depth // pieces
    widths = [right.shape[1] // groups for _, right in entries]
    total = sum(widths)
    count = len(entries)
    outs = []
    if parts is None:
        outs.append((0, total, list(range(pieces))))
    else:
        at = 0
        for width, bit in parts:
            for side in (1, 0):
                outs.append((at, width, [p for p in range(pieces) if (p >> bit & 1) == side]))
            at += width

    def body(order_ref, *refs):
        lefts, rights = refs[:count], refs[count : 2 * count]
        out_refs = refs[len(refs) - len(outs) :]
        for k in range(2):
            odd = order_ref[2 * pl.program_id(0) + k] & 1
            at = 0
            for left_ref, right_ref, width in zip(lefts, rights, widths):
                right = right_ref[:, pl.ds(pl.multiple_of(odd * width, 128), width)]
                term = dot(left_ref[...], right, 0, 0).reshape(pieces, blk, width)
                if extra is not None:
                    term = term + refs[2 * count][:, k, :, at : at + width].astype(F32)
                term = term.astype(BF)
                for out_ref, (first, size, members) in zip(out_refs, outs):
                    low, high = max(at, first), min(at + width, first + size)
                    if low >= high:
                        continue
                    for place, piece in enumerate(members):
                        out_ref[place, k, :, low - first : high - first] = term[
                            piece, :, low - at : high - at
                        ]
                at += width

    def block(number, width):
        return pl.BlockSpec((number, 2, blk, width), lambda i, order: (0, i, 0, 0))

    in_specs = [
        pl.BlockSpec((left.shape[0], depth), lambda i, order: (0, half)) for left, _ in entries
    ]
    in_specs += [
        pl.BlockSpec((right.shape[0], 2 * width), lambda i, order: (0, order[2 * i] // 2))
        for (_, right), width in zip(entries, widths)
    ]
    operands = [left for left, _ in entries] + [right for _, right in entries]
    if extra is not None:
        in_specs.append(block(pieces, total))
        operands.append(extra)
    return pl.pallas_call(
        body,
        grid_spec=pltpu.PrefetchScalarGridSpec(
            num_scalar_prefetch=1,
            grid=(groups // 2,),
            in_specs=in_specs,
            out_specs=[block(len(members), width) for _, width, members in outs],
        ),
        out_shape=[
            jax.ShapeDtypeStruct((len(members), groups, blk, width), BF)
            for _, width, members in outs
        ],
        compiler_params=params(),
        name=name,
    )(order, *operands)


def half_masks(rows):
    lane = lax.broadcasted_iota(jnp.int32, (rows, 128), 1)
    return [
        jnp.where((lane >= 64 * half) & (lane < 64 * half + 64), 1.0, 0.0).astype(F32)
        for half in range(2)
    ]


def lanes_and_rows(share):
    lane = lax.broadcasted_iota(jnp.int32, (share, share), 1)
    row = lax.broadcasted_iota(jnp.int32, (share, share), 0)
    return lane > row


def turn_right(block):
    return pltpu.roll(block, 1, 1, stride=1, stride_axis=0)


def skew(distance, later):
    share = later.shape[0]
    tracks = []
    for n in range(distance.shape[0] // share):
        rows = slice(n * share, (n + 1) * share)
        far, near = turn_right(distance[rows, 0:share]), turn_right(distance[rows, share:])
        tracks.append(jnp.concatenate([far, jnp.where(later, near, far), near], 1))
    return jnp.concatenate(tracks, 0)


def unskew_sources(grid, later):
    share = later.shape[0]
    tracks = []
    for n in range(grid.shape[0] // share):
        old, mid, new = [
            grid[n * share : (n + 1) * share, c * share : (c + 1) * share] for c in range(3)
        ]
        tracks.append(jnp.concatenate([jnp.where(later, old, mid), jnp.where(later, mid, new)], 1))
    return jnp.concatenate(tracks, 0)


def turn_blocks(array_in, share):
    rows = array_in.shape[0]
    return jnp.concatenate(
        [
            jnp.concatenate(
                [turn_right(array_in[r : r + share, c : c + share]) for c in (0, share)], 1
            )
            for r in range(0, rows, share)
        ],
        0,
    )


def self_attention(qk, values, relpos, mask, turned, share):
    rows, window = 3 * share, 3 * share
    groups = values.shape[1] // 256
    long_rows = qk.shape[0]
    halo = long_rows - rows

    def body(q_ref, k_ref, v_ref, rel_ref, mask_ref, turned_ref, ctx_ref, raised_ref, own_ref):
        halves = half_masks(rows)
        later = lanes_and_rows(share)
        lane = lax.broadcasted_iota(jnp.int32, (rows, 128), 1)
        rel = rel_ref[...]
        high = rel.astype(BF)
        split = jnp.concatenate([high, (rel - high.astype(F32)).astype(BF)], 1)
        row_id = lax.broadcasted_iota(jnp.int32, (256, 2 * share), 0) & 127
        track = lax.broadcasted_iota(jnp.int32, (rows, 1), 0) >= share
        own_all = jnp.zeros((rows, 128), F32)
        for pair in range(2):
            cols = slice(128 * pair, 128 * pair + 128)
            q = q_ref[halo:, cols]
            k, v = k_ref[0:window, cols], v_ref[0:window, cols]
            own_k = k_ref[halo:, cols].astype(F32)
            own_v = v_ref[halo:, cols].astype(F32)
            product = q.astype(F32) * own_k
            mixed = jnp.zeros((rows, 128), F32)
            for half in range(2):
                head = 2 * pair + half
                scores = dot(q * halves[half].astype(BF), k, 1, 1)
                table = jnp.where(row_id == turned_ref[...] + 32 * head, 1.0, 0.0).astype(BF)
                scores = scores + skew(dot(split, table, 1, 0), later) + mask_ref[...]
                own = jnp.sum(
                    product * halves[half] + jnp.where(lane == 32 * head, rel, 0.0), -1, keepdims=True
                )
                own = jnp.where(track, own, MASKED)
                top = jnp.maximum(jnp.max(scores, -1, keepdims=True), own)
                raised = jnp.exp(scores - top)
                own_raised = jnp.exp(own - top)
                scale = 1.0 / (jnp.sum(raised, -1, keepdims=True) + own_raised)
                raised = raised.astype(BF)
                raised_ref[head] = raised
                own_all = jnp.where(lane == head, own_raised, own_all)
                own_all = jnp.where(lane == head + 4, scale, own_all)
                mixed = mixed + (dot(raised, v, 1, 0) + own_raised * own_v) * (scale * halves[half])
            ctx_ref[:, cols] = mixed.astype(BF)
        own_ref[...] = own_all

    return pl.pallas_call(
        body,
        grid=(groups,),
        in_specs=[
            pl.BlockSpec((long_rows, 256), lambda j: (0, 2 * j)),
            pl.BlockSpec((long_rows, 256), lambda j: (0, 2 * j + 1)),
            pl.BlockSpec((long_rows, 256), lambda j: (0, j)),
            pl.BlockSpec((rows, 128), lambda j: (0, j)),
            whole((rows, window)),
            whole((1, 2 * share)),
        ],
        out_specs=[
            pl.BlockSpec((rows, 256), lambda j: (0, j)),
            pl.BlockSpec((4, rows, window), lambda j: (j, 0, 0)),
            pl.BlockSpec((rows, 128), lambda j: (0, j)),
        ],
        out_shape=[
            jax.ShapeDtypeStruct((rows, groups * 256), BF),
            jax.ShapeDtypeStruct((4 * groups, rows, window), BF),
            jax.ShapeDtypeStruct((rows, groups * 128), F32),
        ],
        compiler_params=params(),
        name="self_attention",
    )(qk, qk, values, relpos, mask, turned)


def self_attention_back(qk, values, raised, own_raised, grad_ctx, straight, share):
    rows, window = 3 * share, 3 * share
    groups = values.shape[1] // 256
    long_rows = qk.shape[0]
    halo = long_rows - rows

    def body(
        q_ref, k_ref, v_ref, raised_ref, own_ref, grad_ref, straight_ref,
        gq_ref, gkv_ref, grel_ref, sums_ref, rel_sums_ref,
    ):
        halves = half_masks(rows)
        later = lanes_and_rows(share)
        lane = lax.broadcasted_iota(jnp.int32, (rows, 128), 1)
        turn = jnp.where(
            lax.broadcasted_iota(jnp.int32, (2 * share, 2 * share), 0)
            + lax.broadcasted_iota(jnp.int32, (2 * share, 2 * share), 1)
            == 2 * share - 1,
            1.0,
            0.0,
        ).astype(BF)
        column = lax.broadcasted_iota(jnp.int32, (2 * share, 128), 1)
        grel = jnp.zeros((rows, 128), F32)
        own_all = own_ref[...]

        def pick(number):
            return jnp.sum(jnp.where(lane == number, own_all, 0.0), -1, keepdims=True)

        for pair in range(2):
            cols = slice(128 * pair, 128 * pair + 128)
            q = q_ref[halo:, cols]
            k, v = k_ref[0:window, cols], v_ref[0:window, cols]
            own_k = k_ref[halo:, cols].astype(F32)
            own_v = v_ref[halo:, cols].astype(F32)
            scales = [pick(2 * pair + half + 4) for half in range(2)]
            grad_wide = grad_ref[:, cols].astype(F32)
            grad_wide = grad_wide * (scales[0] * halves[0] + scales[1] * halves[1])
            grad = grad_wide.astype(BF)
            own_product = grad_wide * own_v
            gq = jnp.zeros((rows, 128), F32)
            own_spread = jnp.zeros((rows, 128), F32)
            own_weight = jnp.zeros((rows, 128), F32)
            score_parts, prob_parts, q_parts, g_parts = [], [], [], []
            for half in range(2):
                head = 2 * pair + half
                low_half = halves[half].astype(BF)
                p = raised_ref[head]
                p_wide = p.astype(F32)
                grad_half = grad * low_half
                grad_probs = dot(grad_half, v, 1, 1)
                own_p = pick(head)
                own_grad = jnp.sum(own_product * halves[half], -1, keepdims=True)
                row_dot = jnp.sum(p_wide * grad_probs, -1, keepdims=True) + own_p * own_grad
                row_dot = row_dot * scales[half]
                grad_scores = p_wide * (grad_probs - row_dot)
                source = unskew_sources(grad_scores, later).astype(BF)
                grad_scores = grad_scores.astype(BF)
                grad_own = (own_p * (own_grad - row_dot)).astype(BF).astype(F32)
                gq = gq + (dot(grad_scores, k, 1, 0) + grad_own * own_k) * halves[half]
                own_spread = own_spread + grad_own * halves[half]
                own_weight = own_weight + own_p * halves[half]
                score_parts.append(grad_scores)
                prob_parts.append(p)
                q_parts.append(q * low_half)
                g_parts.append(grad_half)
                turned = turn_blocks(dot(source, turn, 1, 0), share).astype(BF)
                table = jnp.where(column == straight_ref[...] + 32 * head, 1.0, 0.0).astype(BF)
                grel = grel + dot(turned, table, 1, 0) + jnp.where(lane == 32 * head, grad_own, 0.0)
            gk = dot(
                jnp.concatenate(q_parts, 0), jnp.concatenate(score_parts, 0), 0, 0
            ).T
            gv = dot(
                jnp.concatenate(g_parts, 0), jnp.concatenate(prob_parts, 0), 0, 0
            ).T
            gq = gq * 0.125
            gq_ref[:, cols] = gq.astype(BF)
            own_gk = own_spread * q.astype(F32)
            own_gv = own_weight * grad_wide
            vcols = slice(256 + 128 * pair, 256 + 128 * pair + 128)
            gkv_ref[0:window, cols] = gk.astype(BF)
            gkv_ref[0:window, vcols] = gv.astype(BF)
            gkv_ref[window:, cols] = own_gk[share:].astype(BF)
            gkv_ref[window:, vcols] = own_gv[share:].astype(BF)
            sums_ref[0:1, cols] = column_sum(gq)
            sums_ref[1:2, cols] = column_sum(gv) + column_sum(own_gv[share:])
        grel_ref[...] = grel.astype(BF)
        rel_sums_ref[...] = column_sum(grel)

    return pl.pallas_call(
        body,
        grid=(groups,),
        in_specs=[
            pl.BlockSpec((long_rows, 256), lambda j: (0, 2 * j)),
            pl.BlockSpec((long_rows, 256), lambda j: (0, 2 * j + 1)),
            pl.BlockSpec((long_rows, 256), lambda j: (0, j)),
            pl.BlockSpec((4, rows, window), lambda j: (j, 0, 0)),
            pl.BlockSpec((rows, 128), lambda j: (0, j)),
            pl.BlockSpec((rows, 256), lambda j: (0, j)),
            whole((2 * share, 1)),
        ],
        out_specs=[
            pl.BlockSpec((rows, 256), lambda j: (0, j)),
            pl.BlockSpec((long_rows, 512), lambda j: (0, j)),
            pl.BlockSpec((rows, 128), lambda j: (0, j)),
            pl.BlockSpec((2, 256), lambda j: (0, j)),
            pl.BlockSpec((1, 128), lambda j: (0, j)),
        ],
        out_shape=[
            jax.ShapeDtypeStruct((rows, groups * 256), BF),
            jax.ShapeDtypeStruct((long_rows, groups * 512), BF),
            jax.ShapeDtypeStruct((rows, groups * 128), BF),
            jax.ShapeDtypeStruct((2, groups * 256), F32),
            jax.ShapeDtypeStruct((1, groups * 128), F32),
        ],
        compiler_params=params(),
        name="self_attention_back",
    )(qk, qk, values, raised, own_raised, grad_ctx, straight)


def cross_attention(queries, kv):
    rows, places = queries.shape[0], kv.shape[0]
    groups = queries.shape[1] // 256

    def body(q_ref, k_ref, v_ref, ctx_ref, raised_ref, scale_ref):
        halves = half_masks(rows)
        lane = lax.broadcasted_iota(jnp.int32, (rows, 128), 1)
        scales = jnp.zeros((rows, 128), F32)
        for pair in range(2):
            cols = slice(128 * pair, 128 * pair + 128)
            q, k, v = q_ref[:, cols], k_ref[:, cols], v_ref[:, cols]
            mixed = jnp.zeros((rows, 128), F32)
            for half in range(2):
                head = 2 * pair + half
                scores = dot(q * halves[half].astype(BF), k, 1, 1)
                raised = jnp.exp(scores - jnp.max(scores, -1, keepdims=True))
                scale = 1.0 / jnp.sum(raised, -1, keepdims=True)
                raised = raised.astype(BF)
                raised_ref[head] = raised
                scales = jnp.where(lane == head, scale, scales)
                mixed = mixed + dot(raised, v, 1, 0) * (scale * halves[half])
            ctx_ref[:, cols] = mixed.astype(BF)
        scale_ref[...] = scales

    return pl.pallas_call(
        body,
        grid=(groups,),
        in_specs=[
            pl.BlockSpec((rows, 256), lambda j: (0, j)),
            pl.BlockSpec((places, 256), lambda j: (0, 2 * j)),
            pl.BlockSpec((places, 256), lambda j: (0, 2 * j + 1)),
        ],
        out_specs=[
            pl.BlockSpec((rows, 256), lambda j: (0, j)),
            pl.BlockSpec((4, rows, places), lambda j: (j, 0, 0)),
            pl.BlockSpec((rows, 128), lambda j: (0, j)),
        ],
        out_shape=[
            jax.ShapeDtypeStruct((rows, groups * 256), BF),
            jax.ShapeDtypeStruct((4 * groups, rows, places), BF),
            jax.ShapeDtypeStruct((rows, groups * 128), F32),
        ],
        compiler_params=params(),
        name="cross_attention",
    )(queries, kv, kv)


def cross_attention_back(queries, kv, raised, scales, grad_ctx):
    rows, places = queries.shape[0], kv.shape[0]
    groups = queries.shape[1] // 256

    def body(q_ref, k_ref, v_ref, raised_ref, scale_ref, grad_ref, gq_ref, gkv_ref, sums_ref):
        halves = half_masks(rows)
        lane = lax.broadcasted_iota(jnp.int32, (rows, 128), 1)
        scale_all = scale_ref[...]
        for pair in range(2):
            cols = slice(128 * pair, 128 * pair + 128)
            q, k, v = q_ref[:, cols], k_ref[:, cols], v_ref[:, cols]
            scale = [
                jnp.sum(jnp.where(lane == 2 * pair + half, scale_all, 0.0), -1, keepdims=True)
                for half in range(2)
            ]
            grad = grad_ref[:, cols].astype(F32) * (scale[0] * halves[0] + scale[1] * halves[1])
            grad = grad.astype(BF)
            gq = jnp.zeros((rows, 128), F32)
            score_parts, prob_parts, q_parts, g_parts = [], [], [], []
            for half in range(2):
                low_half = halves[half].astype(BF)
                p = raised_ref[2 * pair + half]
                p_wide = p.astype(F32)
                grad_half = grad * low_half
                grad_probs = dot(grad_half, v, 1, 1)
                row_dot = jnp.sum(p_wide * grad_probs, -1, keepdims=True) * scale[half]
                grad_scores = (p_wide * (grad_probs - row_dot)).astype(BF)
                gq = gq + dot(grad_scores, k, 1, 0) * halves[half]
                score_parts.append(grad_scores)
                prob_parts.append(p)
                q_parts.append(q * low_half)
                g_parts.append(grad_half)
            gk = dot(
                jnp.concatenate(q_parts, 0), jnp.concatenate(score_parts, 0), 0, 0
            ).T
            gv = dot(
                jnp.concatenate(g_parts, 0), jnp.concatenate(prob_parts, 0), 0, 0
            ).T
            gq = gq * 0.125
            gq_ref[:, cols] = gq.astype(BF)
            vcols = slice(256 + 128 * pair, 256 + 128 * pair + 128)
            gkv_ref[:, cols] = gk.astype(BF)
            gkv_ref[:, vcols] = gv.astype(BF)
            sums_ref[0:1, cols] = column_sum(gq)
            sums_ref[1:2, cols] = column_sum(gv)

    return pl.pallas_call(
        body,
        grid=(groups,),
        in_specs=[
            pl.BlockSpec((rows, 256), lambda j: (0, j)),
            pl.BlockSpec((places, 256), lambda j: (0, 2 * j)),
            pl.BlockSpec((places, 256), lambda j: (0, 2 * j + 1)),
            pl.BlockSpec((4, rows, places), lambda j: (j, 0, 0)),
            pl.BlockSpec((rows, 128), lambda j: (0, j)),
            pl.BlockSpec((rows, 256), lambda j: (0, j)),
        ],
        out_specs=[
            pl.BlockSpec((rows, 256), lambda j: (0, j)),
            pl.BlockSpec((places, 512), lambda j: (0, j)),
            pl.BlockSpec((2, 256), lambda j: (0, j)),
        ],
        out_shape=[
            jax.ShapeDtypeStruct((rows, groups * 256), BF),
            jax.ShapeDtypeStruct((places, groups * 512), BF),
            jax.ShapeDtypeStruct((2, groups * 256), F32),
        ],
        compiler_params=params(),
        name="cross_attention_back",
    )(queries, kv, kv, raised, scales, grad_ctx)


def per_device(
    hidden,
    memory,
    grad_out,
    lengths,
    key_mask,
    buckets,
    self_weight,
    relpos_weight,
    selfout_weight,
    crossq_weight,
    crosskv_weight,
    crossout_weight,
    up_weight,
    down_weight,
    self_bias,
    relpos_bias,
    cross_bias,
    up_bias,
    norm_gain,
    norm_bias,
    out_bias,
):
    batches, groups = lax.axis_size("batch"), lax.axis_size("head")
    b, z = lax.axis_index("batch"), lax.axis_index("head")
    nb = bits_of("batch")
    share, features = hidden.shape[1], hidden.shape[3]
    length = share * groups
    rows, window = 3 * share, 3 * share
    assert share == 128 and hidden.shape[0] == 1 and WIDEST_DOC <= 2 * share
    assert batches == 1 << nb and features % batches == 0 and groups == 4
    near, far = list(range(1, nb)), list(reversed(range(1, nb)))

    turned_ids = jnp.array([bit_reverse(p, nb) for p in range(batches)], jnp.int32)
    to_exchange = b ^ turned_ids
    natural = lax.iota(jnp.int32, batches) ^ b
    to_natural = jnp.zeros_like(natural)
    for bit in range(nb):
        to_natural = to_natural | (((natural >> bit) & 1) << (nb - 1 - bit))
    group_order = z ^ lax.iota(jnp.int32, groups)

    def small_features(stack):
        count = stack.shape[0]
        blocks = stack.reshape(count, batches, features // batches)
        return jnp.take(blocks, to_exchange, axis=1).reshape(count, features)

    blk = self_weight.shape[0]
    assert nb >= 2 and bits_of("head") == 2
    line = Line()
    self_shard = jnp.concatenate([self_weight.reshape(blk, -1), relpos_weight], 1).astype(BF)
    gather_self = Gather(line, line.mark(pin(self_shard)))
    gather_self.send("head", 1)
    ffn_shard = line.mark(
        pin(jnp.concatenate([line.tie(up_weight), down_weight], 1).astype(BF))
    )
    gather_ffn = Gather(line, ffn_shard)

    columns = jnp.concatenate(
        [
            self_bias[0].reshape(groups, -1),
            self_bias[1].reshape(groups, -1),
            cross_bias[0].reshape(groups, -1),
            cross_bias[1].reshape(groups, -1),
            relpos_bias.reshape(groups, -1),
            up_bias.reshape(groups, -1),
        ],
        1,
    )
    columns = jnp.take(columns, group_order, axis=0)
    query_bias, value_bias = columns[:, 0:256], columns[:, 256:512]
    cross_query_bias, cross_value_bias = columns[:, 512:768], columns[:, 768:1024]
    rel_row = columns[:, 1024:1152].reshape(1, -1)
    up_row = columns[:, 1152:].reshape(1, -1)

    memory_own = line.mark(reorder_blocks(line.tie(memory[0]), to_exchange))
    own = jnp.transpose(line.tie(hidden[0]), (1, 0, 2)).reshape(rows, features)
    own = line.mark(reorder_blocks(own, to_exchange))
    upstream = lax.dynamic_slice_in_dim(line.tie(grad_out[0]), z * share, share, 0)
    upstream = jnp.transpose(upstream, (1, 0, 2)).reshape(rows, features)
    upstream = line.mark(reorder_blocks(upstream, to_exchange))
    chain = list(range(groups))

    vectors = small_features(jnp.concatenate([norm_gain, norm_bias, out_bias], 0))
    vectors = vectors.reshape(3, 3, features).transpose(1, 0, 2)
    none = jnp.zeros((groups, 256), F32)

    def affine(bias, scale):
        return jnp.stack([bias, jnp.full(bias.shape, scale, F32)])

    scales = jnp.concatenate([none + 0.125, none + 1.0], 1).reshape(-1)
    qk_affine = jnp.stack([jnp.concatenate([query_bias, none], 1).reshape(-1), scales])
    value_affine = affine(value_bias.reshape(-1), 1.0)
    rel_affine = affine(rel_row[0], 1.0)
    cross_query_affine = affine(cross_query_bias.reshape(-1), 0.125)
    cross_kv_affine = affine(jnp.concatenate([none, cross_value_bias], 1).reshape(-1), 1.0)

    places = lax.iota(jnp.int32, length)
    doc_ends = jnp.cumsum(lengths[0])
    segment = jnp.sum((places[:, None] >= doc_ends[None, :]).astype(jnp.int32), -1)
    lead = window - share
    padded_segment = jnp.concatenate([jnp.full((lead,), -1, jnp.int32), segment])
    padded_mask = jnp.concatenate([jnp.zeros((lead,), jnp.int32), key_mask[0]])
    key_segment = lax.dynamic_slice_in_dim(padded_segment, z * share, window)
    key_open = lax.dynamic_slice_in_dim(padded_mask, z * share, window)
    query_segment = lax.dynamic_slice_in_dim(segment, z * share, share)
    query_at = lax.iota(jnp.int32, share)[:, None] + lead
    key_at = lax.iota(jnp.int32, window)[None, :]
    joined = (query_segment[:, None] == key_segment[None, :]) & (
        (key_open[None, :] == 1) | (query_at == key_at)
    )
    allowed_main = joined & (key_at <= query_at)
    allowed_pred = joined & (key_at < query_at)
    mask = jnp.where(jnp.stack([allowed_main, allowed_pred, allowed_pred]), 0.0, MASKED)
    mask = mask.reshape(rows, window).astype(F32)
    straight = buckets[0 : 2 * share]
    turned = straight[::-1]

    mask = line.mark(line.tie(mask))
    assert nb >= 2 and bits_of("head") == 2
    gather_cross = Gather(
        line,
        jnp.concatenate(
            [selfout_weight, crossq_weight, crosskv_weight.reshape(blk, -1), crossout_weight], 1
        ).astype(BF),
    )
    gather_self.take()
    gather_self.send("head", 0)
    gather_ffn.send("head", 1)
    gather_self.take()
    parts_self = [gather_self.columns(0, 512), gather_self.columns(512, 384)]
    orders_self = [near, far]
    for part, part_order in zip(parts_self, orders_self):
        part.send("batch", part_order[0])
    gather_ffn.take()
    gather_ffn.send("head", 0)
    for number in range(1, nb - 1):
        for part, part_order in zip(parts_self, orders_self):
            part.take()
            part.send("batch", part_order[number])
    gather_cross.send("head", 1)
    gather_ffn.take()
    for part in parts_self:
        part.take()
        part.send("batch", 0)
    gather_cross.take()
    gather_cross.send("head", 0)
    main = line.tie(own[0:share])
    before_one = lax.ppermute(main, "head", [(i, i + 1) for i in chain[:-1]])
    before_two = lax.ppermute(main, "head", [(i, i + 2) for i in chain[:-2]])
    gather_cross.take()
    parts_cross = [gather_cross.columns(0, 512), gather_cross.columns(512, 768)]
    orders_cross = [far, near]
    for part, part_order in zip(parts_cross, orders_cross):
        part.send("batch", part_order[0])
    extended = line.mark(stack_rows(before_two, before_one, line.tie(own)))
    memory_came = swap(line.tie(memory_own), "head", 2)
    weights_qk, weights_vr = [part.close() for part in parts_self]

    order = jnp.concatenate([group_order, to_exchange]).astype(jnp.int32)
    values = line.mark(
        project(line.tie(extended), weights_vr, 0, 256, 256, value_affine, BF, "self_v")
    )
    relpos = line.mark(
        project(line.tie(own), weights_vr, 256, 128, 128, rel_affine, F32, "self_rel")
    )
    for number in range(1, nb - 1):
        for part, part_order in zip(parts_cross, orders_cross):
            part.take()
            part.send("batch", part_order[number])
    weights_ffn = line.tie(gather_ffn.buf).reshape((groups,) + ffn_shard.shape)
    weights_ffn = lax.all_gather(weights_ffn, "batch", axis=0)
    if blk % 128:
        weights_ffn = jnp.take(weights_ffn, to_exchange, axis=0)
    qk = line.mark(project(line.tie(extended), weights_qk, 0, 512, 512, qk_affine, BF, "self_qk"))
    memory_half = line.mark(jnp.concatenate([line.tie(memory_own), memory_came], 0))
    memory_came = swap(memory_half, "head", 1)
    context, self_probs, self_own = self_attention(
        line.tie(qk), values, relpos, mask, turned.reshape(1, -1), share
    )
    line.mark(context)
    for part in parts_cross:
        part.take()
        part.send("batch", 0)
    weights_out, weights_kv = [part.close() for part in parts_cross]
    normed1, normed1_low, unit1, spread1 = close_sublayer(
        line.tie(context), weights_out, 0, 256, own, vectors[0], "self_out"
    )
    line.mark(normed1)
    cross_q = line.mark(
        project(
            line.tie(normed1_low), weights_out, 256, 256, 256, cross_query_affine, BF, "cross_q"
        )
    )
    memory_all = line.mark(jnp.concatenate([line.tie(memory_half), memory_came], 0))
    cross_kv = line.mark(
        project(line.tie(memory_all), weights_kv, 0, 512, 512, cross_kv_affine, BF, "cross_kv")
    )
    cross_context, cross_probs, cross_scales = cross_attention(line.tie(cross_q), cross_kv)
    line.mark(cross_context)
    normed2, normed2_low, unit2, spread2 = close_sublayer(
        line.tie(cross_context), weights_kv, 512, 256, normed1, vectors[1], "cross_out"
    )
    line.mark(normed2)
    (
        active, out_low, third_low, sums_third, upper_low, up_sums,
        second, second_low, sums_second, grad_cross_ctx,
    ) = feed_forward(
        order, line.tie(normed2_low), normed2, weights_ffn, up_row, vectors[2], upstream,
        unit2, spread2, vectors[1][0:1], weights_kv, 512,
    )
    line.mark(second)

    straight_order = lax.iota(jnp.int32, groups)

    def send(entries, name, natural=False):
        left, right = entries[0]
        entries = [(line.tie(left), right)] + entries[1:]
        turn = group_order if natural else straight_order
        (sent,) = weight_products(
            turn, entries, 1, None, None, batches // 2, groups, name + "_send"
        )
        return swap(line.mark(sent), "batch", 1)

    def keep(entries, came, parts, name, natural=False):
        left, right = entries[0]
        entries = [(line.tie(left), right)] + entries[1:]
        parts = [(width, nb - 1 - part_order[0]) for width, part_order in parts]
        turn = group_order if natural else straight_order
        outs = weight_products(
            turn, entries, 0, came, parts, batches // 2, groups, name + "_keep"
        )
        line.mark(outs[0])
        return [outs[k : k + 2] for k in range(0, len(outs), 2)]

    def natural_groups(block):
        return jnp.take(block.reshape(-1, groups, block.shape[1] // groups), group_order, axis=1)

    def pack_sums(earlier):
        feature_sums = jnp.concatenate([after(sums_first, earlier), sums_second, sums_third], 0)
        feature_sums = jnp.take(
            feature_sums.reshape(9, batches, features // batches), to_natural, axis=1
        )
        return jnp.concatenate(
            [
                natural_groups(self_sums).reshape(-1),
                natural_groups(rel_sums).reshape(-1),
                natural_groups(cross_sums).reshape(-1),
                natural_groups(up_sums).reshape(-1),
                feature_sums.reshape(-1),
            ]
        )

    down_entries = [(third_low, active)]
    if blk % 128:
        out_low = reorder_blocks(out_low, to_natural)
    out_low = out_low.reshape(3, share, features)
    layer_out = lax.all_gather(out_low, "head", axis=1, tiled=True)
    down_entries = [(third_low, active)]
    down_came = send(down_entries, "down_grad", True)
    up_entries = [(normed2_low, upper_low)]
    up_came = send(up_entries, "up_grad", True)
    down_halves = keep(down_entries, down_came, [(1024, near)], "down_grad", True)
    up_halves = keep(up_entries, up_came, [(1024, far)], "up_grad", True)
    scatter_ffn = Scatter(line, down_halves + up_halves, (near, far), True)
    grad_cross_q, grad_cross_kv, cross_sums = cross_attention_back(
        cross_q, cross_kv, cross_probs, cross_scales, line.tie(grad_cross_ctx)
    )
    line.mark(grad_cross_q)
    first, first_low, sums_first = cross_query_back(
        line.tie(grad_cross_q), weights_out, 256, 256, second, unit1, spread1, vectors[0][0:1]
    )
    line.mark(first)
    grad_context = project_plain(line.tie(first_low), weights_out, 0, 256, "self_ctx_back")
    line.mark(grad_context)
    grad_q, grad_kv, grad_rel, self_sums, rel_sums = self_attention_back(
        qk, values, self_probs, self_own, line.tie(grad_context), straight.reshape(-1, 1), share
    )
    line.mark(grad_q)
    layer_out = line.tie(layer_out)
    line.mark(layer_out, *line.last)
    scatter_ffn.step()
    memory_order = z ^ jnp.array([0, 2, 1, 3], jnp.int32)
    memory_part = rows_back(
        memory_order, line.tie(grad_cross_kv), weights_kv, 0, 512, "memory_back"
    )
    memory_grad = lax.psum_scatter(
        line.mark(memory_part), "head", scatter_dimension=0, tiled=True
    )
    cross_entries = [
        (normed1_low, grad_cross_q),
        (memory_all, grad_cross_kv),
        (second_low, cross_context),
        (first_low, context),
    ]
    cross_came = send(cross_entries, "cross_grad")
    self_entries = [(own, grad_q), (extended, grad_kv), (own, grad_rel)]
    self_came = send(self_entries, "self_grad")
    halves = keep(cross_entries, cross_came, [(640, near), (640, far)], "cross_grad")
    cross_cuts = ((0, 256, 1), (256, 512, 1), (768, 256, 1), (1024, 256, 1))
    scatter_cross = Scatter(line, halves, (near, far), cuts=cross_cuts)
    halves = keep(self_entries, self_came, [(512, near), (384, far)], "self_grad")
    scatter_self = Scatter(line, halves, (near, far), cuts=((0, 256, 3), (768, 128, 1)))
    while not hasattr(scatter_ffn, "total"):
        scatter_ffn.step()
    memory_grad = line.tie(memory_grad)
    line.mark(memory_grad, *line.last)
    packed = line.mark(pack_sums(line.last[0]))
    packed_bits = [("batch", bit) for bit in range(nb)] + [("head", 0), ("head", 1)]

    def add_packed(packed):
        axis_name, bit = packed_bits.pop(0)
        came = swap(packed, axis_name, 1 << bit)
        packed = line.tie(packed)
        return line.mark(packed + after(came, packed))

    two_grad, one_grad, own_grad = input_back(
        line.tie(grad_q), grad_kv, grad_rel, weights_qk, weights_vr, first
    )
    line.mark(own_grad)
    from_two = lax.ppermute(two_grad, "head", [(i + 2, i) for i in chain[:-2]])
    from_one = lax.ppermute(one_grad, "head", [(i + 1, i) for i in chain[:-1]])
    scatter_cross.step()
    scatter_self.step()
    scatter_ffn.total = line.tie(scatter_ffn.total)
    line.mark(scatter_ffn.total, *line.last)
    own_grad = line.mark(add_halo(line.tie(own_grad), from_one, from_two))
    own_grad = line.mark(reorder_blocks(line.tie(own_grad), to_natural)).reshape(
        3, share, features
    )
    grad_hidden = jnp.transpose(own_grad, (1, 0, 2))[None]
    scatter_cross.step()
    scatter_self.step()
    packed = add_packed(packed)
    grad_memory = line.mark(reorder_blocks(line.tie(memory_grad), to_natural, F32))[None]
    packed = add_packed(packed)
    layer_out = line.mark(copy_tracks(line.tie(layer_out)))
    layer_out = jnp.transpose(layer_out, (1, 0, 2))[None]
    scatter_cross.step()
    packed = add_packed(packed)
    scatter_self.step()
    while packed_bits:
        packed = add_packed(packed)
    ends = [0]
    for size in (2 * features, groups * 128, 2 * features, up_bias.shape[0], 9 * features):
        ends.append(ends[-1] + size)
    self_bias_grad = packed[ends[0] : ends[1]].reshape(2, -1)
    relpos_bias_grad = packed[ends[1] : ends[2]]
    cross_bias_grad = packed[ends[2] : ends[3]].reshape(2, -1)
    up_bias_grad = packed[ends[3] : ends[4]]
    feature_sums = packed[ends[4] : ends[5]].reshape(3, 3, features)
    small = (
        self_bias_grad,
        relpos_bias_grad,
        cross_bias_grad,
        up_bias_grad,
        feature_sums[:, 0],
        feature_sums[:, 1],
        feature_sums[:, 2],
    )
    small = lax.optimization_barrier(small + line.last)[: len(small)]
    line.mark(*small)
    while not hasattr(scatter_cross, "total"):
        scatter_cross.step()
    cross_kv_grad = line.mark(line.tie(scatter_cross.total[1]).reshape(blk, 2, 256))
    while not hasattr(scatter_self, "total"):
        scatter_self.step()
    grads_ffn, grads_cross, grads_self = [
        scatter.total for scatter in (scatter_ffn, scatter_cross, scatter_self)
    ]

    return (
        layer_out,
        grad_hidden,
        grad_memory,
        jnp.transpose(grads_self[0], (1, 0, 2)),
        grads_self[1],
        grads_cross[3],
        grads_cross[0],
        cross_kv_grad,
        grads_cross[2],
        grads_ffn[:, 1024:],
        grads_ffn[:, 0:1024],
    ) + tuple(small)


def solution(mesh):
    in_specs = (
        P("batch", "head", None, None),
        P("batch", "head", None),
        P("batch", None, None, None),
        P("batch", None),
        P("batch", None),
        P(),
        P("batch", None, "head"),
        P("batch", "head"),
        P("batch", "head"),
        P("batch", "head"),
        P("batch", None, "head"),
        P("batch", "head"),
        P("batch", "head"),
        P("batch", "head"),
        P(),
        P(),
        P(),
        P(),
        P(),
        P(),
        P(),
    )
    out_specs = (
        P("batch", None, None, None),
        P("batch", "head", None, None),
        P("batch", "head", None),
        P("batch", None, "head"),
        P("batch", "head"),
        P("batch", "head"),
        P("batch", "head"),
        P("batch", None, "head"),
        P("batch", "head"),
        P("batch", "head"),
        P("batch", "head"),
        P(),
        P(),
        P(),
        P(),
        P(),
        P(),
        P(),
    )
    return jax.shard_map(
        per_device, mesh=mesh, in_specs=in_specs, out_specs=out_specs, check_vma=False
    )
```
